32 devices in a mesh: grp: 2 (over y), ctx: 4 (over z), head: 2 (over x), rep: 2 (over core).
Axes of the slice: x: 2, y: 2, z: 4, core: 2. Of those that a mesh axis runs over, the one named last changes fastest.
Arguments:
- tokens: bfloat16 [4096, 2048], P(('grp', 'ctx', 'rep')), parts along dimension 0, may hold values from -6 to 6
- doc_ids: int32 [4096], P(('grp', 'ctx', 'rep')), parts along dimension 0, may hold values from 0 to 3, never falling along the last dimension, each value on 1 to 1024 neighbouring positions
- dest_rows: int32 [4096], P(('grp', 'ctx', 'rep')), parts along dimension 0, may hold values from 0 to 2047, as said below
- w_query: bfloat16 [2048, 4096], P(None, 'head'), may hold values from -0.125 to 0.125
- w_key: bfloat16 [2048, 512], P(None, 'head'), may hold values from -0.125 to 0.125
- w_value: bfloat16 [2048, 512], P(None, 'head'), may hold values from -0.125 to 0.125
- w_out: bfloat16 [4096, 2048], P('head'), may hold values from -0.09375 to 0.09375
Outputs:
- layer_out: bfloat16 [4096, 2048], P(('grp', 'ctx', 'rep'), 'head'), parts along dimension 0
The draws below stay inside these ranges and needn't reach their ends.
There are 2 independent parts, one for each index of `grp`. The reference program is written for one: setup_inputs(seed, part) draws one part's arguments, and reference() takes and returns one part's arrays. A program takes and returns all parts, laid end to end along the dimension named above; an argument that names none is the same for every part. Nothing has to cross between parts.
Inputs may be any that keep to these rules, and one draw needn't show every extreme that they name: dest_rows is a permutation of the 2048 rows; owner o holds rows o * 256 to (o + 1) * 256 - 1. The 256 tokens of one device go in runs of 16 consecutive tokens, a run to one owner; each device sends 3 * 16 = 48 tokens to half of the owners and 16 to each of the others. `doc_ids`: document number of each token, never falling along the sequence.
All inputs are finite; a program needn't handle non-finite values.
Results may differ from the reference program's by a relative error of at most 0.0078.
Values may be sent and summed in bfloat16 or wider, within the bound.
No kernel may reach another device: no remote copies, remote signals or barrier semaphores. Data moves between devices by JAX's collectives and lax.ppermute only.
A program may use at most 128 MiB of HBM per device.

```python
import math
import jax
import jax.numpy as jnp
import numpy as np
from jax import lax

D = 2048
QH = 32
KVH = 4
HD = 128
TOK_DEV = 256
TOKENS = 2048
BAND = 16
DOCS = 4
DOC_MOST = 1024
N_HEAD = 2


def draw_dest_rows(key, part):
    owners = TOKENS // TOK_DEV
    bands = TOK_DEV // BAND
    first_key, second_key, third_key = jax.random.split(jax.random.fold_in(key, 71), 3)
    order = jax.random.permutation(first_key, owners)
    half_count = owners // 2
    offsets = jnp.concatenate([order[:half_count], order[:half_count], order[:half_count], order[half_count:]])
    offsets = jax.random.permutation(second_key, offsets)
    source = jnp.arange(owners, dtype=jnp.int32)[:, None]
    owner_of = (source + offsets[None, :]) % owners
    slot_perms = jax.vmap(lambda sub_key: jax.random.permutation(sub_key, TOK_DEV))(jax.random.split(third_key, owners))
    local_slot = jnp.arange(bands, dtype=jnp.int32)[:, None] * BAND + jnp.arange(BAND, dtype=jnp.int32)[None, :]
    owner_full = jnp.broadcast_to(owner_of[:, :, None], (owners, bands, BAND))
    local_full = jnp.broadcast_to(local_slot[None, :, :], (owners, bands, BAND))
    slot_final = slot_perms[owner_full, local_full]
    return (owner_full * TOK_DEV + slot_final).reshape(TOKENS).astype(jnp.int32)


def block_scale(key, extent, cuts, smallest, top_value):
    factor_of, own = 1.0, jax.random.fold_in(key, 6)
    for dim, shards_of in cuts:
        heights = jnp.exp(jax.random.uniform(jax.random.fold_in(own, dim), (shards_of,), jnp.float32, smallest / len(cuts), top_value / len(cuts)))
        factor_of = factor_of * jnp.repeat(heights, extent[dim] // shards_of).reshape([-1 if axis == dim else 1 for axis in range(len(extent))])
    return factor_of


def split_up(count, total, bound, slope):
    loads = [(1 << 20) // math.isqrt(grade ** slope) + 1 for grade in range(2, count + 1)]
    rest, given = total - bound - (count - 1), [1] * (count - 1)
    while rest > 0:
        movable = [i for i in range(count - 1) if given[i] < bound]
        pool, remaining = sum([loads[i] for i in movable]), rest
        for i in movable:
            more = min(bound - given[i], max(1, remaining * loads[i] // pool), rest)
            given[i] = given[i] + more
            rest = rest - more
    return np.array([bound] + given)


def uneven(own_key, number_of, total, reach, slope):
    if number_of == 2:
        one = jax.random.randint(own_key, (), max(1, total - reach), min(reach, total - 1) + 1)
        return jnp.stack([one, total - one])
    lengths = jnp.asarray(split_up(number_of, total, reach, slope), jnp.int32)
    twos = (number_of - 1) // 2
    source_of, sink = lengths[1:1 + 2 * twos:2], lengths[2:2 + 2 * twos:2]
    margin = jnp.minimum(source_of - 1, reach - sink)
    passed = jax.random.randint(jax.random.fold_in(own_key, 1), (twos,), 0, 1 << 20) % (margin + 1)
    lengths = lengths.at[1:1 + 2 * twos:2].set(source_of - passed).at[2:2 + 2 * twos:2].set(sink + passed)
    return lengths[jax.random.permutation(jax.random.fold_in(own_key, 2), number_of)]


def bell_draw(stream_key, dims, deviation, limit, cuts=(), kind=jnp.bfloat16):
    values = jax.random.normal(stream_key, dims, jnp.float32) * deviation
    if len(cuts) > 0:
        values = block_scale(stream_key, dims, cuts, -0.22, 0.18) * values
    return jnp.clip(values, min=-limit, max=limit).astype(kind)


def setup_inputs(seed: int = 0, part: int = 0) -> dict:
    key_list = jax.random.split(jax.random.key(seed), 8)
    own_keys = jax.random.split(jax.random.fold_in(key_list[7], part), 8)
    tokens = bell_draw(own_keys[0], (TOKENS, D), 1.0, 6.0, ((0, 8),))
    doc_ids = jnp.searchsorted(jnp.cumsum(uneven(own_keys[1], DOCS, TOKENS, DOC_MOST, 2)), jnp.arange(TOKENS), side="right").astype(jnp.int32)
    dest_rows = draw_dest_rows(jax.random.fold_in(jax.random.fold_in(key_list[7], part), 71), part)
    w_query = bell_draw(key_list[3], (D, QH * HD), D ** -0.5, 0.125, ((1, 2),))
    w_key = bell_draw(key_list[4], (D, KVH * HD), D ** -0.5, 0.125, ((1, 2),))
    w_value = bell_draw(key_list[5], (D, KVH * HD), D ** -0.5, 0.125, ((1, 2),))
    w_out = bell_draw(key_list[6], (QH * HD, D), (QH * HD) ** -0.5, 0.09375, ((0, 2),))
    return {"tokens": tokens, "doc_ids": doc_ids, "dest_rows": dest_rows, "w_query": w_query, "w_key": w_key, "w_value": w_value, "w_out": w_out}


THETA = 1000000.0
EPSILON = 1e-06

def rope_tables(positions, head_dim):
    inverse = jnp.power(THETA, -(jnp.arange(0, head_dim, 2, dtype=jnp.float32) / head_dim))
    angles = positions.astype(jnp.float32)[:, None] * inverse[None, :]
    cosine = jnp.cos(angles)
    sine = jnp.sin(angles)
    return (jnp.concatenate([cosine, cosine], -1), jnp.concatenate([sine, sine], -1))

def project_heads(tokens, weight, positions, head_dim):
    flat = jnp.dot(tokens, weight, preferred_element_type=jnp.float32)
    heads = flat.reshape(flat.shape[0], -1, head_dim)
    normed = heads * lax.rsqrt(lax.optimization_barrier(jnp.mean(heads * heads, axis=-1, keepdims=True)) + EPSILON)
    cosine, sine = rope_tables(positions, head_dim)
    half_dim = head_dim // 2
    rotated = jnp.concatenate([-normed[..., half_dim:], normed[..., :half_dim]], -1)
    return (normed * cosine[:, None, :] + rotated * sine[:, None, :]).astype(jnp.bfloat16)

def reference(tokens, doc_ids, dest_rows, w_query, w_key, w_value, w_out):
    positions = jnp.arange(TOKENS, dtype=jnp.int32)
    groups = QH // KVH
    queries = project_heads(tokens, w_query, positions, HD).reshape(TOKENS, KVH, groups, HD)
    keys_all = project_heads(tokens, w_key, positions, HD).astype(jnp.float32)
    values_all = jnp.dot(tokens, w_value, preferred_element_type=jnp.float32).astype(jnp.bfloat16)
    values_all = values_all.reshape(TOKENS, KVH, HD).astype(jnp.float32)
    score_scale = 1.0 / HD ** 0.5
    block_rows = 128

    def one_block(first_row):
        query_blk = lax.dynamic_slice_in_dim(queries, first_row, block_rows, 0).astype(jnp.float32)
        query_pos = first_row + jnp.arange(block_rows, dtype=jnp.int32)
        query_seg = lax.dynamic_slice_in_dim(doc_ids, first_row, block_rows, 0)
        scores = jnp.einsum('bkgd,nkd->bkgn', query_blk, keys_all) * score_scale
        visible = (doc_ids[None, :] == query_seg[:, None]) & (positions[None, :] <= query_pos[:, None])
        weights = jnp.where(visible[:, None, None, :], jnp.exp(scores), 0.0)
        rounded = weights.astype(jnp.bfloat16).astype(jnp.float32)
        numer = jnp.einsum('bkgn,nkd->bkgd', rounded, values_all)
        result = numer / lax.optimization_barrier(jnp.sum(weights, axis=-1))[..., None]
        return result.astype(jnp.bfloat16).reshape(block_rows, QH * HD)
    starts = jnp.arange(0, TOKENS, block_rows, dtype=jnp.int32)
    attended = lax.map(one_block, starts).reshape(TOKENS, QH * HD)
    group_width = QH * HD // N_HEAD
    mixed = jnp.zeros((TOKENS, D), jnp.float32)
    for group_index in range(N_HEAD):
        lower = group_index * group_width
        partial_value = jnp.dot(attended[:, lower:lower + group_width], w_out[lower:lower + group_width, :], preferred_element_type=jnp.float32)
        mixed = mixed + partial_value.astype(jnp.bfloat16).astype(jnp.float32)
    placed = jnp.zeros_like(mixed).at[dest_rows].set(mixed)
    return placed.astype(jnp.bfloat16)
```

```python
import functools
import math

import jax
import jax.numpy as jnp
from jax import lax
from jax.experimental import pallas as pl
from jax.experimental.pallas import tpu as pltpu
from jax.sharding import PartitionSpec as P

HD = 128
THETA = 1000000.0
EPSILON = 1e-06
HIDE = -1e30
F32 = jnp.float32
BF16 = jnp.bfloat16
VMEM = pl.BlockSpec(memory_space=pltpu.VMEM)
ANY = pl.BlockSpec(memory_space=pl.ANY)
MIB = 1 << 20


def params(mib):
    return pltpu.CompilerParams(vmem_limit_bytes=mib * MIB)


def cost(flops, nbytes, trans=0):
    return pl.CostEstimate(flops=int(flops), bytes_accessed=int(nbytes), transcendentals=int(trans))


def column_of(row):
    n = row.shape[1]
    at = lax.broadcasted_iota(jnp.int32, (n, n), 0) == lax.broadcasted_iota(jnp.int32, (n, n), 1)
    return jnp.sum(jnp.where(at, row, 0.0), axis=1, keepdims=True)


def norm_rope(heads, cosine, sine, factor):
    scale = lax.rsqrt(jnp.mean(heads * heads, axis=-1, keepdims=True) + EPSILON)
    if factor != 1.0:
        scale = scale * factor
    turned = pltpu.roll(heads, HD // 2, 1)
    return ((heads * cosine + turned * sine) * scale).astype(BF16)


def kv_kernel(x_ref, wk_ref, wv_ref, seg_ref, k_ref, v_ref, tab_ref, acc_k, acc_v):
    step = pl.program_id(0)
    rows = x_ref.shape[0]
    first = (lax.axis_index("ctx") * 2 + lax.axis_index("rep")) * rows

    @pl.when(step == 0)
    def _():
        lane = lax.broadcasted_iota(jnp.int32, (1, HD), 1)
        freq = jnp.exp(lax.rem(lane, HD // 2).astype(F32) * (-2.0 * math.log(THETA) / HD))
        pos = (first + lax.broadcasted_iota(jnp.int32, (rows, HD), 0)).astype(F32)
        angle = pos * freq
        tab_ref[:, :HD] = jnp.cos(angle)
        tab_ref[:, HD:] = jnp.where(lane < HD // 2, -jnp.sin(angle), jnp.sin(angle))
        acc_k[...] = jnp.zeros_like(acc_k)
        acc_v[...] = jnp.zeros_like(acc_v)

    acc_k[...] += jnp.dot(x_ref[...], wk_ref[...], preferred_element_type=F32)
    acc_v[...] += jnp.dot(x_ref[...], wv_ref[...], preferred_element_type=F32)

    @pl.when(step == pl.num_programs(0) - 1)
    def _():
        for g in range(acc_k.shape[1] // HD):
            at = pl.ds(g * HD, HD)
            k_ref[0:rows, at] = norm_rope(acc_k[:, at], tab_ref[:, :HD], tab_ref[:, HD:], 1.0)
        wide = k_ref.shape[1]
        line = lax.broadcasted_iota(jnp.int32, (16, wide), 0)
        segs = jnp.zeros((16, wide), F32)
        for i in range(rows // wide):
            segs = jnp.where(line == i, seg_ref[:, i * wide:(i + 1) * wide].astype(F32), segs)
        k_ref[rows:, :] = segs.astype(BF16)
        v_ref[...] = acc_v[...].astype(BF16)


def q_kernel(x_ref, w_ref, tab_ref, q_ref):
    flat = jnp.dot(x_ref[...], w_ref[...], preferred_element_type=F32)
    factor = math.log2(math.e) / math.sqrt(HD)
    for j in range(q_ref.shape[0]):
        q_ref[j] = norm_rope(flat[:, j * HD:(j + 1) * HD], tab_ref[:, :HD], tab_ref[:, HD:], factor)


def route_kernel(ctx, cap, dest_ref, pos_ref, *slot_refs):
    rows = dest_ref.shape[1]
    mine_c, mine_r = lax.axis_index("ctx"), lax.axis_index("rep")
    dest = dest_ref[...]
    owner = lax.div(dest, rows)
    slot = dest - owner * rows
    owner_col = column_of(owner.astype(F32))
    ii = lax.broadcasted_iota(jnp.int32, (rows, rows), 0)
    jj = lax.broadcasted_iota(jnp.int32, (rows, rows), 1)
    before = (owner_col == owner.astype(F32)) & (ii < jj)
    rank = jnp.sum(jnp.where(before, 1.0, 0.0), axis=0, keepdims=True).astype(jnp.int32)
    near_c = jnp.bitwise_xor(lax.div(owner, 2), mine_c)
    near_r = jnp.bitwise_xor(lax.rem(owner, 2), mine_r)
    pos = (near_c * 2 + near_r) * cap + rank
    pos_ref[...] = jnp.broadcast_to(pos, pos_ref.shape)
    pos_col = column_of(pos.astype(F32))
    target_col = column_of((near_r * rows + slot).astype(F32)) + 1.0
    lanes = slot_refs[0].shape[1]
    for k in range(ctx):
        lane = lax.broadcasted_iota(jnp.int32, (rows, lanes), 1)
        hit = (pos_col == (lane + k * 2 * cap).astype(F32)) & (lane < 2 * cap)
        got = jnp.sum(jnp.where(hit, target_col, 0.0), axis=0, keepdims=True) - 1.0
        slot_refs[k][...] = jnp.broadcast_to(got.astype(jnp.int32), slot_refs[k].shape)


def documents(k_ref, rows):
    wide = k_ref.shape[1]
    lines = k_ref[rows:rows + 16, :].astype(F32)
    return jnp.concatenate([lines[i:i + 1] for i in range(rows // wide)], 1)


def add_block(q_ref, k_ref, v_ref, acc_ref, seg_col, lowest, valid, own, fresh):
    heads, rows = q_ref.shape[0], q_ref.shape[1]
    kv_heads = v_ref.shape[1] // HD
    groups = heads // kv_heads
    seg = documents(k_ref, rows)
    seen = valid & (jnp.max(seg) == lowest) if not own else True

    def compute():
        visible = seg == seg_col
        if own:
            ii = lax.broadcasted_iota(jnp.int32, (rows, rows), 0)
            jj = lax.broadcasted_iota(jnp.int32, (rows, rows), 1)
            visible = visible & (jj <= ii)
        bias = jnp.where(visible, 0.0, HIDE)
        for g in range(kv_heads):
            keys = k_ref[0:rows, g * HD:(g + 1) * HD]
            vals = jnp.concatenate([v_ref[:, g * HD:(g + 1) * HD], jnp.ones((rows, HD), BF16)], 1)

            def head(j, _):
                s = lax.dot_general(q_ref[j], keys, (((1,), (1,)), ((), ())), preferred_element_type=F32)
                p = jnp.exp2(s + bias).astype(BF16)
                new = jnp.dot(p, vals, preferred_element_type=F32)
                if fresh:
                    acc_ref[j] = new
                else:
                    acc_ref[j] += new
                return 0

            lax.fori_loop(g * groups, (g + 1) * groups, head, 0, unroll=2)

    if own:
        compute()
    else:
        pl.when(seen)(compute)


def near_kernel(n_hops, q_ref, *refs):
    acc_ref = refs[-1]
    blocks = [(refs[2 * i], refs[2 * i + 1]) for i in range(len(refs) // 2)]
    rows = q_ref.shape[1]
    c, r = lax.axis_index("ctx"), lax.axis_index("rep")
    seg = documents(blocks[0][0], rows)
    seg_col = column_of(seg)
    lowest = jnp.min(seg)
    add_block(q_ref, *blocks[0], acc_ref, seg_col, lowest, True, True, True)
    add_block(q_ref, *blocks[1], acc_ref, seg_col, lowest, r == 1, False, False)
    for i, (k_ref, v_ref) in enumerate(blocks[2:]):
        add_block(q_ref, k_ref, v_ref, acc_ref, seg_col, lowest, c >= i // 2 + 1, False, False)


def far_kernel(hop, q_ref, seg_ref, k0, v0, k1, v1, near_ref, w_ref, att_ref, *rest):
    n_out = len(rest) - 5
    outs, (acc, held, w_buf, sem_a, sem_w) = rest[:n_out], rest[n_out:]
    rows = q_ref.shape[1]
    heads = q_ref.shape[0]
    n_other = lax.axis_size("head") - 1
    half = w_buf.shape[1] // n_other
    c, r, h = lax.axis_index("ctx"), lax.axis_index("rep"), lax.axis_index("head")
    load = pltpu.make_async_copy(near_ref, held, sem_a)
    load.start()
    wide = []
    for d in range(n_other):
        from_ = pl.multiple_of(jnp.bitwise_xor(h, d + 1) * half, half)
        wide.append(pltpu.make_async_copy(w_ref.at[:, pl.ds(from_, half)], w_buf.at[:, pl.ds(d * half, half)], sem_w.at[d]))
        wide[-1].start()
    seg = seg_ref[...].astype(F32)
    seg_col = column_of(seg)
    lowest = jnp.min(seg)
    acc[...] = jnp.zeros_like(acc)
    add_block(q_ref, k0, v0, acc, seg_col, lowest, c >= hop, False, False)
    add_block(q_ref, k1, v1, acc, seg_col, lowest, (c >= hop) & (r == 0), False, False)
    load.wait()
    for j in range(heads):
        both = acc[j] + held[j]
        att_ref[:, j * HD:(j + 1) * HD] = (both[:, :HD] / both[:, HD:]).astype(BF16)
    for copy in wide:
        copy.wait()
    at = 0
    for out in outs:
        width = out.shape[1]
        out[...] = jnp.dot(att_ref[...], w_buf[:, at:at + width], preferred_element_type=F32).astype(BF16)
        at += width


def own_kernel(att_ref, w_ref, *rest):
    n_out = len(rest) - 2
    outs, (w_buf, sem) = rest[:n_out], rest[n_out:]
    half = w_buf.shape[1]
    h = lax.axis_index("head")
    copies, at = [], 0
    for i, out in enumerate(outs):
        width = out.shape[1]
        from_ = pl.multiple_of(h * half + at, 128)
        copies.append(pltpu.make_async_copy(w_ref.at[:, pl.ds(from_, width)], w_buf.at[:, pl.ds(at, width)], sem.at[i]))
        copies[-1].start()
        at += width
    at = 0
    for i, out in enumerate(outs):
        width = out.shape[1]
        copies[i].wait()
        out[...] = jnp.dot(att_ref[...], w_buf[:, at:at + width], preferred_element_type=F32).astype(BF16)
        at += width


def pick_kernel(n_head, pos_ref, *refs):
    shares, outs = refs[:n_head], refs[n_head:]
    rows = shares[0].shape[0]
    span = outs[0].shape[0]
    total = shares[0][...].astype(F32)
    for share in shares[1:]:
        total = total + share[...].astype(F32)
    total = total.astype(BF16)
    pos = pos_ref[0:1, :]
    every = span * len(outs)
    pick = jnp.where(lax.broadcasted_iota(jnp.int32, (every, rows), 0) == pos, 1.0, 0.0).astype(BF16)
    moved = jnp.dot(pick, total, preferred_element_type=F32).astype(BF16)
    for k, out in enumerate(outs):
        out[...] = moved[k * span:(k + 1) * span]


def place_kernel(ctx, rows, *refs):
    blocks, slots, (mine_ref, pair_ref) = refs[:ctx], refs[ctx:2 * ctx], refs[2 * ctx:]
    span = blocks[0].shape[0]
    total = None
    for block, slot in zip(blocks, slots, strict=True):
        at = lax.broadcasted_iota(jnp.int32, (2 * rows, span), 0) == slot[0:1, 0:span]
        put = jnp.dot(jnp.where(at, 1.0, 0.0).astype(BF16), block[...], preferred_element_type=F32)
        total = put if total is None else total + put
    mine_ref[...] = total[:rows].astype(BF16)
    pair_ref[...] = total[rows:].astype(BF16)


def join_kernel(n, *refs):
    out = refs[-1]
    at = 0
    for mine, other in zip(refs[:n], refs[n:2 * n], strict=True):
        width = mine.shape[1]
        out[:, at:at + width] = (mine[...].astype(F32) + other[...].astype(F32)).astype(BF16)
        at += width


def local(tokens, doc_ids, dest_rows, w_query, w_key, w_value, w_out):
    ctx, rep, n_head = lax.axis_size("ctx"), lax.axis_size("rep"), lax.axis_size("head")
    rows, width = tokens.shape
    kv_cols, q_cols = w_key.shape[1], w_query.shape[1]
    heads = q_cols // HD
    out_cols = w_out.shape[1]
    half = out_cols // n_head
    others = n_head - 1
    hops = ctx // 2
    cap = 3 * (rows // (2 * ctx * rep))
    span = 2 * cap
    lanes = -(-span // 128) * 128
    every = ctx * span
    sds = jax.ShapeDtypeStruct
    chunks = (half // 4, half - half // 4)

    up = [(i, i + 1) for i in range(ctx - 1)]
    swap = [(0, 1), (1, 0)]
    seg_row = doc_ids.reshape(1, rows)

    parts = 4
    depth = width // parts
    key0, val0, table = pl.pallas_call(
        kv_kernel,
        grid=(parts,),
        in_specs=[
            pl.BlockSpec((rows, depth), lambda i: (0, i)),
            pl.BlockSpec((depth, kv_cols), lambda i: (i, 0)),
            pl.BlockSpec((depth, kv_cols), lambda i: (i, 0)),
            pl.BlockSpec((1, rows), lambda i: (0, 0)),
        ],
        out_specs=[
            pl.BlockSpec((rows + 16, kv_cols), lambda i: (0, 0)),
            pl.BlockSpec((rows, kv_cols), lambda i: (0, 0)),
            pl.BlockSpec((rows, 2 * HD), lambda i: (0, 0)),
        ],
        out_shape=[sds((rows + 16, kv_cols), BF16), sds((rows, kv_cols), BF16), sds((rows, 2 * HD), F32)],
        scratch_shapes=[pltpu.VMEM((rows, kv_cols), F32), pltpu.VMEM((rows, kv_cols), F32)],
        compiler_params=params(12),
        cost_estimate=cost(4 * rows * width * kv_cols, 2 * width * (rows + 2 * kv_cols)),
        name="keys_values",
    )(tokens, w_key, w_value, seg_row)

    hop_k, hop_v = [key0], [val0]
    for _ in range(hops):
        hop_k.append(lax.ppermute(hop_k[-1], "ctx", up))
        hop_v.append(lax.ppermute(hop_v[-1], "ctx", up))

    step = 2
    queries = pl.pallas_call(
        q_kernel,
        grid=(heads // step,),
        in_specs=[
            pl.BlockSpec((rows, width), lambda i: (0, 0)),
            pl.BlockSpec((width, step * HD), lambda i: (0, i)),
            pl.BlockSpec((rows, 2 * HD), lambda i: (0, 0)),
        ],
        out_specs=pl.BlockSpec((step, rows, HD), lambda i: (i, 0, 0)),
        out_shape=sds((heads, rows, HD), BF16),
        compiler_params=params(16),
        cost_estimate=cost(2 * rows * width * q_cols, 2 * width * (rows + q_cols)),
        name="queries",
    )(tokens, w_query, table)

    route = pl.pallas_call(
        functools.partial(route_kernel, ctx, cap),
        in_specs=[VMEM],
        out_specs=[VMEM] * (1 + ctx),
        out_shape=[sds((8, rows), jnp.int32)] + [sds((8, lanes), jnp.int32)] * ctx,
        compiler_params=params(8),
        cost_estimate=cost(4 * rows * rows, 8 * rows * 4),
        name="routes",
    )
    dest_row, _ = lax.optimization_barrier((dest_rows.reshape(1, rows), val0))
    buffer_pos, *slots = route(dest_row)

    def across(k):
        return [(i, i ^ k) for i in range(ctx)]

    slots = [slots[0]] + [lax.ppermute(slots[k], "ctx", across(k)) for k in range(1, ctx)]

    pair_k, pair_v = [], []
    for i in range(hops + 1):
        perm = [(0, 1)] if i == 0 else [(1, 0)] if i == hops else swap
        pair_k.append(lax.ppermute(hop_k[i], "rep", perm))
        pair_v.append(lax.ppermute(hop_v[i], "rep", perm))

    blocks = []
    for i in range(hops):
        blocks += [hop_k[i], hop_v[i], pair_k[i], pair_v[i]]
    work = heads * rows * rows
    near = pl.pallas_call(
        functools.partial(near_kernel, hops),
        in_specs=[VMEM] * (1 + len(blocks)),
        out_specs=VMEM,
        out_shape=sds((heads, rows, 2 * HD), F32),
        compiler_params=params(16),
        cost_estimate=cost(8 * work * HD * hops, 8 * MIB, 2 * work * hops),
        name="near_attention",
    )(queries, *blocks)

    attended, *far = pl.pallas_call(
        functools.partial(far_kernel, hops),
        in_specs=[VMEM] * 6 + [ANY, ANY],
        out_specs=[VMEM] * (1 + others * len(chunks)),
        out_shape=[sds((rows, heads * HD), BF16)] + [sds((rows, n), BF16) for n in chunks] * others,
        scratch_shapes=[
            pltpu.VMEM((heads, rows, 2 * HD), F32),
            pltpu.VMEM((heads, rows, 2 * HD), F32),
            pltpu.VMEM((heads * HD, others * half), BF16),
            pltpu.SemaphoreType.DMA,
            pltpu.SemaphoreType.DMA((others,)),
        ],
        compiler_params=params(28),
        cost_estimate=cost(8 * work * HD + 2 * rows * heads * HD * half, 10 * MIB, 2 * work),
        name="far_attention_project",
    )(queries, seg_row, hop_k[hops], hop_v[hops], pair_k[hops], pair_v[hops], near, w_out)

    theirs = []
    for j in range(len(chunks)):
        flips = [[(i, i ^ (d + 1)) for i in range(n_head)] for d in range(others)]
        theirs.append([lax.ppermute(far[d * len(chunks) + j], "head", flips[d]) for d in range(others)])

    ours = pl.pallas_call(
        own_kernel,
        in_specs=[VMEM, ANY],
        out_specs=[VMEM] * len(chunks),
        out_shape=[sds((rows, n), BF16) for n in chunks],
        scratch_shapes=[pltpu.VMEM((heads * HD, half), BF16), pltpu.SemaphoreType.DMA((len(chunks),))],
        compiler_params=params(12),
        cost_estimate=cost(2 * rows * heads * HD * half, 5 * MIB),
        name="project_own",
    )(attended, w_out)

    kept, gone = [], []
    for mine, other in zip(ours, theirs, strict=True):
        n = mine.shape[1]
        moved = pl.pallas_call(
            functools.partial(pick_kernel, n_head),
            in_specs=[VMEM] * (1 + n_head),
            out_specs=[VMEM] * ctx,
            out_shape=[sds((span, n), BF16)] * ctx,
            compiler_params=params(8),
            cost_estimate=cost(2 * every * rows * n, 2 * n * (2 * rows + every)),
            name="add_pick",
        )(buffer_pos, mine, *other)
        got = [moved[0]] + [lax.ppermute(moved[k], "ctx", across(k)) for k in range(1, ctx)]
        stay, leave = pl.pallas_call(
            functools.partial(place_kernel, ctx, rows),
            in_specs=[VMEM] * (2 * ctx),
            out_specs=[VMEM] * 2,
            out_shape=[sds((rows, n), BF16)] * 2,
            compiler_params=params(8),
            cost_estimate=cost(4 * every * rows * n, 2 * n * (2 * rows + every)),
            name="place",
        )(*got, *slots)
        kept.append(stay)
        gone.append(lax.ppermute(leave, "rep", swap))

    return pl.pallas_call(
        functools.partial(join_kernel, len(chunks)),
        in_specs=[VMEM] * (2 * len(chunks)),
        out_specs=VMEM,
        out_shape=sds((rows, half), BF16),
        compiler_params=params(8),
        cost_estimate=cost(rows * half, 6 * rows * half),
        name="join",
    )(*kept, *gone)


def solution(mesh):
    return jax.shard_map(
        local,
        mesh=mesh,
        in_specs=(
            P(("grp", "ctx", "rep"), None),
            P(("grp", "ctx", "rep")),
            P(("grp", "ctx", "rep")),
            P(None, "head"),
            P(None, "head"),
            P(None, "head"),
            P("head", None),
        ),
        out_specs=P(("grp", "ctx", "rep"), "head"),
        check_vma=False,
    )
```

```python
import functools
import math

import jax
import jax.numpy as jnp
from jax import lax
from jax.experimental import pallas as pl
from jax.experimental.pallas import tpu as pltpu
from jax.sharding import PartitionSpec as P

HD = 128
THETA = 1000000.0
EPSILON = 1e-06
HIDE = -1e30
F32 = jnp.float32
BF16 = jnp.bfloat16
VMEM = pl.BlockSpec(memory_space=pltpu.VMEM)
ANY = pl.BlockSpec(memory_space=pl.ANY)
MIB = 1 << 20
KV_MIB = 53
Q_MIB = 51
FAR_MIB = 44
PROJECT_MIB = 48


def params(mib):
    return pltpu.CompilerParams(vmem_limit_bytes=mib * MIB)


def cost(flops, nbytes, trans=0):
    return pl.CostEstimate(flops=int(flops), bytes_accessed=int(nbytes), transcendentals=int(trans))


def column_of(row):
    n = row.shape[1]
    at = lax.broadcasted_iota(jnp.int32, (n, n), 0) == lax.broadcasted_iota(jnp.int32, (n, n), 1)
    return jnp.sum(jnp.where(at, row, 0.0), axis=1, keepdims=True)


def norm_rope(heads, cosine, sine, factor):
    scale = lax.rsqrt(jnp.mean(heads * heads, axis=-1, keepdims=True) + EPSILON)
    if factor != 1.0:
        scale = scale * factor
    turned = pltpu.roll(heads, HD // 2, 1)
    return ((heads * cosine + turned * sine) * scale).astype(BF16)


def kv_kernel(parts, x_hbm, wk_hbm, wv_hbm, seg_ref, kv_ref, tab_ref, x_buf, w_buf, sem):
    rows, width = x_buf.shape
    kv_cols = w_buf.shape[1] // 2
    depth = width // parts
    copies = []
    for i in range(parts):
        at = pl.ds(i * depth, depth)
        copies.append([
            pltpu.make_async_copy(x_hbm.at[:, at], x_buf.at[:, at], sem.at[3 * i]),
            pltpu.make_async_copy(wk_hbm.at[at, :], w_buf.at[at, pl.ds(0, kv_cols)], sem.at[3 * i + 1]),
            pltpu.make_async_copy(wv_hbm.at[at, :], w_buf.at[at, pl.ds(kv_cols, kv_cols)], sem.at[3 * i + 2]),
        ])
        for copy in copies[-1]:
            copy.start()
    first = (lax.axis_index("ctx") * 2 + lax.axis_index("rep")) * rows
    lane = lax.broadcasted_iota(jnp.int32, (1, HD), 1)
    freq = jnp.exp(lax.rem(lane, HD // 2).astype(F32) * (-2.0 * math.log(THETA) / HD))
    pos = (first + lax.broadcasted_iota(jnp.int32, (rows, HD), 0)).astype(F32)
    angle = pos * freq
    tab_ref[:, :HD] = jnp.cos(angle)
    tab_ref[:, HD:] = jnp.where(lane < HD // 2, -1.0, 1.0) * jnp.sin(angle)
    line = lax.broadcasted_iota(jnp.int32, (16, kv_cols), 0)
    segs = jnp.zeros((16, kv_cols), F32)
    for i in range(rows // kv_cols):
        segs = jnp.where(line == i, seg_ref[:, i * kv_cols:(i + 1) * kv_cols].astype(F32), segs)
    kv_ref[rows:, :kv_cols] = segs.astype(BF16)
    kv_ref[rows:, kv_cols:] = jnp.zeros((16, kv_cols), BF16)
    total = None
    for i in range(parts):
        for copy in copies[i]:
            copy.wait()
        at = slice(i * depth, (i + 1) * depth)
        part = jnp.dot(x_buf[:, at], w_buf[at, :], preferred_element_type=F32)
        total = part if total is None else total + part
    for at in range(0, kv_cols, HD):
        kv_ref[0:rows, at:at + HD] = norm_rope(total[:, at:at + HD], tab_ref[:, :HD], tab_ref[:, HD:], 1.0)
    kv_ref[0:rows, kv_cols:] = total[:, kv_cols:].astype(BF16)


def q_kernel(parts, x_hbm, w_hbm, tab_ref, q_ref, x_ref, w_buf, sem):
    heads = q_ref.shape[0]
    wide = w_buf.shape[1] // parts
    factor = math.log2(math.e) / math.sqrt(HD)
    tokens = pltpu.make_async_copy(x_hbm, x_ref, sem.at[parts])
    tokens.start()
    copies = []
    for i in range(parts):
        at = pl.ds(i * wide, wide)
        copies.append(pltpu.make_async_copy(w_hbm.at[:, at], w_buf.at[:, at], sem.at[i]))
        copies[-1].start()

    def finish(i, flat):
        for j in range(wide // HD):
            done = norm_rope(flat[:, j * HD:(j + 1) * HD], tab_ref[:, :HD], tab_ref[:, HD:], factor)
            q_ref[i * (wide // HD) + j] = done

    held = None
    tokens.wait()
    for i in range(parts):
        copies[i].wait()
        flat = jnp.dot(x_ref[...], w_buf[:, i * wide:(i + 1) * wide], preferred_element_type=F32)
        if i:
            finish(i - 1, held)
        held = flat
    finish(parts - 1, held)


def route_kernel(ctx, cap, dest_ref, pos_ref, *slot_refs):
    rows = dest_ref.shape[1]
    mine_c, mine_r = lax.axis_index("ctx"), lax.axis_index("rep")
    dest = dest_ref[...]
    owner = lax.div(dest, rows)
    slot = dest - owner * rows
    owner_col = column_of(owner.astype(F32))
    ii = lax.broadcasted_iota(jnp.int32, (rows, rows), 0)
    jj = lax.broadcasted_iota(jnp.int32, (rows, rows), 1)
    before = (owner_col == owner.astype(F32)) & (ii < jj)
    rank = jnp.sum(jnp.where(before, 1.0, 0.0), axis=0, keepdims=True).astype(jnp.int32)
    near_c = jnp.bitwise_xor(lax.div(owner, 2), mine_c)
    near_r = jnp.bitwise_xor(lax.rem(owner, 2), mine_r)
    pos = (near_c * 2 + near_r) * cap + rank
    pos_ref[...] = jnp.broadcast_to(pos, pos_ref.shape)
    pos_col = column_of(pos.astype(F32))
    target_col = column_of(slot.astype(F32)) + 1.0
    lanes = slot_refs[0].shape[1]
    for k in range(ctx):
        lane = lax.broadcasted_iota(jnp.int32, (rows, lanes), 1)
        hit = (pos_col == (lane + k * 2 * cap).astype(F32)) & (lane < 2 * cap)
        got = jnp.sum(jnp.where(hit, target_col, 0.0), axis=0, keepdims=True) - 1.0
        slot_refs[k][...] = jnp.broadcast_to(got, slot_refs[k].shape)


def documents(kv_ref):
    wide = kv_ref.shape[1] // 2
    rows = kv_ref.shape[0] - 16
    lines = kv_ref[rows:rows + 16, :wide].astype(F32)
    return jnp.concatenate([lines[i:i + 1] for i in range(rows // wide)], 1)


def attend(q_ref, blocks, biases, finish):
    heads, rows = q_ref.shape[0], q_ref.shape[1]
    kv_cols = blocks[0].shape[1] // 2
    kv_heads = kv_cols // HD
    groups = heads // kv_heads
    for g in range(kv_heads):
        at = g * HD
        keys = [b[0:rows, at:at + HD] for b in blocks]
        ones = jnp.ones((rows, HD), BF16)
        vals = [jnp.concatenate([b[0:rows, kv_cols + at:kv_cols + at + HD], ones], 1) for b in blocks]
        vals = jnp.concatenate(vals, 0) if len(vals) > 1 else vals[0]

        def head(j, _):
            weights = []
            for key, bias in zip(keys, biases, strict=True):
                s = lax.dot_general(q_ref[j], key, (((1,), (1,)), ((), ())), preferred_element_type=F32)
                weights.append(jnp.exp2(s + bias[...]).astype(BF16))
            p = jnp.concatenate(weights, 1) if len(weights) > 1 else weights[0]
            finish(j, jnp.dot(p, vals, preferred_element_type=F32))
            return 0

        lax.fori_loop(g * groups, (g + 1) * groups, head, 0, unroll=8)


def hide(bias_ref, kv_ref, seg_col):
    bias_ref[...] = jnp.where(documents(kv_ref) == seg_col, 0.0, HIDE)


def choose(to_ref, flag, yes_ref, no_ref):
    @pl.when(flag)
    def _():
        to_ref[...] = yes_ref[...]

    @pl.when(jnp.logical_not(flag))
    def _():
        to_ref[...] = no_ref[...]


def near_kernel(hops, seg_ref, q_ref, *refs):
    hop, pair, out_ref = refs[:hops], refs[hops:2 * hops], refs[2 * hops]
    odd, bias = refs[2 * hops + 1:-1], refs[-1]
    rows = q_ref.shape[1]
    c, r = lax.axis_index("ctx"), lax.axis_index("rep")
    seg = seg_ref[...].astype(F32)
    seg_col = column_of(seg)
    lowest = jnp.min(seg)
    ii = lax.broadcasted_iota(jnp.int32, (rows, rows), 0)
    jj = lax.broadcasted_iota(jnp.int32, (rows, rows), 1)
    bias[0] = jnp.where((seg == seg_col) & (jj <= ii), 0.0, HIDE)
    blocks = [hop[0]]
    for i in range(1, hops):
        choose(odd[i - 1], r == 1, pair[i - 1], pair[i])
        blocks += [odd[i - 1], hop[i]]
    me = c * 2 + r
    size = 3
    for start in range(0, len(blocks), size):
        some = blocks[start:start + size]
        seen = []
        for d in range(start, start + len(some)):
            if d:
                hide(bias.at[d], blocks[d], seg_col)
                seen.append((me >= d) & (jnp.max(documents(blocks[d])) == lowest))
        count = sum([x.astype(jnp.int32) for x in seen]) + (1 if start == 0 else 0)
        for n in range(1, len(some) + 1):
            @pl.when(count == n)
            def _(n=n, start=start, some=some):
                def finish(j, new):
                    if start == 0:
                        out_ref[j] = new
                    else:
                        out_ref[j] += new
                attend(q_ref, some[:n], [bias.at[start + i] for i in range(n)], finish)


def far_kernel(hops, n_other, seg_ref, q_ref, far_ref, to_one, to_zero, near_ref, w_hbm, att_ref, *rest):
    outs, (odd, bias, w_buf, sem) = rest[:n_other], rest[n_other:]
    heads = q_ref.shape[0]
    c, r, h = lax.axis_index("ctx"), lax.axis_index("rep"), lax.axis_index("head")
    start, finish_projection = project(att_ref, w_hbm, w_buf, sem, outs, [(jnp.bitwise_xor(h, d + 1), 0) for d in range(n_other)])
    start()
    seg = seg_ref[...].astype(F32)
    seg_col = column_of(seg)
    lowest = jnp.min(seg)
    choose(odd, r == 1, to_one, to_zero)
    blocks = [odd, far_ref]
    me = c * 2 + r
    seen = []
    for i, d in enumerate((2 * hops - 1, 2 * hops)):
        hide(bias.at[i], blocks[i], seg_col)
        seen.append(((me >= d) & (jnp.max(documents(blocks[i])) == lowest)).astype(jnp.int32))
    count = sum(seen)

    def put(j, both):
        at = j * HD if isinstance(j, int) else pl.multiple_of(j * HD, HD)
        att_ref[:, pl.ds(at, HD)] = (both[:, :HD] / both[:, HD:]).astype(BF16)

    @pl.when(count == 0)
    def _():
        for j in range(heads):
            put(j, near_ref[j])

    for n in (1, 2):
        @pl.when(count == n)
        def _(n=n):
            attend(q_ref, blocks[:n], [bias.at[i] for i in range(n)], lambda j, new: put(j, near_ref[j] + new))

    finish_projection()


def project(att_ref, w_hbm, w_buf, sem, outs, steps):
    half = w_hbm.shape[1] // lax.axis_size("head")
    copies, at = [], 0
    for i, (out, (group, col)) in enumerate(zip(outs, steps, strict=True)):
        wide = out.shape[1]
        from_ = pl.multiple_of(group * half + col, 128)
        copies.append(pltpu.make_async_copy(w_hbm.at[:, pl.ds(from_, wide)], w_buf.at[:, pl.ds(at, wide)], sem.at[i]))
        at += wide

    def start():
        for copy in copies:
            copy.start()

    def finish():
        at = 0
        for out, copy in zip(outs, copies, strict=True):
            copy.wait()
            wide = out.shape[1]
            out[...] = jnp.dot(att_ref[...], w_buf[:, at:at + wide], preferred_element_type=F32).astype(BF16)
            at += wide

    return start, finish


def project_kernel(steps, att_ref, w_hbm, *refs):
    outs, (w_buf, sem) = refs[:len(steps)], refs[len(steps):]
    h = lax.axis_index("head")
    steps = [(jnp.bitwise_xor(h, flip), at) for flip, at in steps]
    start, finish = project(att_ref, w_hbm, w_buf, sem, outs, steps)
    start()
    finish()


def pick_kernel(n_head, ctx, with_slots, span, mark, pos_ref, *refs):
    slots = refs[:ctx] if with_slots else ()
    refs = refs[len(slots):]
    shares, outs = refs[:n_head], refs[n_head:]
    rows = shares[0].shape[0]
    total = shares[0][...].astype(F32)
    for share in shares[1:]:
        total = total + share[...].astype(F32)
    total = total.astype(BF16)
    every = span * ctx
    pick = jnp.where(lax.broadcasted_iota(jnp.int32, (every, rows), 0) == pos_ref[0:1, :], 1.0, 0.0).astype(BF16)
    moved = jnp.dot(pick, total, preferred_element_type=F32).astype(BF16)
    for k, out in enumerate(outs):
        out[0:span, :] = moved[k * span:(k + 1) * span]
        if with_slots:
            out[mark:, :] = jnp.zeros((16, out.shape[1]), BF16)
            lanes = slots[k].shape[1]
            out[mark:, 0:lanes] = jnp.concatenate([slots[k][...]] * 2, 0).astype(BF16)


def place_kernel(ctx, cap, rows, mark, *refs):
    blocks, marked, (mine_ref, pair_ref) = refs[:ctx], refs[ctx:2 * ctx], refs[2 * ctx:]
    span = 2 * cap
    total = None
    for block, marks in zip(blocks, marked, strict=True):
        slot = marks[mark:mark + 16, 0:span].astype(F32)[0:1].astype(jnp.int32)
        lane = lax.broadcasted_iota(jnp.int32, (1, span), 1)
        slot = jnp.where((slot >= 0) & (lane >= cap), slot + rows, slot)
        at = lax.broadcasted_iota(jnp.int32, (2 * rows, span), 0) == slot
        put = jnp.dot(jnp.where(at, 1.0, 0.0).astype(BF16), block[0:span, :], preferred_element_type=F32)
        total = put if total is None else total + put
    mine_ref[...] = total[:rows].astype(BF16)
    pair_ref[...] = total[rows:].astype(BF16)


def join_kernel(n, *refs):
    out = refs[-1]
    at = 0
    for mine, other in zip(refs[:n], refs[n:2 * n], strict=True):
        width = mine.shape[1]
        out[:, at:at + width] = (mine[...].astype(F32) + other[...].astype(F32)).astype(BF16)
        at += width


def after(x, *earlier):
    return lax.optimization_barrier((x, *earlier))[0]


def local(tokens, doc_ids, dest_rows, w_query, w_key, w_value, w_out):
    ctx, rep, n_head = lax.axis_size("ctx"), lax.axis_size("rep"), lax.axis_size("head")
    rows, width = tokens.shape
    kv_cols, q_cols = w_key.shape[1], w_query.shape[1]
    heads = q_cols // HD
    half = w_out.shape[1] // n_head
    others = n_head - 1
    hops = ctx // 2
    cap = 3 * (rows // (2 * ctx * rep))
    span = 2 * cap
    lanes = -(-span // 128) * 128
    every = ctx * span
    sds = jax.ShapeDtypeStruct
    chunks = (half // 2, half - half // 2)

    up = [(i, i + 1) for i in range(ctx - 1)]
    swap = [(0, 1), (1, 0)]
    seg_row = doc_ids.reshape(1, rows)

    parts = 4
    payload = sds((rows + 16, 2 * kv_cols), BF16)
    own, table = pl.pallas_call(
        functools.partial(kv_kernel, parts),
        in_specs=[ANY, ANY, ANY, VMEM],
        out_specs=[VMEM] * 2,
        out_shape=[payload, sds((rows, 2 * HD), F32)],
        scratch_shapes=[
            pltpu.VMEM((rows, width), BF16),
            pltpu.VMEM((width, 2 * kv_cols), BF16),
            pltpu.SemaphoreType.DMA((3 * parts,)),
        ],
        compiler_params=params(KV_MIB),
        cost_estimate=cost(4 * rows * width * kv_cols, 2 * width * (rows + 2 * kv_cols)),
        name="keys_values",
    )(tokens, w_key, w_value, seg_row)

    hop = [own, lax.ppermute(own, "ctx", up)]
    pair = [lax.ppermute(own, "rep", [(0, 1)])]

    parts = 4
    queries = pl.pallas_call(
        functools.partial(q_kernel, parts),
        in_specs=[ANY, ANY, VMEM],
        out_specs=VMEM,
        out_shape=sds((heads, rows, HD), BF16),
        scratch_shapes=[pltpu.VMEM((rows, width), BF16), pltpu.VMEM((width, q_cols), BF16), pltpu.SemaphoreType.DMA((parts + 1,))],
        compiler_params=params(Q_MIB),
        cost_estimate=cost(2 * rows * width * q_cols, 2 * width * (rows + q_cols)),
        name="queries",
    )(tokens, w_query, table)

    for i in range(1, hops + 1):
        if i == 1:
            hop[1] = after(hop[1], queries)
        if i < hops:
            hop.append(lax.ppermute(hop[i], "ctx", up))
            pair.append(lax.ppermute(hop[i], "rep", swap))

    route = pl.pallas_call(
        functools.partial(route_kernel, ctx, cap),
        in_specs=[VMEM],
        out_specs=[VMEM] * (1 + ctx),
        out_shape=[sds((8, rows), jnp.int32)] + [sds((8, lanes), F32)] * ctx,
        compiler_params=params(8),
        cost_estimate=cost(4 * rows * rows, 8 * rows * 4),
        name="routes",
    )
    buffer_pos, *slots = route(after(dest_rows.reshape(1, rows), queries))

    work = heads * rows * rows
    near = pl.pallas_call(
        functools.partial(near_kernel, hops),
        in_specs=[VMEM] * (2 + 2 * hops),
        out_specs=VMEM,
        out_shape=sds((heads, rows, 2 * HD), F32),
        scratch_shapes=[pltpu.VMEM(payload.shape, BF16)] * (hops - 1) + [pltpu.VMEM((2 * hops - 1, rows, rows), F32)],
        compiler_params=params(12),
        cost_estimate=cost(8 * work * HD * hops, 8 * MIB, 2 * work * hops),
        name="near_attention",
    )(after(seg_row, buffer_pos), queries, *hop[:hops], *pair[:hops])

    hop[hops] = after(hop[hops], near)
    pair.append(lax.ppermute(hop[hops], "rep", [(1, 0)]))

    widths = chunks[:1] * others
    attended, *sent = pl.pallas_call(
        functools.partial(far_kernel, hops, others),
        in_specs=[VMEM] * 6 + [ANY],
        out_specs=[VMEM] * (1 + others),
        out_shape=[sds((rows, heads * HD), BF16)] + [sds((rows, n), BF16) for n in widths],
        scratch_shapes=[pltpu.VMEM(payload.shape, BF16), pltpu.VMEM((2, rows, rows), F32)]
        + [pltpu.VMEM((heads * HD, sum(widths)), BF16), pltpu.SemaphoreType.DMA((others,))],
        compiler_params=params(FAR_MIB),
        cost_estimate=cost(8 * work * HD + 2 * rows * heads * HD * chunks[0], 10 * MIB, 2 * work),
        name="far_attention_project",
    )(seg_row, queries, hop[hops], pair[hops - 1], pair[hops], near, w_out)

    def project_some(x, steps, sizes):
        return pl.pallas_call(
            functools.partial(project_kernel, steps),
            in_specs=[VMEM, ANY],
            out_specs=[VMEM] * len(steps),
            out_shape=[sds((rows, n), BF16) for n in sizes],
            scratch_shapes=[pltpu.VMEM((heads * HD, sum(sizes)), BF16), pltpu.SemaphoreType.DMA((len(steps),))],
            compiler_params=params(PROJECT_MIB),
            cost_estimate=cost(2 * rows * heads * HD * sum(sizes), 2 * heads * HD * sum(sizes)),
            name="project",
        )(x, w_out)

    flips = [[(i, i ^ (d + 1)) for i in range(n_head)] for d in range(others)]
    ours, theirs, at = [], [], 0
    for j, n in enumerate(chunks):
        theirs.append([lax.ppermute(x, "head", flip) for x, flip in zip(sent, flips, strict=True)])
        steps, sizes = [(0, at)], [n]
        at += n
        if j + 1 < len(chunks):
            steps += [(d + 1, at) for d in range(others)]
            sizes += [chunks[j + 1]] * others
        mine, *sent = project_some(after(attended, *ours[-1:], *sent), steps, sizes)
        ours.append(mine)

    def across(k):
        return [(i, i ^ k) for i in range(ctx)]

    mark = -(-span // 16) * 16
    moved, got = [], []
    for j, n in enumerate(chunks):
        extra = slots if j == 0 else []
        tall = mark + 16 if j == 0 else span
        picked = pl.pallas_call(
            functools.partial(pick_kernel, n_head, ctx, j == 0, span, mark),
            in_specs=[VMEM] * (1 + len(extra) + n_head),
            out_specs=[VMEM] * ctx,
            out_shape=[sds((tall, n), BF16)] * ctx,
            compiler_params=params(8),
            cost_estimate=cost(2 * every * rows * n, 2 * n * (2 * rows + every)),
            name="add_pick",
        )(after(buffer_pos, *moved), *extra, ours[j], *theirs[j])
        moved += picked
        got.append([picked[0]] + [lax.ppermute(picked[k], "ctx", across(k)) for k in range(1, ctx)])

    kept, gone = [], []
    for j, n in enumerate(chunks):
        first = after(got[j][0], *moved, *kept)
        stay, leave = pl.pallas_call(
            functools.partial(place_kernel, ctx, cap, rows, mark),
            in_specs=[VMEM] * (2 * ctx),
            out_specs=[VMEM] * 2,
            out_shape=[sds((rows, n), BF16)] * 2,
            compiler_params=params(8),
            cost_estimate=cost(4 * every * rows * n, 2 * n * (2 * rows + every)),
            name="place",
        )(first, *got[j][1:], *got[0])
        kept.append(stay)
        gone.append(lax.ppermute(leave, "rep", swap))

    return pl.pallas_call(
        functools.partial(join_kernel, len(chunks)),
        in_specs=[VMEM] * (2 * len(chunks)),
        out_specs=VMEM,
        out_shape=sds((rows, half), BF16),
        compiler_params=params(8),
        cost_estimate=cost(rows * half, 6 * rows * half),
        name="join",
    )(*kept, *gone)


def solution(mesh):
    return jax.shard_map(
        local,
        mesh=mesh,
        in_specs=(
            P(("grp", "ctx", "rep"), None),
            P(("grp", "ctx", "rep")),
            P(("grp", "ctx", "rep")),
            P(None, "head"),
            P(None, "head"),
            P(None, "head"),
            P("head", None),
        ),
        out_specs=P(("grp", "ctx", "rep"), "head"),
        check_vma=False,
    )
```

```python
import functools
import math

import jax
import jax.numpy as jnp
from jax import lax
from jax.experimental import pallas as pl
from jax.experimental.pallas import tpu as pltpu
from jax.sharding import PartitionSpec as P

HD = 128
THETA = 1000000.0
EPSILON = 1e-06
HIDE = -1e30
F32 = jnp.float32
BF16 = jnp.bfloat16
VMEM = pl.BlockSpec(memory_space=pltpu.VMEM)
ANY = pl.BlockSpec(memory_space=pl.ANY)
MIB = 1 << 20
KV_MIB = 53
Q_MIB = 52
FAR_MIB = 44
PROJECT_MIB = 48


def params(mib):
    return pltpu.CompilerParams(vmem_limit_bytes=mib * MIB)


def cost(flops, nbytes, trans=0):
    return pl.CostEstimate(flops=int(flops), bytes_accessed=int(nbytes), transcendentals=int(trans))


def column_of(row):
    n = row.shape[1]
    at = lax.broadcasted_iota(jnp.int32, (n, n), 0) == lax.broadcasted_iota(jnp.int32, (n, n), 1)
    return jnp.sum(jnp.where(at, row, 0.0), axis=1, keepdims=True)


def norm_rope(heads, cosine, sine, factor):
    scale = lax.rsqrt(jnp.mean(heads * heads, axis=-1, keepdims=True) + EPSILON)
    if factor != 1.0:
        scale = scale * factor
    turned = pltpu.roll(heads, HD // 2, 1)
    return ((heads * cosine + turned * sine) * scale).astype(BF16)


def kv_kernel(parts, x_hbm, wk_hbm, wv_hbm, seg_ref, kv_ref, tab_ref, x_buf, w_buf, sem):
    rows, width = x_buf.shape
    kv_cols = w_buf.shape[1] // 2
    depth = width // parts
    copies = []
    for i in range(parts):
        at = pl.ds(i * depth, depth)
        copies.append([
            pltpu.make_async_copy(x_hbm.at[:, at], x_buf.at[:, at], sem.at[3 * i]),
            pltpu.make_async_copy(wk_hbm.at[at, :], w_buf.at[at, pl.ds(0, kv_cols)], sem.at[3 * i + 1]),
            pltpu.make_async_copy(wv_hbm.at[at, :], w_buf.at[at, pl.ds(kv_cols, kv_cols)], sem.at[3 * i + 2]),
        ])
        for copy in copies[-1]:
            copy.start()
    first = (lax.axis_index("ctx") * 2 + lax.axis_index("rep")) * rows
    lane = lax.broadcasted_iota(jnp.int32, (1, HD), 1)
    freq = jnp.exp(lax.rem(lane, HD // 2).astype(F32) * (-2.0 * math.log(THETA) / HD))
    pos = (first + lax.broadcasted_iota(jnp.int32, (rows, HD), 0)).astype(F32)
    angle = pos * freq
    tab_ref[:, :HD] = jnp.cos(angle)
    tab_ref[:, HD:] = jnp.where(lane < HD // 2, -1.0, 1.0) * jnp.sin(angle)
    line = lax.broadcasted_iota(jnp.int32, (16, kv_cols), 0)
    segs = jnp.zeros((16, kv_cols), F32)
    for i in range(rows // kv_cols):
        segs = jnp.where(line == i, seg_ref[:, i * kv_cols:(i + 1) * kv_cols].astype(F32), segs)
    kv_ref[rows:, :kv_cols] = segs.astype(BF16)
    kv_ref[rows:, kv_cols:] = jnp.zeros((16, kv_cols), BF16)
    total = None
    for i in range(parts):
        for copy in copies[i]:
            copy.wait()
        at = slice(i * depth, (i + 1) * depth)
        part = jnp.dot(x_buf[:, at], w_buf[at, :], preferred_element_type=F32)
        total = part if total is None else total + part
    for at in range(0, kv_cols, HD):
        kv_ref[0:rows, at:at + HD] = norm_rope(total[:, at:at + HD], tab_ref[:, :HD], tab_ref[:, HD:], 1.0)
    kv_ref[0:rows, kv_cols:] = total[:, kv_cols:].astype(BF16)


def q_kernel(parts, x_hbm, w_hbm, tab_ref, q_ref, x_ref, w_buf, sem):
    heads = q_ref.shape[0]
    wide = w_buf.shape[1] // parts
    factor = math.log2(math.e) / math.sqrt(HD)
    tokens = pltpu.make_async_copy(x_hbm, x_ref, sem.at[parts])
    tokens.start()
    copies = []
    for i in range(parts):
        at = pl.ds(i * wide, wide)
        copies.append(pltpu.make_async_copy(w_hbm.at[:, at], w_buf.at[:, at], sem.at[i]))
        copies[-1].start()

    def finish(i, flat):
        for j in range(wide // HD):
            done = norm_rope(flat[:, j * HD:(j + 1) * HD], tab_ref[:, :HD], tab_ref[:, HD:], factor)
            q_ref[i * (wide // HD) + j] = done

    held = None
    tokens.wait()
    for i in range(parts):
        copies[i].wait()
        flat = jnp.dot(x_ref[...], w_buf[:, i * wide:(i + 1) * wide], preferred_element_type=F32)
        if i:
            finish(i - 1, held)
        held = flat
    finish(parts - 1, held)


def route_kernel(ctx, cap, dest_ref, pos_ref, *slot_refs):
    rows = dest_ref.shape[1]
    mine_c, mine_r = lax.axis_index("ctx"), lax.axis_index("rep")
    dest = dest_ref[...]
    owner = lax.div(dest, rows)
    slot = dest - owner * rows
    owner_col = column_of(owner.astype(F32))
    ii = lax.broadcasted_iota(jnp.int32, (rows, rows), 0)
    jj = lax.broadcasted_iota(jnp.int32, (rows, rows), 1)
    before = (owner_col == owner.astype(F32)) & (ii < jj)
    rank = jnp.sum(jnp.where(before, 1.0, 0.0), axis=0, keepdims=True).astype(jnp.int32)
    near_c = jnp.bitwise_xor(lax.div(owner, 2), mine_c)
    near_r = jnp.bitwise_xor(lax.rem(owner, 2), mine_r)
    pos = (near_c * 2 + near_r) * cap + rank
    pos_ref[...] = jnp.broadcast_to(pos, pos_ref.shape)
    pos_col = column_of(pos.astype(F32))
    target_col = column_of(slot.astype(F32)) + 1.0
    lanes = slot_refs[0].shape[1]
    for k in range(ctx):
        lane = lax.broadcasted_iota(jnp.int32, (rows, lanes), 1)
        hit = (pos_col == (lane + k * 2 * cap).astype(F32)) & (lane < 2 * cap)
        got = jnp.sum(jnp.where(hit, target_col, 0.0), axis=0, keepdims=True) - 1.0
        slot_refs[k][...] = jnp.broadcast_to(got, slot_refs[k].shape)


def documents(kv_ref):
    wide = kv_ref.shape[1] // 2
    rows = kv_ref.shape[0] - 16
    lines = kv_ref[rows:rows + 16, :wide].astype(F32)
    return jnp.concatenate([lines[i:i + 1] for i in range(rows // wide)], 1)


def attend(q_ref, blocks, biases, finish):
    heads, rows = q_ref.shape[0], q_ref.shape[1]
    kv_cols = blocks[0].shape[1] // 2
    kv_heads = kv_cols // HD
    groups = heads // kv_heads
    for g in range(kv_heads):
        at = g * HD
        keys = [b[0:rows, at:at + HD] for b in blocks]
        ones = jnp.ones((rows, HD), BF16)
        vals = [jnp.concatenate([b[0:rows, kv_cols + at:kv_cols + at + HD], ones], 1) for b in blocks]
        vals = jnp.concatenate(vals, 0) if len(vals) > 1 else vals[0]

        def head(j, _):
            weights = []
            for key, bias in zip(keys, biases, strict=True):
                s = lax.dot_general(q_ref[j], key, (((1,), (1,)), ((), ())), preferred_element_type=F32)
                weights.append(jnp.exp2(s + bias[...]).astype(BF16))
            p = jnp.concatenate(weights, 1) if len(weights) > 1 else weights[0]
            finish(j, jnp.dot(p, vals, preferred_element_type=F32))
            return 0

        lax.fori_loop(g * groups, (g + 1) * groups, head, 0, unroll=8)


def hide(bias_ref, kv_ref, seg_col):
    bias_ref[...] = jnp.where(documents(kv_ref) == seg_col, 0.0, HIDE)


def choose(to_ref, flag, yes_ref, no_ref):
    @pl.when(flag)
    def _():
        to_ref[...] = yes_ref[...]

    @pl.when(jnp.logical_not(flag))
    def _():
        to_ref[...] = no_ref[...]


def near_kernel(hops, seg_ref, q_ref, *refs):
    hop, pair, out_ref = refs[:hops], refs[hops:2 * hops], refs[2 * hops]
    odd, bias = refs[2 * hops + 1:-1], refs[-1]
    rows = q_ref.shape[1]
    c, r = lax.axis_index("ctx"), lax.axis_index("rep")
    seg = seg_ref[...].astype(F32)
    seg_col = column_of(seg)
    lowest = jnp.min(seg)
    ii = lax.broadcasted_iota(jnp.int32, (rows, rows), 0)
    jj = lax.broadcasted_iota(jnp.int32, (rows, rows), 1)
    bias[0] = jnp.where((seg == seg_col) & (jj <= ii), 0.0, HIDE)
    blocks = [hop[0]]
    for i in range(1, hops):
        choose(odd[i - 1], r == 1, pair[i - 1], pair[i])
        blocks += [odd[i - 1], hop[i]]
    me = c * 2 + r
    size = 3
    for start in range(0, len(blocks), size):
        some = blocks[start:start + size]
        seen = []
        for d in range(start, start + len(some)):
            if d:
                hide(bias.at[d], blocks[d], seg_col)
                seen.append((me >= d) & (jnp.max(documents(blocks[d])) == lowest))
        count = sum([x.astype(jnp.int32) for x in seen]) + (1 if start == 0 else 0)
        for n in range(1, len(some) + 1):
            @pl.when(count == n)
            def _(n=n, start=start, some=some):
                def finish(j, new):
                    if start == 0:
                        out_ref[j] = new
                    else:
                        out_ref[j] += new
                attend(q_ref, some[:n], [bias.at[start + i] for i in range(n)], finish)


def far_kernel(hops, n_other, seg_ref, q_ref, far_ref, to_one, to_zero, near_ref, w_hbm, att_ref, *rest):
    outs, (odd, bias, w_buf, sem) = rest[:n_other], rest[n_other:]
    heads = q_ref.shape[0]
    c, r, h = lax.axis_index("ctx"), lax.axis_index("rep"), lax.axis_index("head")
    start, finish_projection = project(att_ref, w_hbm, w_buf, sem, outs, [(jnp.bitwise_xor(h, d + 1), 0) for d in range(n_other)])
    start()
    seg = seg_ref[...].astype(F32)
    seg_col = column_of(seg)
    lowest = jnp.min(seg)
    choose(odd, r == 1, to_one, to_zero)
    blocks = [odd, far_ref]
    me = c * 2 + r
    seen = []
    for i, d in enumerate((2 * hops - 1, 2 * hops)):
        hide(bias.at[i], blocks[i], seg_col)
        seen.append(((me >= d) & (jnp.max(documents(blocks[i])) == lowest)).astype(jnp.int32))
    count = sum(seen)

    def put(j, both):
        at = j * HD if isinstance(j, int) else pl.multiple_of(j * HD, HD)
        att_ref[:, pl.ds(at, HD)] = (both[:, :HD] / both[:, HD:]).astype(BF16)

    @pl.when(count == 0)
    def _():
        for j in range(heads):
            put(j, near_ref[j])

    for n in (1, 2):
        @pl.when(count == n)
        def _(n=n):
            attend(q_ref, blocks[:n], [bias.at[i] for i in range(n)], lambda j, new: put(j, near_ref[j] + new))

    finish_projection()


def project(att_ref, w_hbm, w_buf, sem, outs, steps):
    half = w_hbm.shape[1] // lax.axis_size("head")
    copies, at = [], 0
    for i, (out, (group, col)) in enumerate(zip(outs, steps, strict=True)):
        wide = out.shape[1]
        from_ = pl.multiple_of(group * half + col, 128)
        copies.append(pltpu.make_async_copy(w_hbm.at[:, pl.ds(from_, wide)], w_buf.at[:, pl.ds(at, wide)], sem.at[i]))
        at += wide

    def start():
        for copy in copies:
            copy.start()

    def finish():
        at = 0
        for out, copy in zip(outs, copies, strict=True):
            copy.wait()
            wide = out.shape[1]
            out[...] = jnp.dot(att_ref[...], w_buf[:, at:at + wide], preferred_element_type=F32).astype(BF16)
            at += wide

    return start, finish


def project_kernel(steps, att_ref, w_hbm, *refs):
    outs, (w_buf, sem) = refs[:len(steps)], refs[len(steps):]
    h = lax.axis_index("head")
    steps = [(jnp.bitwise_xor(h, flip), at) for flip, at in steps]
    start, finish = project(att_ref, w_hbm, w_buf, sem, outs, steps)
    start()
    finish()


def add_shares(shares):
    total = shares[0][...].astype(F32)
    for share in shares[1:]:
        total = total + share[...].astype(F32)
    return total.astype(BF16)


def take(pos, count, total):
    hit = lax.broadcasted_iota(jnp.int32, (count, total.shape[0]), 0) == pos
    return jnp.dot(jnp.where(hit, 1.0, 0.0).astype(BF16), total, preferred_element_type=F32).astype(BF16)


def pick_kernel(ctx, n_slots, span, mark, pos_ref, *refs):
    slots, shares, outs = refs[:n_slots], refs[n_slots:-ctx], refs[-ctx:]
    moved = take(pos_ref[0:1, :], span * ctx, add_shares(shares))
    for k, out in enumerate(outs):
        out[0:span, :] = moved[k * span:(k + 1) * span]
        if n_slots:
            out[mark:, :] = jnp.zeros((16, out.shape[1]), BF16)
            lanes = slots[k].shape[1]
            out[mark:, 0:lanes] = jnp.concatenate([slots[k][...]] * 2, 0).astype(BF16)


def slot_line(ref, at, span):
    return ref[at:at + 16, 0:span].astype(F32)[0:1].astype(jnp.int32)


def put(slot, block, count):
    hit = lax.broadcasted_iota(jnp.int32, (count, slot.shape[1]), 0) == slot
    return jnp.dot(jnp.where(hit, 1.0, 0.0).astype(BF16), block, preferred_element_type=F32)


def place_kernel(ctx, cap, rows, mark, *refs):
    blocks, marked, (mine_ref, pair_ref) = refs[:ctx], refs[ctx:2 * ctx], refs[2 * ctx:]
    span = 2 * cap
    total = None
    lane = lax.broadcasted_iota(jnp.int32, (1, span), 1)
    for block, marks in zip(blocks, marked, strict=True):
        slot = slot_line(marks, mark, span)
        slot = jnp.where((slot >= 0) & (lane >= cap), slot + rows, slot)
        some = put(slot, block[0:span, :], 2 * rows)
        total = some if total is None else total + some
    mine_ref[...] = total[:rows].astype(BF16)
    pair_ref[...] = total[rows:].astype(BF16)


def join_kernel(n, *refs):
    out = refs[-1]
    at = 0
    for mine, other in zip(refs[:n], refs[n:2 * n], strict=True):
        width = mine.shape[1]
        out[:, at:at + width] = (mine[...].astype(F32) + other[...].astype(F32)).astype(BF16)
        at += width


def after(x, *earlier):
    return lax.optimization_barrier((x, *earlier))[0]


def local(tokens, doc_ids, dest_rows, w_query, w_key, w_value, w_out):
    ctx, rep, n_head = lax.axis_size("ctx"), lax.axis_size("rep"), lax.axis_size("head")
    rows, width = tokens.shape
    kv_cols, q_cols = w_key.shape[1], w_query.shape[1]
    heads = q_cols // HD
    half = w_out.shape[1] // n_head
    others = n_head - 1
    hops = ctx // 2
    cap = 3 * (rows // (2 * ctx * rep))
    span = 2 * cap
    lanes = -(-span // 128) * 128
    every = ctx * span
    sds = jax.ShapeDtypeStruct
    units = half // 128
    chunks = [n * 128 for n in (units * 3 // 8, units - units * 3 // 8)]

    up = [(i, (i + 1) % ctx) for i in range(ctx)]
    swap = [(0, 1), (1, 0)]
    seg_row = doc_ids.reshape(1, rows)

    parts = 4
    payload = sds((rows + 16, 2 * kv_cols), BF16)
    own, table = pl.pallas_call(
        functools.partial(kv_kernel, parts),
        in_specs=[ANY, ANY, ANY, VMEM],
        out_specs=[VMEM] * 2,
        out_shape=[payload, sds((rows, 2 * HD), F32)],
        scratch_shapes=[
            pltpu.VMEM((rows, width), BF16),
            pltpu.VMEM((width, 2 * kv_cols), BF16),
            pltpu.SemaphoreType.DMA((3 * parts,)),
        ],
        compiler_params=params(KV_MIB),
        cost_estimate=cost(4 * rows * width * kv_cols, 2 * width * (rows + 2 * kv_cols)),
        name="keys_values",
    )(tokens, w_key, w_value, seg_row)

    hop = [own, lax.ppermute(own, "ctx", up)]

    parts = 4
    queries = pl.pallas_call(
        functools.partial(q_kernel, parts),
        in_specs=[ANY, ANY, VMEM],
        out_specs=VMEM,
        out_shape=sds((heads, rows, HD), BF16),
        scratch_shapes=[pltpu.VMEM((rows, width), BF16), pltpu.VMEM((width, q_cols), BF16), pltpu.SemaphoreType.DMA((parts + 1,))],
        compiler_params=params(Q_MIB),
        cost_estimate=cost(2 * rows * width * q_cols, 2 * width * (rows + q_cols)),
        name="queries",
    )(tokens, w_query, table)

    route = pl.pallas_call(
        functools.partial(route_kernel, ctx, cap),
        in_specs=[VMEM],
        out_specs=[VMEM] * (1 + ctx),
        out_shape=[sds((8, rows), jnp.int32)] + [sds((8, lanes), F32)] * ctx,
        compiler_params=params(8),
        cost_estimate=cost(4 * rows * rows, 8 * rows * 4),
        name="routes",
    )
    pair = [lax.ppermute(after(own, queries), "rep", swap)]
    hop[1] = after(hop[1], queries)
    buffer_pos, *slots = route(after(dest_rows.reshape(1, rows), hop[1]))
    for i in range(1, hops):
        hop.append(lax.ppermute(hop[i], "ctx", up))
        pair.append(lax.ppermute(after(hop[i], buffer_pos), "rep", swap))

    work = heads * rows * rows
    near = pl.pallas_call(
        functools.partial(near_kernel, hops),
        in_specs=[VMEM] * (2 + 2 * hops),
        out_specs=VMEM,
        out_shape=sds((heads, rows, 2 * HD), F32),
        scratch_shapes=[pltpu.VMEM(payload.shape, BF16)] * (hops - 1) + [pltpu.VMEM((2 * hops - 1, rows, rows), F32)],
        compiler_params=params(12),
        cost_estimate=cost(8 * work * HD * hops, 8 * MIB, 2 * work * hops),
        name="near_attention",
    )(after(seg_row, buffer_pos), queries, *hop[:hops], *pair[:hops])

    hop[hops] = after(hop[hops], near)
    pair.append(lax.ppermute(hop[hops], "rep", swap))

    widths = chunks[:1] * others
    attended, *sent = pl.pallas_call(
        functools.partial(far_kernel, hops, others),
        in_specs=[VMEM] * 6 + [ANY],
        out_specs=[VMEM] * (1 + others),
        out_shape=[sds((rows, heads * HD), BF16)] + [sds((rows, n), BF16) for n in widths],
        scratch_shapes=[pltpu.VMEM(payload.shape, BF16), pltpu.VMEM((2, rows, rows), F32)]
        + [pltpu.VMEM((heads * HD, sum(widths)), BF16), pltpu.SemaphoreType.DMA((others,))],
        compiler_params=params(FAR_MIB),
        cost_estimate=cost(8 * work * HD + 2 * rows * heads * HD * chunks[0], 10 * MIB, 2 * work),
        name="far_attention_project",
    )(seg_row, queries, hop[hops], pair[hops - 1], pair[hops], near, w_out)

    def project_some(x, steps, sizes):
        return pl.pallas_call(
            functools.partial(project_kernel, steps),
            in_specs=[VMEM, ANY],
            out_specs=[VMEM] * len(steps),
            out_shape=[sds((rows, n), BF16) for n in sizes],
            scratch_shapes=[pltpu.VMEM((heads * HD, sum(sizes)), BF16), pltpu.SemaphoreType.DMA((len(steps),))],
            compiler_params=params(PROJECT_MIB),
            cost_estimate=cost(2 * rows * heads * HD * sum(sizes), 2 * heads * HD * sum(sizes)),
            name="project",
        )(x, w_out)

    flips = [[(i, i ^ (d + 1)) for i in range(n_head)] for d in range(others)]

    def to_heads(xs):
        return [lax.ppermute(x, "head", flip) for x, flip in zip(xs, flips, strict=True)]

    theirs = [to_heads(sent)]
    starts = [sum(chunks[:j]) for j in range(len(chunks))]
    later = range(1, len(chunks))
    steps, sizes = [(0, 0)], chunks[:1]
    for j in later:
        steps += [(d + 1, starts[j]) for d in range(others)]
        sizes = sizes + chunks[j:j + 1] * others
    mine, *sent = project_some(attended, steps, sizes)
    for j in later:
        theirs.append(to_heads(sent[(j - 1) * others:j * others]))

    def across(xs):
        return [xs[0]] + [lax.ppermute(xs[k], "ctx", [(i, i ^ k) for i in range(ctx)]) for k in range(1, ctx)]

    mark = -(-span // 16) * 16
    moved, got, shares = [], [], [[mine, *theirs[0]]]
    for j, n in enumerate(chunks):
        extra = slots if j == 0 else []
        tall = mark + 16 if j == 0 else span
        if j == 1:
            ours = project_some(after(attended, *moved), [(0, starts[i]) for i in later], chunks[1:])
            shares += [[x, *theirs[i + 1]] for i, x in enumerate(ours)]
        picked = pl.pallas_call(
            functools.partial(pick_kernel, ctx, len(extra), span, mark),
            in_specs=[VMEM] * (1 + len(extra) + n_head),
            out_specs=[VMEM] * ctx,
            out_shape=[sds((tall, n), BF16)] * ctx,
            compiler_params=params(8),
            cost_estimate=cost(2 * every * rows * n, 2 * n * (2 * rows + every)),
            name="add_pick",
        )(after(buffer_pos, *sent, *moved), *extra, *shares[j])
        moved += picked
        got.append(across(picked))

    kept, gone = [], []
    for j, n in enumerate(chunks):
        stay, leave = pl.pallas_call(
            functools.partial(place_kernel, ctx, cap, rows, mark),
            in_specs=[VMEM] * (2 * ctx),
            out_specs=[VMEM] * 2,
            out_shape=[sds((rows, n), BF16)] * 2,
            compiler_params=params(8),
            cost_estimate=cost(4 * every * rows * n, 2 * n * (2 * rows + every)),
            name="place",
        )(after(got[j][0], *moved, *kept), *got[j][1:], *got[0])
        kept.append(stay)
        gone.append(lax.ppermute(leave, "rep", swap))

    return pl.pallas_call(
        functools.partial(join_kernel, len(chunks)),
        in_specs=[VMEM] * (2 * len(chunks)),
        out_specs=VMEM,
        out_shape=sds((rows, half), BF16),
        compiler_params=params(8),
        cost_estimate=cost(rows * half, 6 * rows * half),
        name="join",
    )(*kept, *gone)


def solution(mesh):
    return jax.shard_map(
        local,
        mesh=mesh,
        in_specs=(
            P(("grp", "ctx", "rep"), None),
            P(("grp", "ctx", "rep")),
            P(("grp", "ctx", "rep")),
            P(None, "head"),
            P(None, "head"),
            P(None, "head"),
            P("head", None),
        ),
        out_specs=P(("grp", "ctx", "rep"), "head"),
        check_vma=False,
    )
```

```python
import functools
import math

import jax
import jax.numpy as jnp
from jax import lax
from jax.experimental import pallas as pl
from jax.experimental.pallas import tpu as pltpu
from jax.sharding import PartitionSpec as P

HD = 128
THETA = 1000000.0
EPSILON = 1e-06
HIDE = -1e30
F32 = jnp.float32
BF16 = jnp.bfloat16
VMEM = pl.BlockSpec(memory_space=pltpu.VMEM)
ANY = pl.BlockSpec(memory_space=pl.ANY)
MIB = 1 << 20
BUSY = 20 * 10**9
KV_MIB = 53
Q_MIB = 52
FAR_MIB = 44
PROJECT_MIB = 48


def params(mib):
    return pltpu.CompilerParams(vmem_limit_bytes=mib * MIB)


def cost(flops, nbytes, trans=0):
    return pl.CostEstimate(flops=int(flops), bytes_accessed=int(nbytes), transcendentals=int(trans))


def column_of(row):
    n = row.shape[1]
    at = lax.broadcasted_iota(jnp.int32, (n, n), 0) == lax.broadcasted_iota(jnp.int32, (n, n), 1)
    return jnp.sum(jnp.where(at, row, 0.0), axis=1, keepdims=True)


def norm_rope(heads, cosine, sine, factor):
    scale = lax.rsqrt(jnp.mean(heads * heads, axis=-1, keepdims=True) + EPSILON)
    if factor != 1.0:
        scale = scale * factor
    turned = pltpu.roll(heads, HD // 2, 1)
    return ((heads * cosine + turned * sine) * scale).astype(BF16)


def kv_kernel(parts, x_hbm, wk_hbm, wv_hbm, seg_ref, kv_ref, tab_ref, x_buf, w_buf, sem):
    rows, width = x_buf.shape
    kv_cols = w_buf.shape[1] // 2
    depth = width // parts
    copies = []
    for i in range(parts):
        at = pl.ds(i * depth, depth)
        copies.append([
            pltpu.make_async_copy(x_hbm.at[:, at], x_buf.at[:, at], sem.at[3 * i]),
            pltpu.make_async_copy(wk_hbm.at[at, :], w_buf.at[at, pl.ds(0, kv_cols)], sem.at[3 * i + 1]),
            pltpu.make_async_copy(wv_hbm.at[at, :], w_buf.at[at, pl.ds(kv_cols, kv_cols)], sem.at[3 * i + 2]),
        ])
        for copy in copies[-1]:
            copy.start()
    first = (lax.axis_index("ctx") * 2 + lax.axis_index("rep")) * rows
    lane = lax.broadcasted_iota(jnp.int32, (1, HD), 1)
    freq = jnp.exp(lax.rem(lane, HD // 2).astype(F32) * (-2.0 * math.log(THETA) / HD))
    pos = (first + lax.broadcasted_iota(jnp.int32, (rows, HD), 0)).astype(F32)
    angle = pos * freq
    tab_ref[:, :HD] = jnp.cos(angle)
    tab_ref[:, HD:] = jnp.where(lane < HD // 2, -1.0, 1.0) * jnp.sin(angle)
    line = lax.broadcasted_iota(jnp.int32, (16, kv_cols), 0)
    segs = jnp.zeros((16, kv_cols), F32)
    for i in range(rows // kv_cols):
        segs = jnp.where(line == i, seg_ref[:, i * kv_cols:(i + 1) * kv_cols].astype(F32), segs)
    kv_ref[rows:, :kv_cols] = segs.astype(BF16)
    kv_ref[rows:, kv_cols:] = jnp.zeros((16, kv_cols), BF16)
    total = None
    for i in range(parts):
        for copy in copies[i]:
            copy.wait()
        at = slice(i * depth, (i + 1) * depth)
        part = jnp.dot(x_buf[:, at], w_buf[at, :], preferred_element_type=F32)
        total = part if total is None else total + part
    for at in range(0, kv_cols, HD):
        kv_ref[0:rows, at:at + HD] = norm_rope(total[:, at:at + HD], tab_ref[:, :HD], tab_ref[:, HD:], 1.0)
    kv_ref[0:rows, kv_cols:] = total[:, kv_cols:].astype(BF16)


def q_kernel(parts, x_hbm, w_hbm, tab_ref, q_ref, x_ref, w_buf, sem):
    heads = q_ref.shape[0]
    wide = w_buf.shape[1] // parts
    factor = math.log2(math.e) / math.sqrt(HD)
    tokens = pltpu.make_async_copy(x_hbm, x_ref, sem.at[parts])
    tokens.start()
    copies = []
    for i in range(parts):
        at = pl.ds(i * wide, wide)
        copies.append(pltpu.make_async_copy(w_hbm.at[:, at], w_buf.at[:, at], sem.at[i]))
        copies[-1].start()

    def finish(i, flat):
        for j in range(wide // HD):
            done = norm_rope(flat[:, j * HD:(j + 1) * HD], tab_ref[:, :HD], tab_ref[:, HD:], factor)
            q_ref[i * (wide // HD) + j] = done

    held = None
    tokens.wait()
    for i in range(parts):
        copies[i].wait()
        flat = jnp.dot(x_ref[...], w_buf[:, i * wide:(i + 1) * wide], preferred_element_type=F32)
        if i:
            finish(i - 1, held)
        held = flat
    finish(parts - 1, held)


def route_kernel(ctx, cap, dest_ref, pos_ref, all_ref, *slot_refs):
    rows = dest_ref.shape[1]
    mine_c, mine_r = lax.axis_index("ctx"), lax.axis_index("rep")
    dest = dest_ref[...]
    owner = lax.div(dest, rows)
    slot = dest - owner * rows
    owner_col = column_of(owner.astype(F32))
    ii = lax.broadcasted_iota(jnp.int32, (rows, rows), 0)
    jj = lax.broadcasted_iota(jnp.int32, (rows, rows), 1)
    before = (owner_col == owner.astype(F32)) & (ii < jj)
    rank = jnp.sum(jnp.where(before, 1.0, 0.0), axis=0, keepdims=True).astype(jnp.int32)
    near_c = jnp.bitwise_xor(lax.div(owner, 2), mine_c)
    near_r = jnp.bitwise_xor(lax.rem(owner, 2), mine_r)
    pos = (near_c * 2 + near_r) * cap + rank
    pos_ref[...] = jnp.broadcast_to(pos, pos_ref.shape)
    pos_col = column_of(pos.astype(F32))
    target_col = column_of(slot.astype(F32)) + 1.0
    lanes = slot_refs[0].shape[1]
    for k in range(ctx):
        lane = lax.broadcasted_iota(jnp.int32, (rows, lanes), 1)
        hit = (pos_col == (lane + k * 2 * cap).astype(F32)) & (lane < 2 * cap)
        got = jnp.sum(jnp.where(hit, target_col, 0.0), axis=0, keepdims=True) - 1.0
        slot_refs[k][...] = jnp.broadcast_to(got, slot_refs[k].shape)
        all_ref[8 * k:8 * k + 8, :] = jnp.broadcast_to(got, slot_refs[k].shape)


def documents(kv_ref):
    wide = kv_ref.shape[1] // 2
    rows = kv_ref.shape[0] // 128 * 128
    lines = kv_ref[rows:rows + 8, :wide].astype(F32)
    return jnp.concatenate([lines[i:i + 1] for i in range(rows // wide)], 1)


def attend(q_ref, blocks, biases, finish):
    heads, rows = q_ref.shape[0], q_ref.shape[1]
    kv_cols = blocks[0].shape[1] // 2
    kv_heads = kv_cols // HD
    groups = heads // kv_heads
    for g in range(kv_heads):
        at = g * HD
        keys = [b[0:rows, at:at + HD] for b in blocks]
        ones = jnp.ones((rows, HD), BF16)
        vals = [jnp.concatenate([b[0:rows, kv_cols + at:kv_cols + at + HD], ones], 1) for b in blocks]
        vals = jnp.concatenate(vals, 0) if len(vals) > 1 else vals[0]

        def head(j, _):
            weights = []
            for key, bias in zip(keys, biases, strict=True):
                s = lax.dot_general(q_ref[j], key, (((1,), (1,)), ((), ())), preferred_element_type=F32)
                weights.append(jnp.exp2(s + bias[...]).astype(BF16))
            p = jnp.concatenate(weights, 1) if len(weights) > 1 else weights[0]
            finish(j, jnp.dot(p, vals, preferred_element_type=F32))
            return 0

        lax.fori_loop(g * groups, (g + 1) * groups, head, 0, unroll=8)


def hide(bias_ref, kv_ref, seg_col):
    bias_ref[...] = jnp.where(documents(kv_ref) == seg_col, 0.0, HIDE)


def choose(to_ref, flag, yes_ref, no_ref):
    @pl.when(flag)
    def _():
        to_ref[...] = yes_ref[0:to_ref.shape[0], :]

    @pl.when(jnp.logical_not(flag))
    def _():
        to_ref[...] = no_ref[0:to_ref.shape[0], :]


def near_kernel(seg_ref, q_ref, *refs):
    n = (len(refs) - 2) // 2
    blocks, out_ref, copies, bias = refs[:n], refs[n], refs[n + 1:-1], refs[-1]
    for copy, block in zip(copies, blocks, strict=True):
        copy[...] = block[0:copy.shape[0], :]
    rows = q_ref.shape[1]
    seg = seg_ref[...].astype(F32)
    seg_col = column_of(seg)
    ii = lax.broadcasted_iota(jnp.int32, (rows, rows), 0)
    jj = lax.broadcasted_iota(jnp.int32, (rows, rows), 1)
    bias[0] = jnp.where((seg == seg_col) & (jj <= ii), 0.0, HIDE)
    back = [2 * i for i in range(len(blocks))]
    accumulate(q_ref, blocks, back, seg_col, jnp.min(seg), bias, out_ref, out_ref, True)


def middle_kernel(seg_ref, q_ref, *refs):
    n = (len(refs) - 4) // 2
    pair, (near_ref, out_ref), (odd, bias) = refs[:n + 1], refs[n + 1:n + 3], (refs[n + 3:-1], refs[-1])
    seg = seg_ref[...].astype(F32)
    r = lax.axis_index("rep")
    for i in range(n):
        choose(odd[i], r == 1, pair[i], pair[i + 1])
    back = [2 * i + 1 for i in range(n)]
    accumulate(q_ref, odd, back, column_of(seg), jnp.min(seg), bias, near_ref, out_ref, False)


def accumulate(q_ref, blocks, back, seg_col, lowest, bias, in_ref, out_ref, fresh):
    me = lax.axis_index("ctx") * 2 + lax.axis_index("rep")
    size = 3
    for start in range(0, len(blocks), size):
        some = blocks[start:start + size]
        seen = []
        for i, block in enumerate(some, start):
            if back[i]:
                hide(bias.at[i], block, seg_col)
                seen.append(((me >= back[i]) & (jnp.max(documents(block)) == lowest)).astype(jnp.int32))
        first = fresh and start == 0
        count = sum(seen) + (1 if first else 0)
        for n in range(1, len(some) + 1):
            @pl.when(count == n)
            def _(n=n, start=start, some=some, first=first):
                def finish(j, new):
                    out_ref[j] = new if first else in_ref[j] + new
                attend(q_ref, some[:n], [bias.at[start + i] for i in range(n)], finish)


def far_kernel(hops, n_other, seg_ref, q_ref, far_ref, to_one, to_zero, near_ref, w_hbm, att_ref, *rest):
    outs, (odd, bias, w_buf, sem) = rest[:n_other], rest[n_other:]
    heads = q_ref.shape[0]
    c, r, h = lax.axis_index("ctx"), lax.axis_index("rep"), lax.axis_index("head")
    start, finish_projection = project(att_ref, w_hbm, w_buf, sem, outs, [(jnp.bitwise_xor(h, d + 1), 0) for d in range(n_other)])
    start()
    seg = seg_ref[...].astype(F32)
    seg_col = column_of(seg)
    lowest = jnp.min(seg)
    choose(odd, r == 1, to_one, to_zero)
    blocks = [odd, far_ref]
    me = c * 2 + r
    seen = []
    for i, d in enumerate((2 * hops - 1, 2 * hops)):
        hide(bias.at[i], blocks[i], seg_col)
        seen.append(((me >= d) & (jnp.max(documents(blocks[i])) == lowest)).astype(jnp.int32))
    count = sum(seen)

    def put(j, both):
        at = j * HD if isinstance(j, int) else pl.multiple_of(j * HD, HD)
        att_ref[:, pl.ds(at, HD)] = (both[:, :HD] / both[:, HD:]).astype(BF16)

    @pl.when(count == 0)
    def _():
        for j in range(heads):
            put(j, near_ref[j])

    for n in (1, 2):
        @pl.when(count == n)
        def _(n=n):
            attend(q_ref, blocks[:n], [bias.at[i] for i in range(n)], lambda j, new: put(j, near_ref[j] + new))

    finish_projection()


def project(att_ref, w_hbm, w_buf, sem, outs, steps):
    half = w_hbm.shape[1] // lax.axis_size("head")
    copies, at = [], 0
    for i, (out, (group, col)) in enumerate(zip(outs, steps, strict=True)):
        wide = out.shape[1]
        from_ = pl.multiple_of(group * half + col, 128)
        copies.append(pltpu.make_async_copy(w_hbm.at[:, pl.ds(from_, wide)], w_buf.at[:, pl.ds(at, wide)], sem.at[i]))
        at += wide

    def start():
        for copy in copies:
            copy.start()

    def finish():
        at = 0
        for out, copy in zip(outs, copies, strict=True):
            copy.wait()
            wide = out.shape[1]
            out[...] = jnp.dot(att_ref[...], w_buf[:, at:at + wide], preferred_element_type=F32).astype(BF16)
            at += wide

    return start, finish


def project_kernel(steps, att_ref, w_hbm, *refs):
    outs, (w_buf, sem) = refs[:len(steps)], refs[len(steps):]
    h = lax.axis_index("head")
    steps = [(jnp.bitwise_xor(h, flip), at) for flip, at in steps]
    start, finish = project(att_ref, w_hbm, w_buf, sem, outs, steps)
    start()
    finish()


def add_shares(shares):
    total = shares[0][...].astype(F32)
    for share in shares[1:]:
        total = total + share[...].astype(F32)
    return total.astype(BF16)


def take(pos, count, total):
    hit = lax.broadcasted_iota(jnp.int32, (count, total.shape[0]), 0) == pos
    return jnp.dot(jnp.where(hit, 1.0, 0.0).astype(BF16), total, preferred_element_type=F32).astype(BF16)


def pick_kernel(ctx, span, mark, pos_ref, pair_slots, *refs):
    slots, shares, outs = refs[:ctx], refs[ctx:-ctx], refs[-ctx:]
    moved = take(pos_ref[0:1, :], span * ctx, add_shares(shares))
    for k, out in enumerate(outs):
        out[0:span, :] = moved[k * span:(k + 1) * span]
        out[mark:, :] = jnp.zeros((16, out.shape[1]), BF16)
        lanes = slots[k].shape[1]
        out[mark:, 0:lanes] = jnp.concatenate([slots[k][...], pair_slots[8 * k:8 * k + 8, :]], 0).astype(BF16)


def split_kernel(cap, pos_ref, *refs):
    shares, (stay_ref, *leave_refs) = refs[:-3], refs[-3:]
    total = add_shares(shares)
    count = stay_ref.shape[0]
    pos = pos_ref[0:1, :]
    line = lax.div(pos, cap)
    at = lax.div(line, 2) * cap + (pos - line * cap)
    same = line - lax.div(line, 2) * 2 == 0
    stay_ref[...] = take(jnp.where(same, at, -1), count, total)
    leave = take(jnp.where(same, -1, at), count, total)
    part = leave_refs[0].shape[0]
    for i, ref in enumerate(leave_refs):
        ref[...] = leave[i * part:(i + 1) * part]


def merge_kernel(cap, stay_ref, *refs):
    came, outs = refs[:2], refs[2:]
    for k, out in enumerate(outs):
        out[0:cap, :] = stay_ref[k * cap:(k + 1) * cap, :]
        came_ref = came[2 * k // len(outs)]
        first = k % (len(outs) // 2) * cap
        out[cap:, :] = came_ref[first:first + cap, :]


def slot_lines(ref, at, span):
    lines = ref[at:at + 16, 0:span].astype(F32).astype(jnp.int32)
    return lines[0:1], lines[8:9]


def put(slot, block, count):
    hit = lax.broadcasted_iota(jnp.int32, (count, slot.shape[1]), 0) == slot
    return jnp.dot(jnp.where(hit, 1.0, 0.0).astype(BF16), block, preferred_element_type=F32)


def place_kernel(ctx, cap, rows, mark, *refs):
    blocks, (mine_ref, pair_ref) = refs[:ctx], refs[ctx:]
    span = 2 * cap
    total = None
    lane = lax.broadcasted_iota(jnp.int32, (1, span), 1)
    for block in blocks:
        slot, _ = slot_lines(block, mark, span)
        slot = jnp.where((slot >= 0) & (lane >= cap), slot + rows, slot)
        some = put(slot, block[0:span, :], 2 * rows)
        total = some if total is None else total + some
    mine_ref[...] = total[:rows].astype(BF16)
    pair_ref[...] = total[rows:].astype(BF16)


def final_kernel(ctx, cap, mark, *refs):
    marks, blocks, out = refs[:ctx], refs[ctx:-1], refs[-1]
    rows = out.shape[0]
    span = 2 * cap
    lane = lax.broadcasted_iota(jnp.int32, (1, span), 1)
    total = None
    for k in range(ctx):
        mine, pair = slot_lines(marks[k], mark, span)
        slot = jnp.where(lane < cap, mine, pair)
        some = put(slot, blocks[k][...], rows)
        total = some if total is None else total + some
    out[...] = total.astype(BF16)


def join_kernel(mine_ref, pair_ref, rest_ref, out):
    rows, at = mine_ref.shape
    out[:, 0:at] = (mine_ref[...].astype(F32) + pair_ref[...].astype(F32)).astype(BF16)
    out[:, at:] = rest_ref[...]


def after(x, *earlier):
    return lax.optimization_barrier((x, *earlier))[0]


def local(tokens, doc_ids, dest_rows, w_query, w_key, w_value, w_out):
    ctx, rep, n_head = lax.axis_size("ctx"), lax.axis_size("rep"), lax.axis_size("head")
    rows, width = tokens.shape
    kv_cols, q_cols = w_key.shape[1], w_query.shape[1]
    heads = q_cols // HD
    half = w_out.shape[1] // n_head
    others = n_head - 1
    hops = ctx // 2
    cap = 3 * (rows // (2 * ctx * rep))
    span = 2 * cap
    lanes = -(-span // 128) * 128
    every = ctx * span
    sds = jax.ShapeDtypeStruct
    chunks = [half // 2] * 2

    up = [(i, (i + 1) % ctx) for i in range(ctx)]
    swap = [(0, 1), (1, 0)]
    seg_row = doc_ids.reshape(1, rows)

    parts = 4
    payload = sds((rows + 16, 2 * kv_cols), BF16)
    own, table = pl.pallas_call(
        functools.partial(kv_kernel, parts),
        in_specs=[ANY, ANY, ANY, VMEM],
        out_specs=[VMEM] * 2,
        out_shape=[payload, sds((rows, 2 * HD), F32)],
        scratch_shapes=[
            pltpu.VMEM((rows, width), BF16),
            pltpu.VMEM((width, 2 * kv_cols), BF16),
            pltpu.SemaphoreType.DMA((3 * parts,)),
        ],
        compiler_params=params(KV_MIB),
        cost_estimate=cost(4 * rows * width * kv_cols, 2 * width * (rows + 2 * kv_cols)),
        name="keys_values",
    )(tokens, w_key, w_value, seg_row)

    hop = [own, lax.ppermute(own, "ctx", up)]

    parts = 4
    queries = pl.pallas_call(
        functools.partial(q_kernel, parts),
        in_specs=[ANY, ANY, VMEM],
        out_specs=VMEM,
        out_shape=sds((heads, rows, HD), BF16),
        scratch_shapes=[pltpu.VMEM((rows, width), BF16), pltpu.VMEM((width, q_cols), BF16), pltpu.SemaphoreType.DMA((parts + 1,))],
        compiler_params=params(Q_MIB),
        cost_estimate=cost(2 * rows * width * q_cols, 2 * width * (rows + q_cols)),
        name="queries",
    )(tokens, w_query, table)

    route = pl.pallas_call(
        functools.partial(route_kernel, ctx, cap),
        in_specs=[VMEM],
        out_specs=[VMEM] * (2 + ctx),
        out_shape=[sds((8, rows), jnp.int32), sds((8 * ctx, lanes), F32)] + [sds((8, lanes), F32)] * ctx,
        compiler_params=params(8),
        cost_estimate=cost(0, 0),
        name="routes",
    )
    hop[1] = after(hop[1], queries)
    for i in range(1, hops):
        hop.append(lax.ppermute(hop[i], "ctx", up))

    work = heads * rows * rows
    short = sds((rows + 8, 2 * kv_cols), BF16)
    near, *short_hop = pl.pallas_call(
        near_kernel,
        in_specs=[VMEM] * (2 + hops),
        out_specs=[VMEM] * (1 + hops),
        out_shape=[sds((heads, rows, 2 * HD), F32)] + [short] * hops,
        scratch_shapes=[pltpu.VMEM((hops, rows, rows), F32)],
        compiler_params=params(12),
        cost_estimate=cost(4 * work * HD * hops, 8 * MIB, work * hops),
        name="even_attention",
    )(seg_row, queries, *hop[:hops])

    buffer_pos, pair_slots, *slots = route(after(dest_rows.reshape(1, rows), near))
    pair_slots = lax.ppermute(pair_slots, "rep", swap)
    pair = [lax.ppermute(x, "rep", swap) for x in short_hop]
    near = pl.pallas_call(
        middle_kernel,
        in_specs=[VMEM] * (3 + hops),
        out_specs=VMEM,
        out_shape=sds((heads, rows, 2 * HD), F32),
        scratch_shapes=[pltpu.VMEM(short.shape, BF16)] * (hops - 1) + [pltpu.VMEM((hops - 1, rows, rows), F32)],
        input_output_aliases={2 + hops: 0},
        compiler_params=params(12),
        cost_estimate=cost(0, 0),
        name="odd_attention",
    )(after(seg_row, pair_slots), queries, *pair, near)
    hop[hops] = after(hop[hops], near)
    pair.append(lax.ppermute(hop[hops], "rep", swap))

    widths = chunks[:1] * others
    attended, *sent = pl.pallas_call(
        functools.partial(far_kernel, hops, others),
        in_specs=[VMEM] * 6 + [ANY],
        out_specs=[VMEM] * (1 + others),
        out_shape=[sds((rows, heads * HD), BF16)] + [sds((rows, n), BF16) for n in widths],
        scratch_shapes=[pltpu.VMEM(short.shape, BF16), pltpu.VMEM((2, rows, rows), F32)]
        + [pltpu.VMEM((heads * HD, sum(widths)), BF16), pltpu.SemaphoreType.DMA((others,))],
        compiler_params=params(FAR_MIB),
        cost_estimate=cost(8 * work * HD + 2 * rows * heads * HD * chunks[0], 10 * MIB, 2 * work),
        name="far_attention_project",
    )(seg_row, queries, hop[hops], pair[hops - 1], pair[hops], near, w_out)

    def project_some(x, steps, sizes):
        return pl.pallas_call(
            functools.partial(project_kernel, steps),
            in_specs=[VMEM, ANY],
            out_specs=[VMEM] * len(steps),
            out_shape=[sds((rows, n), BF16) for n in sizes],
            scratch_shapes=[pltpu.VMEM((heads * HD, sum(sizes)), BF16), pltpu.SemaphoreType.DMA((len(steps),))],
            compiler_params=params(PROJECT_MIB),
            cost_estimate=cost(BUSY, 0),
            name="project",
        )(x, w_out)

    flips = [[(i, i ^ (d + 1)) for i in range(n_head)] for d in range(others)]

    def to_heads(xs):
        return [lax.ppermute(x, "head", flip) for x, flip in zip(xs, flips, strict=True)]

    theirs = [to_heads(sent)]
    starts = [sum(chunks[:j]) for j in range(len(chunks))]
    later = range(1, len(chunks))
    steps, sizes = [(0, 0)], chunks[:1]
    for j in later:
        steps += [(d + 1, starts[j]) for d in range(others)]
        sizes = sizes + chunks[j:j + 1] * others
    mine, *sent = project_some(attended, steps, sizes)
    for j in later:
        theirs.append(to_heads(sent[(j - 1) * others:j * others]))

    def across(xs):
        return [xs[0]] + [lax.ppermute(xs[k], "ctx", [(i, i ^ k) for i in range(ctx)]) for k in range(1, ctx)]

    mark = -(-span // 16) * 16
    n = chunks[0]
    moved = pl.pallas_call(
        functools.partial(pick_kernel, ctx, span, mark),
        in_specs=[VMEM] * (2 + ctx + n_head),
        out_specs=[VMEM] * ctx,
        out_shape=[sds((mark + 16, n), BF16)] * ctx,
        compiler_params=params(8),
        cost_estimate=cost(0, 0),
        name="add_pick",
    )(after(buffer_pos, *sent), pair_slots, *slots, mine, *theirs[0])
    first = across(moved)

    ours = project_some(after(attended, *moved), [(0, starts[j]) for j in later], chunks[1:])
    held, last = [], list(moved)
    for j in later:
        n = chunks[j]
        stay, *leave = pl.pallas_call(
            functools.partial(split_kernel, cap),
            in_specs=[VMEM] * (1 + n_head),
            out_specs=[VMEM] * 3,
            out_shape=[sds((ctx * cap, n), BF16)] + [sds((ctx * cap // 2, n), BF16)] * 2,
            compiler_params=params(8),
            cost_estimate=cost(0, 0),
            name="add_split",
        )(after(buffer_pos, *last), ours[j - 1], *theirs[j])
        leave = [lax.ppermute(x, "rep", swap) for x in leave]
        moved = pl.pallas_call(
            functools.partial(merge_kernel, cap),
            in_specs=[VMEM] * 3,
            out_specs=[VMEM] * ctx,
            out_shape=[sds((span, n), BF16)] * ctx,
            compiler_params=params(8),
            cost_estimate=cost(0, 0),
            name="merge",
        )(stay, *leave)
        held.append(across(moved))
        last = list(moved)

    n = chunks[0]
    stay, leave = pl.pallas_call(
        functools.partial(place_kernel, ctx, cap, rows, mark),
        in_specs=[VMEM] * ctx,
        out_specs=[VMEM] * 2,
        out_shape=[sds((rows, n), BF16)] * 2,
        compiler_params=params(8),
        cost_estimate=cost(BUSY, 0),
        name="place",
    )(after(first[0], *held[0][:1]), *first[1:])
    leave = lax.ppermute(leave, "rep", swap)

    rest = pl.pallas_call(
        functools.partial(final_kernel, ctx, cap, mark),
        in_specs=[VMEM] * (2 * ctx),
        out_specs=VMEM,
        out_shape=sds((rows, chunks[1]), BF16),
        compiler_params=params(8),
        cost_estimate=cost(BUSY, 0),
        name="place_rest",
    )(first[0], *first[1:], *held[0])

    return pl.pallas_call(
        join_kernel,
        in_specs=[VMEM] * 3,
        out_specs=VMEM,
        out_shape=sds((rows, half), BF16),
        compiler_params=params(8),
        cost_estimate=cost(0, 0),
        name="join",
    )(stay, leave, rest)


def solution(mesh):
    return jax.shard_map(
        local,
        mesh=mesh,
        in_specs=(
            P(("grp", "ctx", "rep"), None),
            P(("grp", "ctx", "rep")),
            P(("grp", "ctx", "rep")),
            P(None, "head"),
            P(None, "head"),
            P(None, "head"),
            P("head", None),
        ),
        out_specs=P(("grp", "ctx", "rep"), "head"),
        check_vma=False,
    )
```

```python
import functools
import math

import jax
import jax.numpy as jnp
from jax import lax
from jax.experimental import pallas as pl
from jax.experimental.pallas import tpu as pltpu
from jax.sharding import PartitionSpec as P

HD = 128
THETA = 1000000.0
EPSILON = 1e-06
HIDE = -1e30
F32 = jnp.float32
BF16 = jnp.bfloat16
VMEM = pl.BlockSpec(memory_space=pltpu.VMEM)
ANY = pl.BlockSpec(memory_space=pl.ANY)
MIB = 1 << 20
BUSY = 20 * 10**9
EVEN_COST = 0
KV_MIB = 53
Q_MIB = 52
FAR_MIB = 44
PROJECT_MIB = 48


def params(mib):
    return pltpu.CompilerParams(vmem_limit_bytes=mib * MIB)


def cost(flops, nbytes, trans=0):
    return pl.CostEstimate(flops=int(flops), bytes_accessed=int(nbytes), transcendentals=int(trans))


def column_of(row):
    n = row.shape[1]
    at = lax.broadcasted_iota(jnp.int32, (n, n), 0) == lax.broadcasted_iota(jnp.int32, (n, n), 1)
    return jnp.sum(jnp.where(at, row, 0.0), axis=1, keepdims=True)


def norm_rope(heads, cosine, sine, factor):
    scale = lax.rsqrt(jnp.mean(heads * heads, axis=-1, keepdims=True) + EPSILON)
    if factor != 1.0:
        scale = scale * factor
    turned = pltpu.roll(heads, HD // 2, 1)
    return ((heads * cosine + turned * sine) * scale).astype(BF16)


def kv_kernel(parts, x_hbm, wk_hbm, wv_hbm, seg_ref, kv_ref, tab_ref, x_buf, w_buf, sem):
    rows, width = x_buf.shape
    kv_cols = w_buf.shape[1] // 2
    depth = width // parts
    copies = []
    for i in range(parts):
        at = pl.ds(i * depth, depth)
        copies.append([
            pltpu.make_async_copy(x_hbm.at[:, at], x_buf.at[:, at], sem.at[3 * i]),
            pltpu.make_async_copy(wk_hbm.at[at, :], w_buf.at[at, pl.ds(0, kv_cols)], sem.at[3 * i + 1]),
            pltpu.make_async_copy(wv_hbm.at[at, :], w_buf.at[at, pl.ds(kv_cols, kv_cols)], sem.at[3 * i + 2]),
        ])
        for copy in copies[-1]:
            copy.start()
    first = (lax.axis_index("ctx") * 2 + lax.axis_index("rep")) * rows
    lane = lax.broadcasted_iota(jnp.int32, (1, HD), 1)
    freq = jnp.exp(lax.rem(lane, HD // 2).astype(F32) * (-2.0 * math.log(THETA) / HD))
    pos = (first + lax.broadcasted_iota(jnp.int32, (rows, HD), 0)).astype(F32)
    angle = pos * freq
    tab_ref[:, :HD] = jnp.cos(angle)
    tab_ref[:, HD:] = jnp.where(lane < HD // 2, -1.0, 1.0) * jnp.sin(angle)
    line = lax.broadcasted_iota(jnp.int32, (16, kv_cols), 0)
    segs = jnp.zeros((16, kv_cols), F32)
    for i in range(rows // kv_cols):
        segs = jnp.where(line == i, seg_ref[:, i * kv_cols:(i + 1) * kv_cols].astype(F32), segs)
    kv_ref[rows:, :kv_cols] = segs.astype(BF16)
    kv_ref[rows:, kv_cols:] = jnp.zeros((16, kv_cols), BF16)
    total = None
    for i in range(parts):
        for copy in copies[i]:
            copy.wait()
        at = slice(i * depth, (i + 1) * depth)
        part = jnp.dot(x_buf[:, at], w_buf[at, :], preferred_element_type=F32)
        total = part if total is None else total + part
    for at in range(0, kv_cols, HD):
        kv_ref[0:rows, at:at + HD] = norm_rope(total[:, at:at + HD], tab_ref[:, :HD], tab_ref[:, HD:], 1.0)
    kv_ref[0:rows, kv_cols:] = total[:, kv_cols:].astype(BF16)


def q_kernel(parts, x_hbm, w_hbm, tab_ref, q_ref, x_ref, w_buf, sem):
    heads = q_ref.shape[0]
    wide = w_buf.shape[1] // parts
    factor = math.log2(math.e) / math.sqrt(HD)
    tokens = pltpu.make_async_copy(x_hbm, x_ref, sem.at[parts])
    tokens.start()
    copies = []
    for i in range(parts):
        at = pl.ds(i * wide, wide)
        copies.append(pltpu.make_async_copy(w_hbm.at[:, at], w_buf.at[:, at], sem.at[i]))
        copies[-1].start()

    def finish(i, flat):
        for j in range(wide // HD):
            done = norm_rope(flat[:, j * HD:(j + 1) * HD], tab_ref[:, :HD], tab_ref[:, HD:], factor)
            q_ref[i * (wide // HD) + j] = done

    held = None
    tokens.wait()
    for i in range(parts):
        copies[i].wait()
        flat = jnp.dot(x_ref[...], w_buf[:, i * wide:(i + 1) * wide], preferred_element_type=F32)
        if i:
            finish(i - 1, held)
        held = flat
    finish(parts - 1, held)


def route_kernel(ctx, cap, dest_ref, pos_ref, all_ref, *slot_refs):
    rows = dest_ref.shape[1]
    mine_c, mine_r = lax.axis_index("ctx"), lax.axis_index("rep")
    dest = dest_ref[...]
    owner = lax.div(dest, rows)
    slot = dest - owner * rows
    owner_col = column_of(owner.astype(F32))
    ii = lax.broadcasted_iota(jnp.int32, (rows, rows), 0)
    jj = lax.broadcasted_iota(jnp.int32, (rows, rows), 1)
    before = (owner_col == owner.astype(F32)) & (ii < jj)
    rank = jnp.sum(jnp.where(before, 1.0, 0.0), axis=0, keepdims=True).astype(jnp.int32)
    near_c = jnp.bitwise_xor(lax.div(owner, 2), mine_c)
    near_r = jnp.bitwise_xor(lax.rem(owner, 2), mine_r)
    pos = (near_c * 2 + near_r) * cap + rank
    pos_ref[...] = jnp.broadcast_to(pos, pos_ref.shape)
    pos_col = column_of(pos.astype(F32))
    target_col = column_of(slot.astype(F32)) + 1.0
    lanes = slot_refs[0].shape[1]
    for k in range(ctx):
        lane = lax.broadcasted_iota(jnp.int32, (rows, lanes), 1)
        hit = (pos_col == (lane + k * 2 * cap).astype(F32)) & (lane < 2 * cap)
        got = jnp.sum(jnp.where(hit, target_col, 0.0), axis=0, keepdims=True) - 1.0
        slot_refs[k][...] = jnp.broadcast_to(got, slot_refs[k].shape)
        all_ref[8 * k:8 * k + 8, :] = jnp.broadcast_to(got, slot_refs[k].shape)


def documents(kv_ref):
    wide = kv_ref.shape[1] // 2
    rows = kv_ref.shape[0] // 128 * 128
    lines = kv_ref[rows:rows + 8, :wide].astype(F32)
    return jnp.concatenate([lines[i:i + 1] for i in range(rows // wide)], 1)


def attend(q_ref, blocks, biases, finish):
    heads, rows = q_ref.shape[0], q_ref.shape[1]
    kv_cols = blocks[0].shape[1] // 2
    kv_heads = kv_cols // HD
    groups = heads // kv_heads
    for g in range(kv_heads):
        at = g * HD
        keys = [b[0:rows, at:at + HD] for b in blocks]
        ones = jnp.ones((rows, HD), BF16)
        vals = [jnp.concatenate([b[0:rows, kv_cols + at:kv_cols + at + HD], ones], 1) for b in blocks]
        vals = jnp.concatenate(vals, 0) if len(vals) > 1 else vals[0]

        def head(j, _):
            weights = []
            for key, bias in zip(keys, biases, strict=True):
                s = lax.dot_general(q_ref[j], key, (((1,), (1,)), ((), ())), preferred_element_type=F32)
                weights.append(jnp.exp2(s + bias[...]).astype(BF16))
            p = jnp.concatenate(weights, 1) if len(weights) > 1 else weights[0]
            finish(j, jnp.dot(p, vals, preferred_element_type=F32))
            return 0

        lax.fori_loop(g * groups, (g + 1) * groups, head, 0, unroll=8)


def hide(bias_ref, kv_ref, seg_col):
    bias_ref[...] = jnp.where(documents(kv_ref) == seg_col, 0.0, HIDE)


def choose(to_ref, flag, yes_ref, no_ref):
    @pl.when(flag)
    def _():
        to_ref[...] = yes_ref[0:to_ref.shape[0], :]

    @pl.when(jnp.logical_not(flag))
    def _():
        to_ref[...] = no_ref[0:to_ref.shape[0], :]


def near_kernel(seg_ref, q_ref, *refs):
    blocks, out_ref, bias = refs[:-2], refs[-2], refs[-1]
    rows = q_ref.shape[1]
    seg = seg_ref[...].astype(F32)
    seg_col = column_of(seg)
    ii = lax.broadcasted_iota(jnp.int32, (rows, rows), 0)
    jj = lax.broadcasted_iota(jnp.int32, (rows, rows), 1)
    bias[0] = jnp.where((seg == seg_col) & (jj <= ii), 0.0, HIDE)
    back = [2 * i for i in range(len(blocks))]
    accumulate(q_ref, blocks, back, seg_col, jnp.min(seg), bias, out_ref, out_ref, True)


def shorten_kernel(*refs):
    n = len(refs) // 2
    for short, block in zip(refs[n:], refs[:n], strict=True):
        short[...] = block[0:short.shape[0], :]


def middle_kernel(seg_ref, q_ref, *refs):
    n = (len(refs) - 4) // 2
    pair, (near_ref, out_ref), (odd, bias) = refs[:n + 1], refs[n + 1:n + 3], (refs[n + 3:-1], refs[-1])
    seg = seg_ref[...].astype(F32)
    r = lax.axis_index("rep")
    for i in range(n):
        choose(odd[i], r == 1, pair[i], pair[i + 1])
    back = [2 * i + 1 for i in range(n)]
    accumulate(q_ref, odd, back, column_of(seg), jnp.min(seg), bias, near_ref, out_ref, False)


def accumulate(q_ref, blocks, back, seg_col, lowest, bias, in_ref, out_ref, fresh):
    me = lax.axis_index("ctx") * 2 + lax.axis_index("rep")
    size = 3
    for start in range(0, len(blocks), size):
        some = blocks[start:start + size]
        seen = []
        for i, block in enumerate(some, start):
            if back[i]:
                hide(bias.at[i], block, seg_col)
                seen.append(((me >= back[i]) & (jnp.max(documents(block)) == lowest)).astype(jnp.int32))
        first = fresh and start == 0
        count = sum(seen) + (1 if first else 0)
        for n in range(1, len(some) + 1):
            @pl.when(count == n)
            def _(n=n, start=start, some=some, first=first):
                def finish(j, new):
                    out_ref[j] = new if first else in_ref[j] + new
                attend(q_ref, some[:n], [bias.at[start + i] for i in range(n)], finish)


def far_kernel(hops, n_other, seg_ref, q_ref, far_ref, to_one, to_zero, near_ref, w_hbm, att_ref, *rest):
    outs, (odd, bias, w_buf, sem) = rest[:n_other], rest[n_other:]
    heads = q_ref.shape[0]
    c, r, h = lax.axis_index("ctx"), lax.axis_index("rep"), lax.axis_index("head")
    start, finish_projection = project(att_ref, w_hbm, w_buf, sem, outs, [(jnp.bitwise_xor(h, d + 1), 0) for d in range(n_other)])
    start()
    seg = seg_ref[...].astype(F32)
    seg_col = column_of(seg)
    lowest = jnp.min(seg)
    choose(odd, r == 1, to_one, to_zero)
    blocks = [odd, far_ref]
    me = c * 2 + r
    seen = []
    for i, d in enumerate((2 * hops - 1, 2 * hops)):
        hide(bias.at[i], blocks[i], seg_col)
        seen.append(((me >= d) & (jnp.max(documents(blocks[i])) == lowest)).astype(jnp.int32))
    count = sum(seen)

    def put(j, both):
        at = j * HD if isinstance(j, int) else pl.multiple_of(j * HD, HD)
        att_ref[:, pl.ds(at, HD)] = (both[:, :HD] / both[:, HD:]).astype(BF16)

    @pl.when(count == 0)
    def _():
        for j in range(heads):
            put(j, near_ref[j])

    for n in (1, 2):
        @pl.when(count == n)
        def _(n=n):
            attend(q_ref, blocks[:n], [bias.at[i] for i in range(n)], lambda j, new: put(j, near_ref[j] + new))

    finish_projection()


def project(att_ref, w_hbm, w_buf, sem, outs, steps):
    half = w_hbm.shape[1] // lax.axis_size("head")
    copies, at = [], 0
    for i, (out, (group, col)) in enumerate(zip(outs, steps, strict=True)):
        wide = out.shape[1]
        from_ = pl.multiple_of(group * half + col, 128)
        copies.append(pltpu.make_async_copy(w_hbm.at[:, pl.ds(from_, wide)], w_buf.at[:, pl.ds(at, wide)], sem.at[i]))
        at += wide

    def start():
        for copy in copies:
            copy.start()

    def finish():
        at = 0
        for out, copy in zip(outs, copies, strict=True):
            copy.wait()
            wide = out.shape[1]
            out[...] = jnp.dot(att_ref[...], w_buf[:, at:at + wide], preferred_element_type=F32).astype(BF16)
            at += wide

    return start, finish


def project_kernel(steps, att_ref, w_hbm, *refs):
    outs, (w_buf, sem) = refs[:len(steps)], refs[len(steps):]
    h = lax.axis_index("head")
    steps = [(jnp.bitwise_xor(h, flip), at) for flip, at in steps]
    start, finish = project(att_ref, w_hbm, w_buf, sem, outs, steps)
    start()
    finish()


def add_shares(shares):
    total = shares[0][...].astype(F32)
    for share in shares[1:]:
        total = total + share[...].astype(F32)
    return total.astype(BF16)


def take(pos, count, total):
    hit = lax.broadcasted_iota(jnp.int32, (count, total.shape[0]), 0) == pos
    return jnp.dot(jnp.where(hit, 1.0, 0.0).astype(BF16), total, preferred_element_type=F32).astype(BF16)


def pick_kernel(ctx, span, mark, pos_ref, pair_slots, *refs):
    slots, shares, outs = refs[:ctx], refs[ctx:-ctx], refs[-ctx:]
    moved = take(pos_ref[0:1, :], span * ctx, add_shares(shares))
    for k, out in enumerate(outs):
        out[0:span, :] = moved[k * span:(k + 1) * span]
        out[mark:, :] = jnp.zeros((8, out.shape[1]), BF16)
        lanes = slots[k].shape[1]
        top = lax.broadcasted_iota(jnp.int32, (8, lanes), 0) < 4
        out[mark:, 0:lanes] = jnp.where(top, slots[k][...], pair_slots[8 * k:8 * k + 8, :]).astype(BF16)


def split_kernel(cap, pos_ref, *refs):
    shares, (stay_ref, *leave_refs) = refs[:-3], refs[-3:]
    total = add_shares(shares)
    count = stay_ref.shape[0]
    pos = pos_ref[0:1, :]
    line = lax.div(pos, cap)
    at = lax.div(line, 2) * cap + (pos - line * cap)
    same = line - lax.div(line, 2) * 2 == 0
    stay_ref[...] = take(jnp.where(same, at, -1), count, total)
    leave = take(jnp.where(same, -1, at), count, total)
    part = leave_refs[0].shape[0]
    for i, ref in enumerate(leave_refs):
        ref[...] = leave[i * part:(i + 1) * part]


def merge_kernel(cap, stay_ref, *refs):
    came, outs = refs[:2], refs[2:]
    for k, out in enumerate(outs):
        out[0:cap, :] = stay_ref[k * cap:(k + 1) * cap, :]
        came_ref = came[2 * k // len(outs)]
        first = k % (len(outs) // 2) * cap
        out[cap:, :] = came_ref[first:first + cap, :]


def slot_lines(ref, at, span):
    lines = ref[at:at + 8, 0:span].astype(F32).astype(jnp.int32)
    return lines[0:1], lines[4:5]


def put(slot, block, count):
    hit = lax.broadcasted_iota(jnp.int32, (count, slot.shape[1]), 0) == slot
    return jnp.dot(jnp.where(hit, 1.0, 0.0).astype(BF16), block, preferred_element_type=F32)


def place_kernel(ctx, cap, rows, mark, *refs):
    blocks, (mine_ref, pair_ref) = refs[:ctx], refs[ctx:]
    span = 2 * cap
    total = None
    lane = lax.broadcasted_iota(jnp.int32, (1, span), 1)
    for block in blocks:
        slot, _ = slot_lines(block, mark, span)
        slot = jnp.where((slot >= 0) & (lane >= cap), slot + rows, slot)
        some = put(slot, block[0:span, :], 2 * rows)
        total = some if total is None else total + some
    mine_ref[...] = total[:rows].astype(BF16)
    pair_ref[...] = total[rows:].astype(BF16)


def final_kernel(ctx, cap, mark, *refs):
    marks, blocks, out = refs[:ctx], refs[ctx:-1], refs[-1]
    rows = out.shape[0]
    span = 2 * cap
    lane = lax.broadcasted_iota(jnp.int32, (1, span), 1)
    total = None
    for k in range(ctx):
        mine, pair = slot_lines(marks[k], mark, span)
        slot = jnp.where(lane < cap, mine, pair)
        some = put(slot, blocks[k][...], rows)
        total = some if total is None else total + some
    out[...] = total.astype(BF16)


def join_kernel(mine_ref, pair_ref, rest_ref, out):
    rows, at = mine_ref.shape
    out[:, 0:at] = (mine_ref[...].astype(F32) + pair_ref[...].astype(F32)).astype(BF16)
    out[:, at:] = rest_ref[...]


def after(x, *earlier):
    return lax.optimization_barrier((x, *earlier))[0]


def local(tokens, doc_ids, dest_rows, w_query, w_key, w_value, w_out):
    ctx, rep, n_head = lax.axis_size("ctx"), lax.axis_size("rep"), lax.axis_size("head")
    rows, width = tokens.shape
    kv_cols, q_cols = w_key.shape[1], w_query.shape[1]
    heads = q_cols // HD
    half = w_out.shape[1] // n_head
    others = n_head - 1
    hops = ctx // 2
    cap = 3 * (rows // (2 * ctx * rep))
    span = 2 * cap
    lanes = -(-span // 128) * 128
    every = ctx * span
    sds = jax.ShapeDtypeStruct
    chunks = [half // 2] * 2

    up = [(i, (i + 1) % ctx) for i in range(ctx)]
    swap = [(0, 1), (1, 0)]
    seg_row = doc_ids.reshape(1, rows)

    parts = 4
    payload = sds((rows + 16, 2 * kv_cols), BF16)
    own, table = pl.pallas_call(
        functools.partial(kv_kernel, parts),
        in_specs=[ANY, ANY, ANY, VMEM],
        out_specs=[VMEM] * 2,
        out_shape=[payload, sds((rows, 2 * HD), F32)],
        scratch_shapes=[
            pltpu.VMEM((rows, width), BF16),
            pltpu.VMEM((width, 2 * kv_cols), BF16),
            pltpu.SemaphoreType.DMA((3 * parts,)),
        ],
        compiler_params=params(KV_MIB),
        cost_estimate=cost(4 * rows * width * kv_cols, 2 * width * (rows + 2 * kv_cols)),
        name="keys_values",
    )(tokens, w_key, w_value, seg_row)

    hop = [own, lax.ppermute(own, "ctx", up)]

    parts = 4
    queries = pl.pallas_call(
        functools.partial(q_kernel, parts),
        in_specs=[ANY, ANY, VMEM],
        out_specs=VMEM,
        out_shape=sds((heads, rows, HD), BF16),
        scratch_shapes=[pltpu.VMEM((rows, width), BF16), pltpu.VMEM((width, q_cols), BF16), pltpu.SemaphoreType.DMA((parts + 1,))],
        compiler_params=params(Q_MIB),
        cost_estimate=cost(2 * rows * width * q_cols, 2 * width * (rows + q_cols)),
        name="queries",
    )(tokens, w_query, table)

    route = pl.pallas_call(
        functools.partial(route_kernel, ctx, cap),
        in_specs=[VMEM],
        out_specs=[VMEM] * (2 + ctx),
        out_shape=[sds((8, rows), jnp.int32), sds((8 * ctx, lanes), F32)] + [sds((8, lanes), F32)] * ctx,
        compiler_params=params(8),
        cost_estimate=cost(0, 0),
        name="routes",
    )
    hop[1] = after(hop[1], queries)
    for i in range(1, hops):
        hop.append(lax.ppermute(hop[i], "ctx", [(j, j + 1) for j in range(i, ctx - 1)]))

    short = sds((rows + 8, 2 * kv_cols), BF16)
    short_hop = pl.pallas_call(
        shorten_kernel,
        in_specs=[VMEM] * hops,
        out_specs=[VMEM] * hops,
        out_shape=[short] * hops,
        compiler_params=params(8),
        cost_estimate=cost(0, 0),
        name="shorten",
    )(*hop[:hops])
    pair = [lax.ppermute(x, "rep", swap) for x in short_hop]

    work = heads * rows * rows
    near = pl.pallas_call(
        near_kernel,
        in_specs=[VMEM] * (2 + hops),
        out_specs=VMEM,
        out_shape=sds((heads, rows, 2 * HD), F32),
        scratch_shapes=[pltpu.VMEM((hops, rows, rows), F32)],
        compiler_params=params(12),
        cost_estimate=cost(EVEN_COST, 0),
        name="even_attention",
    )(after(seg_row, *short_hop), queries, *hop[:hops])

    buffer_pos, pair_slots, *slots = route(after(dest_rows.reshape(1, rows), near))
    pair_slots = lax.ppermute(pair_slots, "rep", swap)
    pair = [lax.ppermute(x, "rep", swap) for x in short_hop]
    near = pl.pallas_call(
        middle_kernel,
        in_specs=[VMEM] * (3 + hops),
        out_specs=VMEM,
        out_shape=sds((heads, rows, 2 * HD), F32),
        scratch_shapes=[pltpu.VMEM(short.shape, BF16)] * (hops - 1) + [pltpu.VMEM((hops - 1, rows, rows), F32)],
        input_output_aliases={2 + hops: 0},
        compiler_params=params(12),
        cost_estimate=cost(0, 0),
        name="odd_attention",
    )(after(seg_row, buffer_pos), queries, *pair, near)
    hop[hops] = after(hop[hops], near)
    pair.append(lax.ppermute(hop[hops], "rep", swap))

    widths = chunks[:1] * others
    attended, *sent = pl.pallas_call(
        functools.partial(far_kernel, hops, others),
        in_specs=[VMEM] * 6 + [ANY],
        out_specs=[VMEM] * (1 + others),
        out_shape=[sds((rows, heads * HD), BF16)] + [sds((rows, n), BF16) for n in widths],
        scratch_shapes=[pltpu.VMEM(short.shape, BF16), pltpu.VMEM((2, rows, rows), F32)]
        + [pltpu.VMEM((heads * HD, sum(widths)), BF16), pltpu.SemaphoreType.DMA((others,))],
        compiler_params=params(FAR_MIB),
        cost_estimate=cost(8 * work * HD + 2 * rows * heads * HD * chunks[0], 10 * MIB, 2 * work),
        name="far_attention_project",
    )(after(seg_row, pair_slots), queries, hop[hops], pair[hops - 1], pair[hops], near, w_out)

    def project_some(x, steps, sizes):
        return pl.pallas_call(
            functools.partial(project_kernel, steps),
            in_specs=[VMEM, ANY],
            out_specs=[VMEM] * len(steps),
            out_shape=[sds((rows, n), BF16) for n in sizes],
            scratch_shapes=[pltpu.VMEM((heads * HD, sum(sizes)), BF16), pltpu.SemaphoreType.DMA((len(steps),))],
            compiler_params=params(PROJECT_MIB),
            cost_estimate=cost(BUSY, 0),
            name="project",
        )(x, w_out)

    flips = [[(i, i ^ (d + 1)) for i in range(n_head)] for d in range(others)]

    def to_heads(xs):
        return [lax.ppermute(x, "head", flip) for x, flip in zip(xs, flips, strict=True)]

    theirs = [to_heads(sent)]
    starts = [sum(chunks[:j]) for j in range(len(chunks))]
    later = range(1, len(chunks))
    steps, sizes = [(0, 0)], chunks[:1]
    for j in later:
        steps += [(d + 1, starts[j]) for d in range(others)]
        sizes = sizes + chunks[j:j + 1] * others
    mine, *sent = project_some(attended, steps, sizes)
    for j in later:
        theirs.append(to_heads(sent[(j - 1) * others:j * others]))

    def across(xs):
        return [xs[0]] + [lax.ppermute(xs[k], "ctx", [(i, i ^ k) for i in range(ctx)]) for k in range(1, ctx)]

    mark = -(-span // 16) * 16
    n = chunks[0]
    moved = pl.pallas_call(
        functools.partial(pick_kernel, ctx, span, mark),
        in_specs=[VMEM] * (2 + ctx + n_head),
        out_specs=[VMEM] * ctx,
        out_shape=[sds((mark + 8, n), BF16)] * ctx,
        compiler_params=params(8),
        cost_estimate=cost(0, 0),
        name="add_pick",
    )(after(buffer_pos, *sent), pair_slots, *slots, mine, *theirs[0])
    first = across(moved)

    ours = project_some(after(attended, *moved), [(0, starts[j]) for j in later], chunks[1:])
    held, last = [], list(moved)
    for j in later:
        n = chunks[j]
        stay, *leave = pl.pallas_call(
            functools.partial(split_kernel, cap),
            in_specs=[VMEM] * (1 + n_head),
            out_specs=[VMEM] * 3,
            out_shape=[sds((ctx * cap, n), BF16)] + [sds((ctx * cap // 2, n), BF16)] * 2,
            compiler_params=params(8),
            cost_estimate=cost(0, 0),
            name="add_split",
        )(after(buffer_pos, *last), ours[j - 1], *theirs[j])
        leave = [lax.ppermute(x, "rep", swap) for x in leave]
        moved = pl.pallas_call(
            functools.partial(merge_kernel, cap),
            in_specs=[VMEM] * 3,
            out_specs=[VMEM] * ctx,
            out_shape=[sds((span, n), BF16)] * ctx,
            compiler_params=params(8),
            cost_estimate=cost(0, 0),
            name="merge",
        )(stay, *leave)
        held.append(across(moved))
        last = list(moved)

    n = chunks[0]
    stay, leave = pl.pallas_call(
        functools.partial(place_kernel, ctx, cap, rows, mark),
        in_specs=[VMEM] * ctx,
        out_specs=[VMEM] * 2,
        out_shape=[sds((rows, n), BF16)] * 2,
        compiler_params=params(8),
        cost_estimate=cost(BUSY, 0),
        name="place",
    )(after(first[0], *held[0][:1]), *first[1:])
    leave = lax.ppermute(leave, "rep", swap)

    rest = pl.pallas_call(
        functools.partial(final_kernel, ctx, cap, mark),
        in_specs=[VMEM] * (2 * ctx),
        out_specs=VMEM,
        out_shape=sds((rows, chunks[1]), BF16),
        compiler_params=params(8),
        cost_estimate=cost(BUSY, 0),
        name="place_rest",
    )(first[0], *first[1:], *held[0])

    return pl.pallas_call(
        join_kernel,
        in_specs=[VMEM] * 3,
        out_specs=VMEM,
        out_shape=sds((rows, half), BF16),
        compiler_params=params(8),
        cost_estimate=cost(0, 0),
        name="join",
    )(stay, leave, rest)


def solution(mesh):
    return jax.shard_map(
        local,
        mesh=mesh,
        in_specs=(
            P(("grp", "ctx", "rep"), None),
            P(("grp", "ctx", "rep")),
            P(("grp", "ctx", "rep")),
            P(None, "head"),
            P(None, "head"),
            P(None, "head"),
            P("head", None),
        ),
        out_specs=P(("grp", "ctx", "rep"), "head"),
        check_vma=False,
    )
```

```python
import functools
import math

import jax
import jax.numpy as jnp
from jax import lax
from jax.experimental import pallas as pl
from jax.experimental.pallas import tpu as pltpu
from jax.sharding import PartitionSpec as P

HD = 128
THETA = 1000000.0
EPSILON = 1e-06
HIDE = -1e30
F32 = jnp.float32
BF16 = jnp.bfloat16
VMEM = pl.BlockSpec(memory_space=pltpu.VMEM)
ANY = pl.BlockSpec(memory_space=pl.ANY)
MIB = 1 << 20
BUSY = 20 * 10**9
EVEN_COST = 0
KV_MIB = 53
Q_MIB = 52
FAR_MIB = 44
PROJECT_MIB = 48


def params(mib):
    return pltpu.CompilerParams(vmem_limit_bytes=mib * MIB)


def cost(flops, nbytes, trans=0):
    return pl.CostEstimate(flops=int(flops), bytes_accessed=int(nbytes), transcendentals=int(trans))


def column_of(row):
    n = row.shape[1]
    at = lax.broadcasted_iota(jnp.int32, (n, n), 0) == lax.broadcasted_iota(jnp.int32, (n, n), 1)
    return jnp.sum(jnp.where(at, row, 0.0), axis=1, keepdims=True)


def norm_rope(heads, cosine, sine, factor):
    scale = lax.rsqrt(jnp.mean(heads * heads, axis=-1, keepdims=True) + EPSILON)
    if factor != 1.0:
        scale = scale * factor
    turned = pltpu.roll(heads, HD // 2, 1)
    return ((heads * cosine + turned * sine) * scale).astype(BF16)


def kv_kernel(parts, x_hbm, wk_hbm, wv_hbm, seg_hbm, kv_ref, tab_ref, x_buf, w_buf, seg_ref, sem):
    rows, width = x_buf.shape
    kv_cols = w_buf.shape[1] // 2
    depth = width // parts
    copies = []
    for i in range(parts):
        at = pl.ds(i * depth, depth)
        copies.append([
            pltpu.make_async_copy(x_hbm.at[:, at], x_buf.at[:, at], sem.at[3 * i]),
            pltpu.make_async_copy(wk_hbm.at[at, :], w_buf.at[at, pl.ds(0, kv_cols)], sem.at[3 * i + 1]),
            pltpu.make_async_copy(wv_hbm.at[at, :], w_buf.at[at, pl.ds(kv_cols, kv_cols)], sem.at[3 * i + 2]),
        ])
        for copy in copies[-1]:
            copy.start()
    docs = pltpu.make_async_copy(seg_hbm, seg_ref, sem.at[3 * parts])
    docs.start()
    first = (lax.axis_index("ctx") * 2 + lax.axis_index("rep")) * rows
    lane = lax.broadcasted_iota(jnp.int32, (1, HD), 1)
    freq = jnp.exp(lax.rem(lane, HD // 2).astype(F32) * (-2.0 * math.log(THETA) / HD))
    pos = (first + lax.broadcasted_iota(jnp.int32, (rows, HD), 0)).astype(F32)
    angle = pos * freq
    tab_ref[:, :HD] = jnp.cos(angle)
    tab_ref[:, HD:] = jnp.where(lane < HD // 2, -1.0, 1.0) * jnp.sin(angle)
    docs.wait()
    line = lax.broadcasted_iota(jnp.int32, (16, kv_cols), 0)
    segs = jnp.zeros((16, kv_cols), F32)
    for i in range(rows // kv_cols):
        segs = jnp.where(line == i, seg_ref[:, i * kv_cols:(i + 1) * kv_cols].astype(F32), segs)
    kv_ref[rows:, :kv_cols] = segs.astype(BF16)
    kv_ref[rows:, kv_cols:] = jnp.zeros((16, kv_cols), BF16)
    total = None
    for i in range(parts):
        for copy in copies[i]:
            copy.wait()
        at = slice(i * depth, (i + 1) * depth)
        part = jnp.dot(x_buf[:, at], w_buf[at, :], preferred_element_type=F32)
        total = part if total is None else total + part
    for at in range(0, kv_cols, HD):
        kv_ref[0:rows, at:at + HD] = norm_rope(total[:, at:at + HD], tab_ref[:, :HD], tab_ref[:, HD:], 1.0)
    kv_ref[0:rows, kv_cols:] = total[:, kv_cols:].astype(BF16)


def q_kernel(parts, x_hbm, w_hbm, tab_ref, q_ref, x_ref, w_buf, sem):
    heads = q_ref.shape[0]
    wide = w_buf.shape[1] // parts
    factor = math.log2(math.e) / math.sqrt(HD)
    tokens = pltpu.make_async_copy(x_hbm, x_ref, sem.at[parts])
    tokens.start()
    copies = []
    for i in range(parts):
        at = pl.ds(i * wide, wide)
        copies.append(pltpu.make_async_copy(w_hbm.at[:, at], w_buf.at[:, at], sem.at[i]))
        copies[-1].start()

    def finish(i, flat):
        for j in range(wide // HD):
            done = norm_rope(flat[:, j * HD:(j + 1) * HD], tab_ref[:, :HD], tab_ref[:, HD:], factor)
            q_ref[i * (wide // HD) + j] = done

    held = None
    tokens.wait()
    for i in range(parts):
        copies[i].wait()
        flat = jnp.dot(x_ref[...], w_buf[:, i * wide:(i + 1) * wide], preferred_element_type=F32)
        if i:
            finish(i - 1, held)
        held = flat
    finish(parts - 1, held)


def route_kernel(ctx, cap, dest_ref, pos_ref, all_ref, *slot_refs):
    rows = dest_ref.shape[1]
    mine_c, mine_r = lax.axis_index("ctx"), lax.axis_index("rep")
    dest = dest_ref[...]
    owner = lax.div(dest, rows)
    slot = dest - owner * rows
    owner_col = column_of(owner.astype(F32))
    ii = lax.broadcasted_iota(jnp.int32, (rows, rows), 0)
    jj = lax.broadcasted_iota(jnp.int32, (rows, rows), 1)
    before = (owner_col == owner.astype(F32)) & (ii < jj)
    rank = jnp.sum(jnp.where(before, 1.0, 0.0), axis=0, keepdims=True).astype(jnp.int32)
    near_c = jnp.bitwise_xor(lax.div(owner, 2), mine_c)
    near_r = jnp.bitwise_xor(lax.rem(owner, 2), mine_r)
    pos = (near_c * 2 + near_r) * cap + rank
    pos_ref[...] = jnp.broadcast_to(pos, pos_ref.shape)
    pos_col = column_of(pos.astype(F32))
    target_col = column_of(slot.astype(F32)) + 1.0
    lanes = slot_refs[0].shape[1]
    for k in range(ctx):
        lane = lax.broadcasted_iota(jnp.int32, (rows, lanes), 1)
        hit = (pos_col == (lane + k * 2 * cap).astype(F32)) & (lane < 2 * cap)
        got = jnp.sum(jnp.where(hit, target_col, 0.0), axis=0, keepdims=True) - 1.0
        slot_refs[k][...] = jnp.broadcast_to(got, slot_refs[k].shape)
        all_ref[8 * k:8 * k + 8, :] = jnp.broadcast_to(got, slot_refs[k].shape)


def documents(kv_ref):
    wide = kv_ref.shape[1] // 2
    rows = kv_ref.shape[0] // 128 * 128
    lines = kv_ref[rows:rows + 8, :wide].astype(F32)
    return jnp.concatenate([lines[i:i + 1] for i in range(rows // wide)], 1)


def attend(q_ref, blocks, biases, finish):
    heads, rows = q_ref.shape[0], q_ref.shape[1]
    kv_cols = blocks[0].shape[1] // 2
    kv_heads = kv_cols // HD
    groups = heads // kv_heads
    for g in range(kv_heads):
        at = g * HD
        keys = [b[0:rows, at:at + HD] for b in blocks]
        ones = jnp.ones((rows, HD), BF16)
        vals = [jnp.concatenate([b[0:rows, kv_cols + at:kv_cols + at + HD], ones], 1) for b in blocks]
        vals = jnp.concatenate(vals, 0) if len(vals) > 1 else vals[0]

        def head(j, _):
            weights = []
            for key, bias in zip(keys, biases, strict=True):
                s = lax.dot_general(q_ref[j], key, (((1,), (1,)), ((), ())), preferred_element_type=F32)
                weights.append(jnp.exp2(s + bias[...]).astype(BF16))
            p = jnp.concatenate(weights, 1) if len(weights) > 1 else weights[0]
            finish(j, jnp.dot(p, vals, preferred_element_type=F32))
            return 0

        lax.fori_loop(g * groups, (g + 1) * groups, head, 0, unroll=8)


def hide(bias_ref, kv_ref, seg_col):
    bias_ref[...] = jnp.where(documents(kv_ref) == seg_col, 0.0, HIDE)


def choose(to_ref, flag, yes_ref, no_ref):
    @pl.when(flag)
    def _():
        to_ref[...] = yes_ref[0:to_ref.shape[0], :]

    @pl.when(jnp.logical_not(flag))
    def _():
        to_ref[...] = no_ref[0:to_ref.shape[0], :]


def near_kernel(seg_ref, q_ref, *refs):
    blocks, out_ref, bias = refs[:-2], refs[-2], refs[-1]
    rows = q_ref.shape[1]
    seg = seg_ref[...].astype(F32)
    seg_col = column_of(seg)
    ii = lax.broadcasted_iota(jnp.int32, (rows, rows), 0)
    jj = lax.broadcasted_iota(jnp.int32, (rows, rows), 1)
    bias[0] = jnp.where((seg == seg_col) & (jj <= ii), 0.0, HIDE)
    back = [2 * i for i in range(len(blocks))]
    accumulate(q_ref, blocks, back, seg_col, jnp.min(seg), bias, out_ref, out_ref, True)


def shorten_kernel(*refs):
    n = len(refs) // 2
    for short, block in zip(refs[n:], refs[:n], strict=True):
        short[...] = block[0:short.shape[0], :]


def middle_kernel(seg_ref, q_ref, *refs):
    n = (len(refs) - 4) // 2
    pair, (near_ref, out_ref), (odd, bias) = refs[:n + 1], refs[n + 1:n + 3], (refs[n + 3:-1], refs[-1])
    seg = seg_ref[...].astype(F32)
    r = lax.axis_index("rep")
    for i in range(n):
        choose(odd[i], r == 1, pair[i], pair[i + 1])
    back = [2 * i + 1 for i in range(n)]
    accumulate(q_ref, odd, back, column_of(seg), jnp.min(seg), bias, near_ref, out_ref, False)


def accumulate(q_ref, blocks, back, seg_col, lowest, bias, in_ref, out_ref, fresh):
    me = lax.axis_index("ctx") * 2 + lax.axis_index("rep")
    size = 3
    for start in range(0, len(blocks), size):
        some = blocks[start:start + size]
        seen = []
        for i, block in enumerate(some, start):
            if back[i]:
                hide(bias.at[i], block, seg_col)
                seen.append(((me >= back[i]) & (jnp.max(documents(block)) == lowest)).astype(jnp.int32))
        first = fresh and start == 0
        count = sum(seen) + (1 if first else 0)
        for n in range(1, len(some) + 1):
            @pl.when(count == n)
            def _(n=n, start=start, some=some, first=first):
                def finish(j, new):
                    out_ref[j] = new if first else in_ref[j] + new
                attend(q_ref, some[:n], [bias.at[start + i] for i in range(n)], finish)


def far_kernel(hops, n_other, seg_ref, q_ref, far_ref, to_one, to_zero, near_ref, w_hbm, att_ref, *rest):
    outs, (odd, bias, w_buf, sem) = rest[:n_other], rest[n_other:]
    heads = q_ref.shape[0]
    c, r, h = lax.axis_index("ctx"), lax.axis_index("rep"), lax.axis_index("head")
    start, finish_projection = project(att_ref, w_hbm, w_buf, sem, outs, [(jnp.bitwise_xor(h, d + 1), 0) for d in range(n_other)])
    start()
    seg = seg_ref[...].astype(F32)
    seg_col = column_of(seg)
    lowest = jnp.min(seg)
    choose(odd, r == 1, to_one, to_zero)
    blocks = [odd, far_ref]
    me = c * 2 + r
    seen = []
    for i, d in enumerate((2 * hops - 1, 2 * hops)):
        hide(bias.at[i], blocks[i], seg_col)
        seen.append(((me >= d) & (jnp.max(documents(blocks[i])) == lowest)).astype(jnp.int32))
    count = sum(seen)

    def put(j, both):
        at = j * HD if isinstance(j, int) else pl.multiple_of(j * HD, HD)
        att_ref[:, pl.ds(at, HD)] = (both[:, :HD] / both[:, HD:]).astype(BF16)

    @pl.when(count == 0)
    def _():
        for j in range(heads):
            put(j, near_ref[j])

    for n in (1, 2):
        @pl.when(count == n)
        def _(n=n):
            attend(q_ref, blocks[:n], [bias.at[i] for i in range(n)], lambda j, new: put(j, near_ref[j] + new))

    finish_projection()


def project(att_ref, w_hbm, w_buf, sem, outs, steps):
    half = w_hbm.shape[1] // lax.axis_size("head")
    copies, at = [], 0
    for i, (out, (group, col)) in enumerate(zip(outs, steps, strict=True)):
        wide = out.shape[1]
        from_ = pl.multiple_of(group * half + col, 128)
        copies.append(pltpu.make_async_copy(w_hbm.at[:, pl.ds(from_, wide)], w_buf.at[:, pl.ds(at, wide)], sem.at[i]))
        at += wide

    def start():
        for copy in copies:
            copy.start()

    def finish():
        at = 0
        for out, copy in zip(outs, copies, strict=True):
            copy.wait()
            wide = out.shape[1]
            out[...] = jnp.dot(att_ref[...], w_buf[:, at:at + wide], preferred_element_type=F32).astype(BF16)
            at += wide

    return start, finish


def project_kernel(steps, att_ref, w_hbm, *refs):
    outs, (w_buf, sem) = refs[:len(steps)], refs[len(steps):]
    h = lax.axis_index("head")
    steps = [(jnp.bitwise_xor(h, flip), at) for flip, at in steps]
    start, finish = project(att_ref, w_hbm, w_buf, sem, outs, steps)
    start()
    finish()


def add_shares(shares):
    total = shares[0][...].astype(F32)
    for share in shares[1:]:
        total = total + share[...].astype(F32)
    return total.astype(BF16)


def take(pos, count, total):
    hit = lax.broadcasted_iota(jnp.int32, (count, total.shape[0]), 0) == pos
    return jnp.dot(jnp.where(hit, 1.0, 0.0).astype(BF16), total, preferred_element_type=F32).astype(BF16)


def pick_kernel(ctx, span, mark, pos_ref, pair_slots, *refs):
    slots, shares, outs = refs[:ctx], refs[ctx:-ctx], refs[-ctx:]
    moved = take(pos_ref[0:1, :], span * ctx, add_shares(shares))
    for k, out in enumerate(outs):
        out[0:span, :] = moved[k * span:(k + 1) * span]
        out[mark:, :] = jnp.zeros((8, out.shape[1]), BF16)
        lanes = slots[k].shape[1]
        top = lax.broadcasted_iota(jnp.int32, (8, lanes), 0) < 4
        out[mark:, 0:lanes] = jnp.where(top, slots[k][...], pair_slots[8 * k:8 * k + 8, :]).astype(BF16)


def split_kernel(cap, pos_ref, *refs):
    shares, (stay_ref, *leave_refs) = refs[:-3], refs[-3:]
    total = add_shares(shares)
    count = stay_ref.shape[0]
    pos = pos_ref[0:1, :]
    line = lax.div(pos, cap)
    at = lax.div(line, 2) * cap + (pos - line * cap)
    same = line - lax.div(line, 2) * 2 == 0
    stay_ref[...] = take(jnp.where(same, at, -1), count, total)
    leave = take(jnp.where(same, -1, at), count, total)
    part = leave_refs[0].shape[0]
    for i, ref in enumerate(leave_refs):
        ref[...] = leave[i * part:(i + 1) * part]


def merge_kernel(cap, stay_ref, *refs):
    came, outs = refs[:2], refs[2:]
    for k, out in enumerate(outs):
        out[0:cap, :] = stay_ref[k * cap:(k + 1) * cap, :]
        came_ref = came[2 * k // len(outs)]
        first = k % (len(outs) // 2) * cap
        out[cap:, :] = came_ref[first:first + cap, :]


def slot_lines(ref, at, span):
    lines = ref[at:at + 8, 0:span].astype(F32).astype(jnp.int32)
    return lines[0:1], lines[4:5]


def put(slot, block, count):
    hit = lax.broadcasted_iota(jnp.int32, (count, slot.shape[1]), 0) == slot
    return jnp.dot(jnp.where(hit, 1.0, 0.0).astype(BF16), block, preferred_element_type=F32)


def place_kernel(ctx, cap, rows, mark, *refs):
    blocks, (mine_ref, pair_ref) = refs[:ctx], refs[ctx:]
    span = 2 * cap
    total = None
    lane = lax.broadcasted_iota(jnp.int32, (1, span), 1)
    for block in blocks:
        slot, _ = slot_lines(block, mark, span)
        slot = jnp.where((slot >= 0) & (lane >= cap), slot + rows, slot)
        some = put(slot, block[0:span, :], 2 * rows)
        total = some if total is None else total + some
    mine_ref[...] = total[:rows].astype(BF16)
    pair_ref[...] = total[rows:].astype(BF16)


def final_kernel(ctx, cap, mark, *refs):
    marks, blocks, out = refs[:ctx], refs[ctx:-1], refs[-1]
    rows = out.shape[0]
    span = 2 * cap
    lane = lax.broadcasted_iota(jnp.int32, (1, span), 1)
    total = None
    for k in range(ctx):
        mine, pair = slot_lines(marks[k], mark, span)
        slot = jnp.where(lane < cap, mine, pair)
        some = put(slot, blocks[k][...], rows)
        total = some if total is None else total + some
    out[...] = total.astype(BF16)


def join_kernel(mine_ref, pair_ref, rest_ref, out):
    rows, at = mine_ref.shape
    out[:, 0:at] = (mine_ref[...].astype(F32) + pair_ref[...].astype(F32)).astype(BF16)
    out[:, at:] = rest_ref[...]


def after(x, *earlier):
    return lax.optimization_barrier((x, *earlier))[0]


def local(tokens, doc_ids, dest_rows, w_query, w_key, w_value, w_out):
    ctx, rep, n_head = lax.axis_size("ctx"), lax.axis_size("rep"), lax.axis_size("head")
    rows, width = tokens.shape
    kv_cols, q_cols = w_key.shape[1], w_query.shape[1]
    heads = q_cols // HD
    half = w_out.shape[1] // n_head
    others = n_head - 1
    hops = ctx // 2
    cap = 3 * (rows // (2 * ctx * rep))
    span = 2 * cap
    lanes = -(-span // 128) * 128
    every = ctx * span
    sds = jax.ShapeDtypeStruct
    chunks = [half // 2] * 2

    up = [(i, (i + 1) % ctx) for i in range(ctx)]
    swap = [(0, 1), (1, 0)]
    seg_row = doc_ids.reshape(1, rows)

    parts = 4
    payload = sds((rows + 16, 2 * kv_cols), BF16)
    own, table = pl.pallas_call(
        functools.partial(kv_kernel, parts),
        in_specs=[ANY, ANY, ANY, pl.BlockSpec(memory_space=pltpu.HBM)],
        out_specs=[VMEM] * 2,
        out_shape=[payload, sds((rows, 2 * HD), F32)],
        scratch_shapes=[
            pltpu.VMEM((rows, width), BF16),
            pltpu.VMEM((width, 2 * kv_cols), BF16),
            pltpu.VMEM((1, rows), jnp.int32),
            pltpu.SemaphoreType.DMA((3 * parts + 1,)),
        ],
        compiler_params=params(KV_MIB),
        cost_estimate=cost(4 * rows * width * kv_cols, 2 * width * (rows + 2 * kv_cols)),
        name="keys_values",
    )(tokens, w_key, w_value, pltpu.with_memory_space_constraint(seg_row, pltpu.HBM))

    hop = [own, lax.ppermute(own, "ctx", up)]

    parts = 4
    queries = pl.pallas_call(
        functools.partial(q_kernel, parts),
        in_specs=[ANY, ANY, VMEM],
        out_specs=VMEM,
        out_shape=sds((heads, rows, HD), BF16),
        scratch_shapes=[pltpu.VMEM((rows, width), BF16), pltpu.VMEM((width, q_cols), BF16), pltpu.SemaphoreType.DMA((parts + 1,))],
        compiler_params=params(Q_MIB),
        cost_estimate=cost(2 * rows * width * q_cols, 2 * width * (rows + q_cols)),
        name="queries",
    )(tokens, w_query, table)

    route = pl.pallas_call(
        functools.partial(route_kernel, ctx, cap),
        in_specs=[VMEM],
        out_specs=[VMEM] * (2 + ctx),
        out_shape=[sds((8, rows), jnp.int32), sds((8 * ctx, lanes), F32)] + [sds((8, lanes), F32)] * ctx,
        compiler_params=params(8),
        cost_estimate=cost(0, 0),
        name="routes",
    )
    buffer_pos, pair_slots, *slots = route(after(dest_rows.reshape(1, rows), queries))
    hop[1] = after(hop[1], queries, buffer_pos)
    for i in range(1, hops):
        hop.append(lax.ppermute(hop[i], "ctx", [(j, j) for j in range(i)] + [(j, j + 1) for j in range(i, ctx - 1)] + [(ctx - 1, i)]))

    short = sds((rows + 8, 2 * kv_cols), BF16)
    short_hop = pl.pallas_call(
        shorten_kernel,
        in_specs=[VMEM] * hops,
        out_specs=[VMEM] * hops,
        out_shape=[short] * hops,
        compiler_params=params(8),
        cost_estimate=cost(0, 0),
        name="shorten",
    )(*hop[:hops])
    pair = [lax.ppermute(x, "rep", swap) for x in short_hop]

    work = heads * rows * rows
    near = pl.pallas_call(
        near_kernel,
        in_specs=[VMEM] * (2 + hops),
        out_specs=VMEM,
        out_shape=sds((heads, rows, 2 * HD), F32),
        scratch_shapes=[pltpu.VMEM((hops, rows, rows), F32)],
        compiler_params=params(12),
        cost_estimate=cost(EVEN_COST, 0),
        name="even_attention",
    )(after(seg_row, *short_hop), queries, *hop[:hops])

    pair_slots = lax.ppermute(pair_slots, "rep", swap)
    pair = [lax.ppermute(x, "rep", swap) for x in short_hop]
    near = pl.pallas_call(
        middle_kernel,
        in_specs=[VMEM] * (3 + hops),
        out_specs=VMEM,
        out_shape=sds((heads, rows, 2 * HD), F32),
        scratch_shapes=[pltpu.VMEM(short.shape, BF16)] * (hops - 1) + [pltpu.VMEM((hops - 1, rows, rows), F32)],
        input_output_aliases={2 + hops: 0},
        compiler_params=params(12),
        cost_estimate=cost(0, 0),
        name="odd_attention",
    )(seg_row, queries, *pair, near)
    hop[hops] = after(hop[hops], near)
    pair.append(lax.ppermute(hop[hops], "rep", swap))

    widths = chunks[:1] * others
    attended, *sent = pl.pallas_call(
        functools.partial(far_kernel, hops, others),
        in_specs=[VMEM] * 6 + [ANY],
        out_specs=[VMEM] * (1 + others),
        out_shape=[sds((rows, heads * HD), BF16)] + [sds((rows, n), BF16) for n in widths],
        scratch_shapes=[pltpu.VMEM(short.shape, BF16), pltpu.VMEM((2, rows, rows), F32)]
        + [pltpu.VMEM((heads * HD, sum(widths)), BF16), pltpu.SemaphoreType.DMA((others,))],
        compiler_params=params(FAR_MIB),
        cost_estimate=cost(8 * work * HD + 2 * rows * heads * HD * chunks[0], 10 * MIB, 2 * work),
        name="far_attention_project",
    )(after(seg_row, pair_slots), queries, hop[hops], pair[hops - 1], pair[hops], near, w_out)

    def project_some(x, steps, sizes):
        return pl.pallas_call(
            functools.partial(project_kernel, steps),
            in_specs=[VMEM, ANY],
            out_specs=[VMEM] * len(steps),
            out_shape=[sds((rows, n), BF16) for n in sizes],
            scratch_shapes=[pltpu.VMEM((heads * HD, sum(sizes)), BF16), pltpu.SemaphoreType.DMA((len(steps),))],
            compiler_params=params(PROJECT_MIB),
            cost_estimate=cost(BUSY, 0),
            name="project",
        )(x, w_out)

    flips = [[(i, i ^ (d + 1)) for i in range(n_head)] for d in range(others)]

    def to_heads(xs):
        return [lax.ppermute(x, "head", flip) for x, flip in zip(xs, flips, strict=True)]

    theirs = [to_heads(sent)]
    starts = [sum(chunks[:j]) for j in range(len(chunks))]
    later = range(1, len(chunks))
    steps, sizes = [(0, 0)], chunks[:1]
    for j in later:
        steps += [(d + 1, starts[j]) for d in range(others)]
        sizes = sizes + chunks[j:j + 1] * others
    mine, *sent = project_some(attended, steps, sizes)
    for j in later:
        theirs.append(to_heads(sent[(j - 1) * others:j * others]))

    def across(xs):
        return [xs[0]] + [lax.ppermute(xs[k], "ctx", [(i, i ^ k) for i in range(ctx)]) for k in range(1, ctx)]

    mark = -(-span // 16) * 16
    n = chunks[0]
    moved = pl.pallas_call(
        functools.partial(pick_kernel, ctx, span, mark),
        in_specs=[VMEM] * (2 + ctx + n_head),
        out_specs=[VMEM] * ctx,
        out_shape=[sds((mark + 8, n), BF16)] * ctx,
        compiler_params=params(8),
        cost_estimate=cost(0, 0),
        name="add_pick",
    )(after(buffer_pos, *sent), pair_slots, *slots, mine, *theirs[0])
    first = across(moved)

    ours = project_some(after(attended, *moved), [(0, starts[j]) for j in later], chunks[1:])
    held, last = [], list(moved)
    for j in later:
        n = chunks[j]
        stay, *leave = pl.pallas_call(
            functools.partial(split_kernel, cap),
            in_specs=[VMEM] * (1 + n_head),
            out_specs=[VMEM] * 3,
            out_shape=[sds((ctx * cap, n), BF16)] + [sds((ctx * cap // 2, n), BF16)] * 2,
            compiler_params=params(8),
            cost_estimate=cost(0, 0),
            name="add_split",
        )(after(buffer_pos, *last), ours[j - 1], *theirs[j])
        leave = [lax.ppermute(x, "rep", swap) for x in leave]
        moved = pl.pallas_call(
            functools.partial(merge_kernel, cap),
            in_specs=[VMEM] * 3,
            out_specs=[VMEM] * ctx,
            out_shape=[sds((span, n), BF16)] * ctx,
            compiler_params=params(8),
            cost_estimate=cost(0, 0),
            name="merge",
        )(stay, *leave)
        held.append(across(moved))
        last = list(moved)

    n = chunks[0]
    stay, leave = pl.pallas_call(
        functools.partial(place_kernel, ctx, cap, rows, mark),
        in_specs=[VMEM] * ctx,
        out_specs=[VMEM] * 2,
        out_shape=[sds((rows, n), BF16)] * 2,
        compiler_params=params(8),
        cost_estimate=cost(BUSY, 0),
        name="place",
    )(after(first[0], *held[0][:1]), *first[1:])
    leave = lax.ppermute(leave, "rep", swap)

    rest = pl.pallas_call(
        functools.partial(final_kernel, ctx, cap, mark),
        in_specs=[VMEM] * (2 * ctx),
        out_specs=VMEM,
        out_shape=sds((rows, chunks[1]), BF16),
        compiler_params=params(8),
        cost_estimate=cost(BUSY, 0),
        name="place_rest",
    )(first[0], *first[1:], *held[0])

    return pl.pallas_call(
        join_kernel,
        in_specs=[VMEM] * 3,
        out_specs=VMEM,
        out_shape=sds((rows, half), BF16),
        compiler_params=params(8),
        cost_estimate=cost(0, 0),
        name="join",
    )(stay, leave, rest)


def solution(mesh):
    return jax.shard_map(
        local,
        mesh=mesh,
        in_specs=(
            P(("grp", "ctx", "rep"), None),
            P(("grp", "ctx", "rep")),
            P(("grp", "ctx", "rep")),
            P(None, "head"),
            P(None, "head"),
            P(None, "head"),
            P("head", None),
        ),
        out_specs=P(("grp", "ctx", "rep"), "head"),
        check_vma=False,
    )
```

```python
import functools
import math

import jax
import jax.numpy as jnp
from jax import lax
from jax.experimental import pallas as pl
from jax.experimental.pallas import tpu as pltpu
from jax.sharding import PartitionSpec as P

HD = 128
THETA = 1000000.0
EPSILON = 1e-06
HIDE = -1e30
F32 = jnp.float32
BF16 = jnp.bfloat16
VMEM = pl.BlockSpec(memory_space=pltpu.VMEM)
ANY = pl.BlockSpec(memory_space=pl.ANY)
MIB = 1 << 20
BUSY = 20 * 10**9
EVEN_COST = 0
KV_MIB = 53
Q_MIB = 52
FAR_MIB = 44
PROJECT_MIB = 48


def params(mib):
    return pltpu.CompilerParams(vmem_limit_bytes=mib * MIB)


def cost(flops, nbytes, trans=0):
    return pl.CostEstimate(flops=int(flops), bytes_accessed=int(nbytes), transcendentals=int(trans))


def column_of(row):
    n = row.shape[1]
    at = lax.broadcasted_iota(jnp.int32, (n, n), 0) == lax.broadcasted_iota(jnp.int32, (n, n), 1)
    return jnp.sum(jnp.where(at, row, 0.0), axis=1, keepdims=True)


def norm_rope(heads, cosine, sine, factor):
    scale = lax.rsqrt(jnp.mean(heads * heads, axis=-1, keepdims=True) + EPSILON)
    if factor != 1.0:
        scale = scale * factor
    turned = pltpu.roll(heads, HD // 2, 1)
    return ((heads * cosine + turned * sine) * scale).astype(BF16)


def kv_kernel(parts, x_hbm, wk_hbm, wv_hbm, seg_hbm, kv_ref, tab_ref, x_buf, w_buf, seg_ref, sem):
    rows, width = x_buf.shape
    kv_cols = w_buf.shape[1] // 2
    depth = width // parts
    copies = []
    for i in range(parts):
        at = pl.ds(i * depth, depth)
        copies.append([
            pltpu.make_async_copy(x_hbm.at[:, at], x_buf.at[:, at], sem.at[3 * i]),
            pltpu.make_async_copy(wk_hbm.at[at, :], w_buf.at[at, pl.ds(0, kv_cols)], sem.at[3 * i + 1]),
            pltpu.make_async_copy(wv_hbm.at[at, :], w_buf.at[at, pl.ds(kv_cols, kv_cols)], sem.at[3 * i + 2]),
        ])
        for copy in copies[-1]:
            copy.start()
    docs = pltpu.make_async_copy(seg_hbm, seg_ref, sem.at[3 * parts])
    docs.start()
    first = (lax.axis_index("ctx") * 2 + lax.axis_index("rep")) * rows
    lane = lax.broadcasted_iota(jnp.int32, (1, HD), 1)
    freq = jnp.exp(lax.rem(lane, HD // 2).astype(F32) * (-2.0 * math.log(THETA) / HD))
    pos = (first + lax.broadcasted_iota(jnp.int32, (rows, HD), 0)).astype(F32)
    angle = pos * freq
    tab_ref[:, :HD] = jnp.cos(angle)
    tab_ref[:, HD:] = jnp.where(lane < HD // 2, -1.0, 1.0) * jnp.sin(angle)
    docs.wait()
    line = lax.broadcasted_iota(jnp.int32, (16, kv_cols), 0)
    segs = jnp.zeros((16, kv_cols), F32)
    for i in range(rows // kv_cols):
        segs = jnp.where(line == i, seg_ref[:, i * kv_cols:(i + 1) * kv_cols].astype(F32), segs)
    kv_ref[rows:, :kv_cols] = segs.astype(BF16)
    kv_ref[rows:, kv_cols:] = jnp.zeros((16, kv_cols), BF16)
    total = None
    for i in range(parts):
        for copy in copies[i]:
            copy.wait()
        at = slice(i * depth, (i + 1) * depth)
        part = jnp.dot(x_buf[:, at], w_buf[at, :], preferred_element_type=F32)
        total = part if total is None else total + part
    for at in range(0, kv_cols, HD):
        kv_ref[0:rows, at:at + HD] = norm_rope(total[:, at:at + HD], tab_ref[:, :HD], tab_ref[:, HD:], 1.0)
    kv_ref[0:rows, kv_cols:] = total[:, kv_cols:].astype(BF16)


def q_kernel(parts, x_hbm, w_hbm, tab_ref, q_ref, x_ref, w_buf, sem):
    heads = q_ref.shape[0]
    wide = w_buf.shape[1] // parts
    factor = math.log2(math.e) / math.sqrt(HD)
    tokens = pltpu.make_async_copy(x_hbm, x_ref, sem.at[parts])
    tokens.start()
    copies = []
    for i in range(parts):
        at = pl.ds(i * wide, wide)
        copies.append(pltpu.make_async_copy(w_hbm.at[:, at], w_buf.at[:, at], sem.at[i]))
        copies[-1].start()

    def finish(i, flat):
        for j in range(wide // HD):
            done = norm_rope(flat[:, j * HD:(j + 1) * HD], tab_ref[:, :HD], tab_ref[:, HD:], factor)
            q_ref[i * (wide // HD) + j] = done

    held = None
    tokens.wait()
    for i in range(parts):
        copies[i].wait()
        flat = jnp.dot(x_ref[...], w_buf[:, i * wide:(i + 1) * wide], preferred_element_type=F32)
        if i:
            finish(i - 1, held)
        held = flat
    finish(parts - 1, held)


def route_kernel(ctx, cap, dest_ref, pos_ref, all_ref, *slot_refs):
    rows = dest_ref.shape[1]
    mine_c, mine_r = lax.axis_index("ctx"), lax.axis_index("rep")
    dest = dest_ref[...]
    owner = lax.div(dest, rows)
    slot = dest - owner * rows
    owner_col = column_of(owner.astype(F32))
    ii = lax.broadcasted_iota(jnp.int32, (rows, rows), 0)
    jj = lax.broadcasted_iota(jnp.int32, (rows, rows), 1)
    before = (owner_col == owner.astype(F32)) & (ii < jj)
    rank = jnp.sum(jnp.where(before, 1.0, 0.0), axis=0, keepdims=True).astype(jnp.int32)
    near_c = jnp.bitwise_xor(lax.div(owner, 2), mine_c)
    near_r = jnp.bitwise_xor(lax.rem(owner, 2), mine_r)
    pos = (near_c * 2 + near_r) * cap + rank
    pos_ref[...] = jnp.broadcast_to(pos, pos_ref.shape)
    pos_col = column_of(pos.astype(F32))
    target_col = column_of(slot.astype(F32)) + 1.0
    lanes = slot_refs[0].shape[1]
    for k in range(ctx):
        lane = lax.broadcasted_iota(jnp.int32, (rows, lanes), 1)
        hit = (pos_col == (lane + k * 2 * cap).astype(F32)) & (lane < 2 * cap)
        got = jnp.sum(jnp.where(hit, target_col, 0.0), axis=0, keepdims=True) - 1.0
        slot_refs[k][...] = jnp.broadcast_to(got, slot_refs[k].shape)
        all_ref[8 * k:8 * k + 8, :] = jnp.broadcast_to(got, slot_refs[k].shape)


def documents(kv_ref):
    wide = kv_ref.shape[1] // 2
    rows = kv_ref.shape[0] // 128 * 128
    lines = kv_ref[rows:rows + 8, :wide].astype(F32)
    return jnp.concatenate([lines[i:i + 1] for i in range(rows // wide)], 1)


def attend(q_ref, blocks, biases, finish):
    heads, rows = q_ref.shape[0], q_ref.shape[1]
    kv_cols = blocks[0].shape[1] // 2
    kv_heads = kv_cols // HD
    groups = heads // kv_heads
    for g in range(kv_heads):
        at = g * HD
        keys = [b[0:rows, at:at + HD] for b in blocks]
        ones = jnp.ones((rows, HD), BF16)
        vals = [jnp.concatenate([b[0:rows, kv_cols + at:kv_cols + at + HD], ones], 1) for b in blocks]
        vals = jnp.concatenate(vals, 0) if len(vals) > 1 else vals[0]

        def head(j, _):
            weights = []
            for key, bias in zip(keys, biases, strict=True):
                s = lax.dot_general(q_ref[j], key, (((1,), (1,)), ((), ())), preferred_element_type=F32)
                weights.append(jnp.exp2(s + bias[...]).astype(BF16))
            p = jnp.concatenate(weights, 1) if len(weights) > 1 else weights[0]
            finish(j, jnp.dot(p, vals, preferred_element_type=F32))
            return 0

        lax.fori_loop(g * groups, (g + 1) * groups, head, 0, unroll=8)


def hide(bias_ref, kv_ref, seg_col):
    bias_ref[...] = jnp.where(documents(kv_ref) == seg_col, 0.0, HIDE)


def choose(to_ref, flag, yes_ref, no_ref):
    @pl.when(flag)
    def _():
        to_ref[...] = yes_ref[0:to_ref.shape[0], :]

    @pl.when(jnp.logical_not(flag))
    def _():
        to_ref[...] = no_ref[0:to_ref.shape[0], :]


def near_kernel(seg_ref, q_ref, *refs):
    blocks, out_ref, bias = refs[:-2], refs[-2], refs[-1]
    rows = q_ref.shape[1]
    seg = seg_ref[...].astype(F32)
    seg_col = column_of(seg)
    ii = lax.broadcasted_iota(jnp.int32, (rows, rows), 0)
    jj = lax.broadcasted_iota(jnp.int32, (rows, rows), 1)
    bias[0] = jnp.where((seg == seg_col) & (jj <= ii), 0.0, HIDE)
    back = [2 * i for i in range(len(blocks))]
    accumulate(q_ref, blocks, back, seg_col, jnp.min(seg), bias, out_ref, out_ref, True)


def shorten_kernel(*refs):
    n = len(refs) // 2
    for short, block in zip(refs[n:], refs[:n], strict=True):
        short[...] = block[0:short.shape[0], :]


def middle_kernel(seg_ref, q_ref, *refs):
    n = (len(refs) - 4) // 2
    pair, (near_ref, out_ref), (odd, bias) = refs[:n + 1], refs[n + 1:n + 3], (refs[n + 3:-1], refs[-1])
    seg = seg_ref[...].astype(F32)
    r = lax.axis_index("rep")
    for i in range(n):
        choose(odd[i], r == 1, pair[i], pair[i + 1])
    back = [2 * i + 1 for i in range(n)]
    accumulate(q_ref, odd, back, column_of(seg), jnp.min(seg), bias, near_ref, out_ref, False)


def accumulate(q_ref, blocks, back, seg_col, lowest, bias, in_ref, out_ref, fresh):
    me = lax.axis_index("ctx") * 2 + lax.axis_index("rep")
    size = 3
    for start in range(0, len(blocks), size):
        some = blocks[start:start + size]
        seen = []
        for i, block in enumerate(some, start):
            if back[i]:
                hide(bias.at[i], block, seg_col)
                seen.append(((me >= back[i]) & (jnp.max(documents(block)) == lowest)).astype(jnp.int32))
        first = fresh and start == 0
        count = sum(seen) + (1 if first else 0)
        for n in range(1, len(some) + 1):
            @pl.when(count == n)
            def _(n=n, start=start, some=some, first=first):
                def finish(j, new):
                    out_ref[j] = new if first else in_ref[j] + new
                attend(q_ref, some[:n], [bias.at[start + i] for i in range(n)], finish)


def far_kernel(hops, n_other, seg_ref, q_ref, far_ref, to_one, to_zero, near_ref, w_hbm, att_ref, *rest):
    outs, (odd, bias, w_buf, sem) = rest[:n_other], rest[n_other:]
    heads = q_ref.shape[0]
    c, r, h = lax.axis_index("ctx"), lax.axis_index("rep"), lax.axis_index("head")
    start, finish_projection = project(att_ref, w_hbm, w_buf, sem, outs, [(jnp.bitwise_xor(h, d + 1), 0) for d in range(n_other)])
    start()
    seg = seg_ref[...].astype(F32)
    seg_col = column_of(seg)
    lowest = jnp.min(seg)
    choose(odd, r == 1, to_one, to_zero)
    blocks = [odd, far_ref]
    me = c * 2 + r
    seen = []
    for i, d in enumerate((2 * hops - 1, 2 * hops)):
        hide(bias.at[i], blocks[i], seg_col)
        seen.append(((me >= d) & (jnp.max(documents(blocks[i])) == lowest)).astype(jnp.int32))
    count = sum(seen)

    def put(j, both):
        at = j * HD if isinstance(j, int) else pl.multiple_of(j * HD, HD)
        att_ref[:, pl.ds(at, HD)] = (both[:, :HD] / both[:, HD:]).astype(BF16)

    @pl.when(count == 0)
    def _():
        for j in range(heads):
            put(j, near_ref[j])

    for n in (1, 2):
        @pl.when(count == n)
        def _(n=n):
            attend(q_ref, blocks[:n], [bias.at[i] for i in range(n)], lambda j, new: put(j, near_ref[j] + new))

    finish_projection()


def project(att_ref, w_hbm, w_buf, sem, outs, steps):
    half = w_hbm.shape[1] // lax.axis_size("head")
    copies, at = [], 0
    for i, (out, (group, col)) in enumerate(zip(outs, steps, strict=True)):
        wide = out.shape[1]
        from_ = pl.multiple_of(group * half + col, 128)
        copies.append(pltpu.make_async_copy(w_hbm.at[:, pl.ds(from_, wide)], w_buf.at[:, pl.ds(at, wide)], sem.at[i]))
        at += wide

    def start():
        for copy in copies:
            copy.start()

    def finish():
        at = 0
        for out, copy in zip(outs, copies, strict=True):
            copy.wait()
            wide = out.shape[1]
            out[...] = jnp.dot(att_ref[...], w_buf[:, at:at + wide], preferred_element_type=F32).astype(BF16)
            at += wide

    return start, finish


def project_kernel(steps, att_ref, w_hbm, *refs):
    outs, (w_buf, sem) = refs[:len(steps)], refs[len(steps):]
    h = lax.axis_index("head")
    steps = [(jnp.bitwise_xor(h, flip), at) for flip, at in steps]
    start, finish = project(att_ref, w_hbm, w_buf, sem, outs, steps)
    start()
    finish()


def add_shares(shares):
    total = shares[0][...].astype(F32)
    for share in shares[1:]:
        total = total + share[...].astype(F32)
    return total.astype(BF16)


def take(pos, count, total):
    hit = lax.broadcasted_iota(jnp.int32, (count, total.shape[0]), 0) == pos
    return jnp.dot(jnp.where(hit, 1.0, 0.0).astype(BF16), total, preferred_element_type=F32).astype(BF16)


def pick_kernel(ctx, span, mark, pos_ref, pair_slots, *refs):
    slots, shares, outs = refs[:ctx], refs[ctx:-ctx], refs[-ctx:]
    moved = take(pos_ref[0:1, :], span * ctx, add_shares(shares))
    for k, out in enumerate(outs):
        out[0:span, :] = moved[k * span:(k + 1) * span]
        out[mark:, :] = jnp.zeros((8, out.shape[1]), BF16)
        lanes = slots[k].shape[1]
        top = lax.broadcasted_iota(jnp.int32, (8, lanes), 0) < 4
        out[mark:, 0:lanes] = jnp.where(top, slots[k][...], pair_slots[8 * k:8 * k + 8, :]).astype(BF16)


def split_kernel(cap, pos_ref, *refs):
    shares, (stay_ref, *leave_refs) = refs[:-3], refs[-3:]
    total = add_shares(shares)
    count = stay_ref.shape[0]
    pos = pos_ref[0:1, :]
    line = lax.div(pos, cap)
    at = lax.div(line, 2) * cap + (pos - line * cap)
    same = line - lax.div(line, 2) * 2 == 0
    stay_ref[...] = take(jnp.where(same, at, -1), count, total)
    leave = take(jnp.where(same, -1, at), count, total)
    part = leave_refs[0].shape[0]
    for i, ref in enumerate(leave_refs):
        ref[...] = leave[i * part:(i + 1) * part]


def merge_kernel(cap, stay_ref, *refs):
    came, outs = refs[:2], refs[2:]
    for k, out in enumerate(outs):
        out[0:cap, :] = stay_ref[k * cap:(k + 1) * cap, :]
        came_ref = came[2 * k // len(outs)]
        first = k % (len(outs) // 2) * cap
        out[cap:, :] = came_ref[first:first + cap, :]


def slot_lines(ref, at, span):
    lines = ref[at:at + 8, 0:span].astype(F32).astype(jnp.int32)
    return lines[0:1], lines[4:5]


def put(slot, block, count):
    hit = lax.broadcasted_iota(jnp.int32, (count, slot.shape[1]), 0) == slot
    return jnp.dot(jnp.where(hit, 1.0, 0.0).astype(BF16), block, preferred_element_type=F32)


def place_kernel(ctx, cap, rows, mark, *refs):
    blocks, (mine_ref, pair_ref) = refs[:ctx], refs[ctx:]
    span = 2 * cap
    total = None
    lane = lax.broadcasted_iota(jnp.int32, (1, span), 1)
    for block in blocks:
        slot, _ = slot_lines(block, mark, span)
        slot = jnp.where((slot >= 0) & (lane >= cap), slot + rows, slot)
        some = put(slot, block[0:span, :], 2 * rows)
        total = some if total is None else total + some
    mine_ref[...] = total[:rows].astype(BF16)
    pair_ref[...] = total[rows:].astype(BF16)


def final_kernel(ctx, cap, mark, *refs):
    marks, blocks, out = refs[:ctx], refs[ctx:-1], refs[-1]
    rows = out.shape[0]
    span = 2 * cap
    lane = lax.broadcasted_iota(jnp.int32, (1, span), 1)
    total = None
    for k in range(ctx):
        mine, pair = slot_lines(marks[k], mark, span)
        slot = jnp.where(lane < cap, mine, pair)
        some = put(slot, blocks[k][...], rows)
        total = some if total is None else total + some
    out[...] = total.astype(BF16)


def join_kernel(mine_ref, pair_ref, rest_ref, out):
    rows, at = mine_ref.shape
    out[:, 0:at] = (mine_ref[...].astype(F32) + pair_ref[...].astype(F32)).astype(BF16)
    out[:, at:] = rest_ref[...]


def after(x, *earlier):
    return lax.optimization_barrier((x, *earlier))[0]


def local(tokens, doc_ids, dest_rows, w_query, w_key, w_value, w_out):
    ctx, rep, n_head = lax.axis_size("ctx"), lax.axis_size("rep"), lax.axis_size("head")
    rows, width = tokens.shape
    kv_cols, q_cols = w_key.shape[1], w_query.shape[1]
    heads = q_cols // HD
    half = w_out.shape[1] // n_head
    others = n_head - 1
    hops = ctx // 2
    cap = 3 * (rows // (2 * ctx * rep))
    span = 2 * cap
    lanes = -(-span // 128) * 128
    every = ctx * span
    sds = jax.ShapeDtypeStruct
    chunks = [half // 2] * 2

    up = [(i, (i + 1) % ctx) for i in range(ctx)]
    swap = [(0, 1), (1, 0)]
    seg_row = doc_ids.reshape(1, rows)

    parts = 4
    payload = sds((rows + 16, 2 * kv_cols), BF16)
    own, table = pl.pallas_call(
        functools.partial(kv_kernel, parts),
        in_specs=[ANY, ANY, ANY, pl.BlockSpec(memory_space=pltpu.HBM)],
        out_specs=[VMEM] * 2,
        out_shape=[payload, sds((rows, 2 * HD), F32)],
        scratch_shapes=[
            pltpu.VMEM((rows, width), BF16),
            pltpu.VMEM((width, 2 * kv_cols), BF16),
            pltpu.VMEM((1, rows), jnp.int32),
            pltpu.SemaphoreType.DMA((3 * parts + 1,)),
        ],
        compiler_params=params(KV_MIB),
        cost_estimate=cost(4 * rows * width * kv_cols, 2 * width * (rows + 2 * kv_cols)),
        name="keys_values",
    )(tokens, w_key, w_value, pltpu.with_memory_space_constraint(seg_row, pltpu.HBM))

    hop = [own, lax.ppermute(own, "ctx", up)]

    parts = 4
    queries = pl.pallas_call(
        functools.partial(q_kernel, parts),
        in_specs=[ANY, ANY, VMEM],
        out_specs=VMEM,
        out_shape=sds((heads, rows, HD), BF16),
        scratch_shapes=[pltpu.VMEM((rows, width), BF16), pltpu.VMEM((width, q_cols), BF16), pltpu.SemaphoreType.DMA((parts + 1,))],
        compiler_params=params(Q_MIB),
        cost_estimate=cost(2 * rows * width * q_cols, 2 * width * (rows + q_cols)),
        name="queries",
    )(tokens, w_query, table)

    route = pl.pallas_call(
        functools.partial(route_kernel, ctx, cap),
        in_specs=[VMEM],
        out_specs=[VMEM] * (2 + ctx),
        out_shape=[sds((8, rows), jnp.int32), sds((8 * ctx, lanes), F32)] + [sds((8, lanes), F32)] * ctx,
        compiler_params=params(8),
        cost_estimate=cost(0, 0),
        name="routes",
    )
    buffer_pos, pair_slots, *slots = route(after(dest_rows.reshape(1, rows), queries))
    hop[1] = after(hop[1], queries, buffer_pos)
    for i in range(1, hops):
        hop.append(lax.ppermute(hop[i], "ctx", [(j, j + 1) for j in range(i, ctx - 1)]))

    short = sds((rows + 8, 2 * kv_cols), BF16)
    short_hop = pl.pallas_call(
        shorten_kernel,
        in_specs=[VMEM] * hops,
        out_specs=[VMEM] * hops,
        out_shape=[short] * hops,
        compiler_params=params(8),
        cost_estimate=cost(0, 0),
        name="shorten",
    )(*hop[:hops])
    pair = [lax.ppermute(x, "rep", swap) for x in short_hop]

    work = heads * rows * rows
    near = pl.pallas_call(
        near_kernel,
        in_specs=[VMEM] * (2 + hops),
        out_specs=VMEM,
        out_shape=sds((heads, rows, 2 * HD), F32),
        scratch_shapes=[pltpu.VMEM((hops, rows, rows), F32)],
        compiler_params=params(12),
        cost_estimate=cost(EVEN_COST, 0),
        name="even_attention",
    )(after(seg_row, *short_hop), queries, *hop[:hops])

    pair_slots = lax.ppermute(pair_slots, "rep", swap)
    pair = [lax.ppermute(x, "rep", swap) for x in short_hop]
    near = pl.pallas_call(
        middle_kernel,
        in_specs=[VMEM] * (3 + hops),
        out_specs=VMEM,
        out_shape=sds((heads, rows, 2 * HD), F32),
        scratch_shapes=[pltpu.VMEM(short.shape, BF16)] * (hops - 1) + [pltpu.VMEM((hops - 1, rows, rows), F32)],
        input_output_aliases={2 + hops: 0},
        compiler_params=params(12),
        cost_estimate=cost(0, 0),
        name="odd_attention",
    )(seg_row, queries, *pair, near)
    hop[hops] = after(hop[hops], near)
    pair.append(lax.ppermute(hop[hops], "rep", swap))

    widths = chunks[:1] * others
    attended, *sent = pl.pallas_call(
        functools.partial(far_kernel, hops, others),
        in_specs=[VMEM] * 6 + [ANY],
        out_specs=[VMEM] * (1 + others),
        out_shape=[sds((rows, heads * HD), BF16)] + [sds((rows, n), BF16) for n in widths],
        scratch_shapes=[pltpu.VMEM(short.shape, BF16), pltpu.VMEM((2, rows, rows), F32)]
        + [pltpu.VMEM((heads * HD, sum(widths)), BF16), pltpu.SemaphoreType.DMA((others,))],
        compiler_params=params(FAR_MIB),
        cost_estimate=cost(8 * work * HD + 2 * rows * heads * HD * chunks[0], 10 * MIB, 2 * work),
        name="far_attention_project",
    )(after(seg_row, pair_slots), queries, hop[hops], pair[hops - 1], pair[hops], near, w_out)

    def project_some(x, steps, sizes):
        return pl.pallas_call(
            functools.partial(project_kernel, steps),
            in_specs=[VMEM, ANY],
            out_specs=[VMEM] * len(steps),
            out_shape=[sds((rows, n), BF16) for n in sizes],
            scratch_shapes=[pltpu.VMEM((heads * HD, sum(sizes)), BF16), pltpu.SemaphoreType.DMA((len(steps),))],
            compiler_params=params(PROJECT_MIB),
            cost_estimate=cost(BUSY, 0),
            name="project",
        )(x, w_out)

    flips = [[(i, i ^ (d + 1)) for i in range(n_head)] for d in range(others)]

    def to_heads(xs):
        return [lax.ppermute(x, "head", flip) for x, flip in zip(xs, flips, strict=True)]

    theirs = [to_heads(sent)]
    starts = [sum(chunks[:j]) for j in range(len(chunks))]
    later = range(1, len(chunks))
    steps, sizes = [(0, 0)], chunks[:1]
    for j in later:
        steps += [(d + 1, starts[j]) for d in range(others)]
        sizes = sizes + chunks[j:j + 1] * others
    mine, *sent = project_some(attended, steps, sizes)
    for j in later:
        theirs.append(to_heads(sent[(j - 1) * others:j * others]))

    def across(xs):
        return [xs[0]] + [lax.ppermute(xs[k], "ctx", [(i, i ^ k) for i in range(ctx)]) for k in range(1, ctx)]

    mark = -(-span // 16) * 16
    n = chunks[0]
    moved = pl.pallas_call(
        functools.partial(pick_kernel, ctx, span, mark),
        in_specs=[VMEM] * (2 + ctx + n_head),
        out_specs=[VMEM] * ctx,
        out_shape=[sds((mark + 8, n), BF16)] * ctx,
        compiler_params=params(8),
        cost_estimate=cost(0, 0),
        name="add_pick",
    )(after(buffer_pos, *sent), pair_slots, *slots, mine, *theirs[0])
    first = across(moved)

    ours = project_some(after(attended, *moved), [(0, starts[j]) for j in later], chunks[1:])
    held, last = [], list(moved)
    for j in later:
        n = chunks[j]
        stay, *leave = pl.pallas_call(
            functools.partial(split_kernel, cap),
            in_specs=[VMEM] * (1 + n_head),
            out_specs=[VMEM] * 3,
            out_shape=[sds((ctx * cap, n), BF16)] + [sds((ctx * cap // 2, n), BF16)] * 2,
            compiler_params=params(8),
            cost_estimate=cost(0, 0),
            name="add_split",
        )(after(buffer_pos, *last), ours[j - 1], *theirs[j])
        leave = [lax.ppermute(x, "rep", swap) for x in leave]
        moved = pl.pallas_call(
            functools.partial(merge_kernel, cap),
            in_specs=[VMEM] * 3,
            out_specs=[VMEM] * ctx,
            out_shape=[sds((span, n), BF16)] * ctx,
            compiler_params=params(8),
            cost_estimate=cost(0, 0),
            name="merge",
        )(stay, *leave)
        held.append(across(moved))
        last = list(moved)

    n = chunks[0]
    stay, leave = pl.pallas_call(
        functools.partial(place_kernel, ctx, cap, rows, mark),
        in_specs=[VMEM] * ctx,
        out_specs=[VMEM] * 2,
        out_shape=[sds((rows, n), BF16)] * 2,
        compiler_params=params(8),
        cost_estimate=cost(BUSY, 0),
        name="place",
    )(after(first[0], *held[0][:1]), *first[1:])
    leave = lax.ppermute(leave, "rep", swap)

    rest = pl.pallas_call(
        functools.partial(final_kernel, ctx, cap, mark),
        in_specs=[VMEM] * (2 * ctx),
        out_specs=VMEM,
        out_shape=sds((rows, chunks[1]), BF16),
        compiler_params=params(8),
        cost_estimate=cost(BUSY, 0),
        name="place_rest",
    )(first[0], *first[1:], *held[0])

    return pl.pallas_call(
        join_kernel,
        in_specs=[VMEM] * 3,
        out_specs=VMEM,
        out_shape=sds((rows, half), BF16),
        compiler_params=params(8),
        cost_estimate=cost(0, 0),
        name="join",
    )(stay, leave, rest)


def solution(mesh):
    return jax.shard_map(
        local,
        mesh=mesh,
        in_specs=(
            P(("grp", "ctx", "rep"), None),
            P(("grp", "ctx", "rep")),
            P(("grp", "ctx", "rep")),
            P(None, "head"),
            P(None, "head"),
            P(None, "head"),
            P("head", None),
        ),
        out_specs=P(("grp", "ctx", "rep"), "head"),
        check_vma=False,
    )
```

```python
import functools
import math

import jax
import jax.numpy as jnp
from jax import lax
from jax.experimental import pallas as pl
from jax.experimental.pallas import tpu as pltpu
from jax.sharding import PartitionSpec as P

HD = 128
THETA = 1000000.0
EPSILON = 1e-06
HIDE = -1e30
F32 = jnp.float32
BF16 = jnp.bfloat16
VMEM = pl.BlockSpec(memory_space=pltpu.VMEM)
ANY = pl.BlockSpec(memory_space=pl.ANY)
MIB = 1 << 20
BUSY = 20 * 10**9
EVEN_COST = 0
KV_MIB = 53
Q_MIB = 52
FAR_MIB = 44
PROJECT_MIB = 48


def params(mib):
    return pltpu.CompilerParams(vmem_limit_bytes=mib * MIB)


def cost(flops, nbytes, trans=0):
    return pl.CostEstimate(flops=int(flops), bytes_accessed=int(nbytes), transcendentals=int(trans))


def column_of(row):
    n = row.shape[1]
    at = lax.broadcasted_iota(jnp.int32, (n, n), 0) == lax.broadcasted_iota(jnp.int32, (n, n), 1)
    return jnp.sum(jnp.where(at, row, 0.0), axis=1, keepdims=True)


def norm_rope(heads, cosine, sine, factor):
    scale = lax.rsqrt(jnp.mean(heads * heads, axis=-1, keepdims=True) + EPSILON)
    if factor != 1.0:
        scale = scale * factor
    turned = pltpu.roll(heads, HD // 2, 1)
    return ((heads * cosine + turned * sine) * scale).astype(BF16)


def kv_kernel(parts, x_hbm, wk_hbm, wv_hbm, seg_hbm, kv_ref, tab_ref, x_buf, w_buf, seg_ref, sem):
    rows, width = x_buf.shape
    kv_cols = w_buf.shape[1] // 2
    depth = width // parts
    docs = pltpu.make_async_copy(seg_hbm, seg_ref, sem.at[3 * parts])
    docs.start()
    copies = []
    for i in range(parts):
        at = pl.ds(i * depth, depth)
        copies.append([
            pltpu.make_async_copy(x_hbm.at[:, at], x_buf.at[:, at], sem.at[3 * i]),
            pltpu.make_async_copy(wk_hbm.at[at, :], w_buf.at[at, pl.ds(0, kv_cols)], sem.at[3 * i + 1]),
            pltpu.make_async_copy(wv_hbm.at[at, :], w_buf.at[at, pl.ds(kv_cols, kv_cols)], sem.at[3 * i + 2]),
        ])
        for copy in copies[-1]:
            copy.start()
    first = (lax.axis_index("ctx") * 2 + lax.axis_index("rep")) * rows
    lane = lax.broadcasted_iota(jnp.int32, (1, HD), 1)
    freq = jnp.exp(lax.rem(lane, HD // 2).astype(F32) * (-2.0 * math.log(THETA) / HD))
    pos = (first + lax.broadcasted_iota(jnp.int32, (rows, HD), 0)).astype(F32)
    angle = pos * freq
    tab_ref[:, :HD] = jnp.cos(angle)
    tab_ref[:, HD:] = jnp.where(lane < HD // 2, -1.0, 1.0) * jnp.sin(angle)
    total = None
    for i in range(parts):
        for copy in copies[i]:
            copy.wait()
        at = slice(i * depth, (i + 1) * depth)
        part = jnp.dot(x_buf[:, at], w_buf[at, :], preferred_element_type=F32)
        total = part if total is None else total + part
    for at in range(0, kv_cols, HD):
        kv_ref[0:rows, at:at + HD] = norm_rope(total[:, at:at + HD], tab_ref[:, :HD], tab_ref[:, HD:], 1.0)
    kv_ref[0:rows, kv_cols:] = total[:, kv_cols:].astype(BF16)
    docs.wait()
    line = lax.broadcasted_iota(jnp.int32, (16, kv_cols), 0)
    segs = jnp.zeros((16, kv_cols), F32)
    for i in range(rows // kv_cols):
        segs = jnp.where(line == i, seg_ref[:, i * kv_cols:(i + 1) * kv_cols].astype(F32), segs)
    kv_ref[rows:, :kv_cols] = segs.astype(BF16)
    kv_ref[rows:, kv_cols:] = jnp.zeros((16, kv_cols), BF16)


def q_kernel(parts, x_hbm, w_hbm, tab_ref, q_ref, x_ref, w_buf, sem):
    heads = q_ref.shape[0]
    wide = w_buf.shape[1] // parts
    factor = math.log2(math.e) / math.sqrt(HD)
    tokens = pltpu.make_async_copy(x_hbm, x_ref, sem.at[parts])
    tokens.start()
    copies = []
    for i in range(parts):
        at = pl.ds(i * wide, wide)
        copies.append(pltpu.make_async_copy(w_hbm.at[:, at], w_buf.at[:, at], sem.at[i]))
        copies[-1].start()

    def finish(i, flat):
        for j in range(wide // HD):
            done = norm_rope(flat[:, j * HD:(j + 1) * HD], tab_ref[:, :HD], tab_ref[:, HD:], factor)
            q_ref[i * (wide // HD) + j] = done

    held = None
    tokens.wait()
    for i in range(parts):
        copies[i].wait()
        flat = jnp.dot(x_ref[...], w_buf[:, i * wide:(i + 1) * wide], preferred_element_type=F32)
        if i:
            finish(i - 1, held)
        held = flat
    finish(parts - 1, held)


def route_kernel(ctx, cap, dest_ref, pos_ref, all_ref, *slot_refs):
    rows = dest_ref.shape[1]
    mine_c, mine_r = lax.axis_index("ctx"), lax.axis_index("rep")
    dest = dest_ref[...]
    owner = lax.div(dest, rows)
    slot = dest - owner * rows
    owner_col = column_of(owner.astype(F32))
    ii = lax.broadcasted_iota(jnp.int32, (rows, rows), 0)
    jj = lax.broadcasted_iota(jnp.int32, (rows, rows), 1)
    before = (owner_col == owner.astype(F32)) & (ii < jj)
    rank = jnp.sum(jnp.where(before, 1.0, 0.0), axis=0, keepdims=True).astype(jnp.int32)
    near_c = jnp.bitwise_xor(lax.div(owner, 2), mine_c)
    near_r = jnp.bitwise_xor(lax.rem(owner, 2), mine_r)
    pos = (near_c * 2 + near_r) * cap + rank
    pos_ref[...] = jnp.broadcast_to(pos, pos_ref.shape)
    pos_col = column_of(pos.astype(F32))
    target_col = column_of(slot.astype(F32)) + 1.0
    lanes = slot_refs[0].shape[1]
    for k in range(ctx):
        lane = lax.broadcasted_iota(jnp.int32, (rows, lanes), 1)
        hit = (pos_col == (lane + k * 2 * cap).astype(F32)) & (lane < 2 * cap)
        got = jnp.sum(jnp.where(hit, target_col, 0.0), axis=0, keepdims=True) - 1.0
        slot_refs[k][...] = jnp.broadcast_to(got, slot_refs[k].shape)
        all_ref[8 * k:8 * k + 8, :] = jnp.broadcast_to(got, slot_refs[k].shape)


def documents(kv_ref):
    wide = kv_ref.shape[1] // 2
    rows = kv_ref.shape[0] // 128 * 128
    lines = kv_ref[rows:rows + 8, :wide].astype(F32)
    return jnp.concatenate([lines[i:i + 1] for i in range(rows // wide)], 1)


def attend(q_ref, blocks, biases, finish):
    heads, rows = q_ref.shape[0], q_ref.shape[1]
    kv_cols = blocks[0].shape[1] // 2
    kv_heads = kv_cols // HD
    groups = heads // kv_heads
    for g in range(kv_heads):
        at = g * HD
        keys = [b[0:rows, at:at + HD] for b in blocks]
        ones = jnp.ones((rows, HD), BF16)
        vals = [jnp.concatenate([b[0:rows, kv_cols + at:kv_cols + at + HD], ones], 1) for b in blocks]
        vals = jnp.concatenate(vals, 0) if len(vals) > 1 else vals[0]

        def head(j, _):
            weights = []
            for key, bias in zip(keys, biases, strict=True):
                s = lax.dot_general(q_ref[j], key, (((1,), (1,)), ((), ())), preferred_element_type=F32)
                weights.append(jnp.exp2(s + bias[...]).astype(BF16))
            p = jnp.concatenate(weights, 1) if len(weights) > 1 else weights[0]
            finish(j, jnp.dot(p, vals, preferred_element_type=F32))
            return 0

        lax.fori_loop(g * groups, (g + 1) * groups, head, 0, unroll=8)


def hide(bias_ref, kv_ref, seg_col):
    bias_ref[...] = jnp.where(documents(kv_ref) == seg_col, 0.0, HIDE)


def choose(to_ref, flag, yes_ref, no_ref):
    @pl.when(flag)
    def _():
        to_ref[...] = yes_ref[0:to_ref.shape[0], :]

    @pl.when(jnp.logical_not(flag))
    def _():
        to_ref[...] = no_ref[0:to_ref.shape[0], :]


def near_kernel(seg_ref, q_ref, *refs):
    blocks, out_ref, bias = refs[:-2], refs[-2], refs[-1]
    rows = q_ref.shape[1]
    seg = seg_ref[...].astype(F32)
    seg_col = column_of(seg)
    ii = lax.broadcasted_iota(jnp.int32, (rows, rows), 0)
    jj = lax.broadcasted_iota(jnp.int32, (rows, rows), 1)
    bias[0] = jnp.where((seg == seg_col) & (jj <= ii), 0.0, HIDE)
    back = [2 * i for i in range(len(blocks))]
    accumulate(q_ref, blocks, back, seg_col, jnp.min(seg), bias, out_ref, out_ref, True)


def shorten_kernel(*refs):
    n = len(refs) // 2
    for short, block in zip(refs[n:], refs[:n], strict=True):
        short[...] = block[0:short.shape[0], :]


def middle_kernel(seg_ref, q_ref, *refs):
    n = (len(refs) - 4) // 2
    pair, (near_ref, out_ref), (odd, bias) = refs[:n + 1], refs[n + 1:n + 3], (refs[n + 3:-1], refs[-1])
    seg = seg_ref[...].astype(F32)
    r = lax.axis_index("rep")
    for i in range(n):
        choose(odd[i], r == 1, pair[i], pair[i + 1])
    back = [2 * i + 1 for i in range(n)]
    accumulate(q_ref, odd, back, column_of(seg), jnp.min(seg), bias, near_ref, out_ref, False)


def accumulate(q_ref, blocks, back, seg_col, lowest, bias, in_ref, out_ref, fresh):
    me = lax.axis_index("ctx") * 2 + lax.axis_index("rep")
    size = 3
    for start in range(0, len(blocks), size):
        some = blocks[start:start + size]
        seen = []
        for i, block in enumerate(some, start):
            if back[i]:
                hide(bias.at[i], block, seg_col)
                seen.append(((me >= back[i]) & (jnp.max(documents(block)) == lowest)).astype(jnp.int32))
        first = fresh and start == 0
        count = sum(seen) + (1 if first else 0)
        for n in range(1, len(some) + 1):
            @pl.when(count == n)
            def _(n=n, start=start, some=some, first=first):
                def finish(j, new):
                    out_ref[j] = new if first else in_ref[j] + new
                attend(q_ref, some[:n], [bias.at[start + i] for i in range(n)], finish)


def far_kernel(hops, n_other, seg_ref, q_ref, far_ref, to_one, to_zero, near_ref, w_hbm, att_ref, *rest):
    outs, (odd, bias, w_buf, sem) = rest[:n_other], rest[n_other:]
    heads = q_ref.shape[0]
    c, r, h = lax.axis_index("ctx"), lax.axis_index("rep"), lax.axis_index("head")
    start, finish_projection = project(att_ref, w_hbm, w_buf, sem, outs, [(jnp.bitwise_xor(h, d + 1), 0) for d in range(n_other)])
    start()
    seg = seg_ref[...].astype(F32)
    seg_col = column_of(seg)
    lowest = jnp.min(seg)
    choose(odd, r == 1, to_one, to_zero)
    blocks = [odd, far_ref]
    me = c * 2 + r
    seen = []
    for i, d in enumerate((2 * hops - 1, 2 * hops)):
        hide(bias.at[i], blocks[i], seg_col)
        seen.append(((me >= d) & (jnp.max(documents(blocks[i])) == lowest)).astype(jnp.int32))
    count = sum(seen)

    def put(j, both):
        at = j * HD if isinstance(j, int) else pl.multiple_of(j * HD, HD)
        att_ref[:, pl.ds(at, HD)] = (both[:, :HD] / both[:, HD:]).astype(BF16)

    @pl.when(count == 0)
    def _():
        for j in range(heads):
            put(j, near_ref[j])

    for n in (1, 2):
        @pl.when(count == n)
        def _(n=n):
            attend(q_ref, blocks[:n], [bias.at[i] for i in range(n)], lambda j, new: put(j, near_ref[j] + new))

    finish_projection()


def project(att_ref, w_hbm, w_buf, sem, outs, steps):
    half = w_hbm.shape[1] // lax.axis_size("head")
    copies, at = [], 0
    for i, (out, (group, col)) in enumerate(zip(outs, steps, strict=True)):
        wide = out.shape[1]
        from_ = pl.multiple_of(group * half + col, 128)
        copies.append(pltpu.make_async_copy(w_hbm.at[:, pl.ds(from_, wide)], w_buf.at[:, pl.ds(at, wide)], sem.at[i]))
        at += wide

    def start():
        for copy in copies:
            copy.start()

    def finish():
        at = 0
        for out, copy in zip(outs, copies, strict=True):
            copy.wait()
            wide = out.shape[1]
            out[...] = jnp.dot(att_ref[...], w_buf[:, at:at + wide], preferred_element_type=F32).astype(BF16)
            at += wide

    return start, finish


def project_kernel(steps, att_ref, w_hbm, *refs):
    outs, (w_buf, sem) = refs[:len(steps)], refs[len(steps):]
    h = lax.axis_index("head")
    steps = [(jnp.bitwise_xor(h, flip), at) for flip, at in steps]
    start, finish = project(att_ref, w_hbm, w_buf, sem, outs, steps)
    start()
    finish()


def add_shares(shares):
    total = shares[0][...].astype(F32)
    for share in shares[1:]:
        total = total + share[...].astype(F32)
    return total.astype(BF16)


def take(pos, count, total):
    hit = lax.broadcasted_iota(jnp.int32, (count, total.shape[0]), 0) == pos
    return jnp.dot(jnp.where(hit, 1.0, 0.0).astype(BF16), total, preferred_element_type=F32).astype(BF16)


def pick_kernel(ctx, span, mark, pos_ref, pair_slots, *refs):
    slots, shares, outs = refs[:ctx], refs[ctx:-ctx], refs[-ctx:]
    moved = take(pos_ref[0:1, :], span * ctx, add_shares(shares))
    for k, out in enumerate(outs):
        out[0:span, :] = moved[k * span:(k + 1) * span]
        out[mark:, :] = jnp.zeros((8, out.shape[1]), BF16)
        lanes = slots[k].shape[1]
        top = lax.broadcasted_iota(jnp.int32, (8, lanes), 0) < 4
        out[mark:, 0:lanes] = jnp.where(top, slots[k][...], pair_slots[8 * k:8 * k + 8, :]).astype(BF16)


def split_kernel(cap, pos_ref, *refs):
    shares, (stay_ref, *leave_refs) = refs[:-3], refs[-3:]
    total = add_shares(shares)
    count = stay_ref.shape[0]
    pos = pos_ref[0:1, :]
    line = lax.div(pos, cap)
    at = lax.div(line, 2) * cap + (pos - line * cap)
    same = line - lax.div(line, 2) * 2 == 0
    stay_ref[...] = take(jnp.where(same, at, -1), count, total)
    leave = take(jnp.where(same, -1, at), count, total)
    part = leave_refs[0].shape[0]
    for i, ref in enumerate(leave_refs):
        ref[...] = leave[i * part:(i + 1) * part]


def merge_kernel(cap, stay_ref, *refs):
    came, outs = refs[:2], refs[2:]
    for k, out in enumerate(outs):
        out[0:cap, :] = stay_ref[k * cap:(k + 1) * cap, :]
        came_ref = came[2 * k // len(outs)]
        first = k % (len(outs) // 2) * cap
        out[cap:, :] = came_ref[first:first + cap, :]


def slot_lines(ref, at, span):
    lines = ref[at:at + 8, 0:span].astype(F32).astype(jnp.int32)
    return lines[0:1], lines[4:5]


def put(slot, block, count):
    hit = lax.broadcasted_iota(jnp.int32, (count, slot.shape[1]), 0) == slot
    return jnp.dot(jnp.where(hit, 1.0, 0.0).astype(BF16), block, preferred_element_type=F32)


def place_kernel(ctx, cap, rows, mark, *refs):
    blocks, (mine_ref, pair_ref) = refs[:ctx], refs[ctx:]
    span = 2 * cap
    total = None
    lane = lax.broadcasted_iota(jnp.int32, (1, span), 1)
    for block in blocks:
        slot, _ = slot_lines(block, mark, span)
        slot = jnp.where((slot >= 0) & (lane >= cap), slot + rows, slot)
        some = put(slot, block[0:span, :], 2 * rows)
        total = some if total is None else total + some
    mine_ref[...] = total[:rows].astype(BF16)
    pair_ref[...] = total[rows:].astype(BF16)


def final_kernel(ctx, cap, mark, *refs):
    marks, blocks, out = refs[:ctx], refs[ctx:-1], refs[-1]
    rows = out.shape[0]
    span = 2 * cap
    lane = lax.broadcasted_iota(jnp.int32, (1, span), 1)
    total = None
    for k in range(ctx):
        mine, pair = slot_lines(marks[k], mark, span)
        slot = jnp.where(lane < cap, mine, pair)
        some = put(slot, blocks[k][...], rows)
        total = some if total is None else total + some
    out[...] = total.astype(BF16)


def join_kernel(mine_ref, pair_ref, rest_ref, out):
    rows, at = mine_ref.shape
    out[:, 0:at] = (mine_ref[...].astype(F32) + pair_ref[...].astype(F32)).astype(BF16)
    out[:, at:] = rest_ref[...]


def after(x, *earlier):
    return lax.optimization_barrier((x, *earlier))[0]


def local(tokens, doc_ids, dest_rows, w_query, w_key, w_value, w_out):
    ctx, rep, n_head = lax.axis_size("ctx"), lax.axis_size("rep"), lax.axis_size("head")
    rows, width = tokens.shape
    kv_cols, q_cols = w_key.shape[1], w_query.shape[1]
    heads = q_cols // HD
    half = w_out.shape[1] // n_head
    others = n_head - 1
    hops = ctx // 2
    cap = 3 * (rows // (2 * ctx * rep))
    span = 2 * cap
    lanes = -(-span // 128) * 128
    every = ctx * span
    sds = jax.ShapeDtypeStruct
    chunks = [half // 2] * 2

    up = [(i, (i + 1) % ctx) for i in range(ctx)]
    swap = [(0, 1), (1, 0)]
    seg_row = doc_ids.reshape(1, rows)

    parts = 4
    payload = sds((rows + 16, 2 * kv_cols), BF16)
    own, table = pl.pallas_call(
        functools.partial(kv_kernel, parts),
        in_specs=[ANY, ANY, ANY, pl.BlockSpec(memory_space=pltpu.HBM)],
        out_specs=[VMEM] * 2,
        out_shape=[payload, sds((rows, 2 * HD), F32)],
        scratch_shapes=[
            pltpu.VMEM((rows, width), BF16),
            pltpu.VMEM((width, 2 * kv_cols), BF16),
            pltpu.VMEM((1, rows), jnp.int32),
            pltpu.SemaphoreType.DMA((3 * parts + 1,)),
        ],
        compiler_params=params(KV_MIB),
        cost_estimate=cost(4 * rows * width * kv_cols, 2 * width * (rows + 2 * kv_cols)),
        name="keys_values",
    )(tokens, w_key, w_value, pltpu.with_memory_space_constraint(seg_row, pltpu.HBM))

    hop = [own, lax.ppermute(own, "ctx", up)]

    parts = 4
    queries = pl.pallas_call(
        functools.partial(q_kernel, parts),
        in_specs=[ANY, ANY, VMEM],
        out_specs=VMEM,
        out_shape=sds((heads, rows, HD), BF16),
        scratch_shapes=[pltpu.VMEM((rows, width), BF16), pltpu.VMEM((width, q_cols), BF16), pltpu.SemaphoreType.DMA((parts + 1,))],
        compiler_params=params(Q_MIB),
        cost_estimate=cost(2 * rows * width * q_cols, 2 * width * (rows + q_cols)),
        name="queries",
    )(tokens, w_query, table)

    route = pl.pallas_call(
        functools.partial(route_kernel, ctx, cap),
        in_specs=[VMEM],
        out_specs=[VMEM] * (2 + ctx),
        out_shape=[sds((8, rows), jnp.int32), sds((8 * ctx, lanes), F32)] + [sds((8, lanes), F32)] * ctx,
        compiler_params=params(8),
        cost_estimate=cost(0, 0),
        name="routes",
    )
    buffer_pos, pair_slots, *slots = route(after(dest_rows.reshape(1, rows), queries))
    hop[1] = after(hop[1], queries, buffer_pos)
    for i in range(1, hops):
        hop.append(lax.ppermute(hop[i], "ctx", [(j, j + 1) for j in range(i, ctx - 1)]))

    short = sds((rows + 8, 2 * kv_cols), BF16)
    short_hop = pl.pallas_call(
        shorten_kernel,
        in_specs=[VMEM] * hops,
        out_specs=[VMEM] * hops,
        out_shape=[short] * hops,
        compiler_params=params(8),
        cost_estimate=cost(0, 0),
        name="shorten",
    )(*hop[:hops])
    pair = [lax.ppermute(x, "rep", swap) for x in short_hop]

    work = heads * rows * rows
    near = pl.pallas_call(
        near_kernel,
        in_specs=[VMEM] * (2 + hops),
        out_specs=VMEM,
        out_shape=sds((heads, rows, 2 * HD), F32),
        scratch_shapes=[pltpu.VMEM((hops, rows, rows), F32)],
        compiler_params=params(12),
        cost_estimate=cost(EVEN_COST, 0),
        name="even_attention",
    )(after(seg_row, *short_hop), queries, *hop[:hops])

    pair_slots = lax.ppermute(pair_slots, "rep", swap)
    pair = [lax.ppermute(x, "rep", swap) for x in short_hop]
    near = pl.pallas_call(
        middle_kernel,
        in_specs=[VMEM] * (3 + hops),
        out_specs=VMEM,
        out_shape=sds((heads, rows, 2 * HD), F32),
        scratch_shapes=[pltpu.VMEM(short.shape, BF16)] * (hops - 1) + [pltpu.VMEM((hops - 1, rows, rows), F32)],
        input_output_aliases={2 + hops: 0},
        compiler_params=params(12),
        cost_estimate=cost(0, 0),
        name="odd_attention",
    )(seg_row, queries, *pair, near)
    hop[hops] = after(hop[hops], near)
    pair.append(lax.ppermute(hop[hops], "rep", swap))

    widths = chunks[:1] * others
    attended, *sent = pl.pallas_call(
        functools.partial(far_kernel, hops, others),
        in_specs=[VMEM] * 6 + [ANY],
        out_specs=[VMEM] * (1 + others),
        out_shape=[sds((rows, heads * HD), BF16)] + [sds((rows, n), BF16) for n in widths],
        scratch_shapes=[pltpu.VMEM(short.shape, BF16), pltpu.VMEM((2, rows, rows), F32)]
        + [pltpu.VMEM((heads * HD, sum(widths)), BF16), pltpu.SemaphoreType.DMA((others,))],
        compiler_params=params(FAR_MIB),
        cost_estimate=cost(8 * work * HD + 2 * rows * heads * HD * chunks[0], 10 * MIB, 2 * work),
        name="far_attention_project",
    )(after(seg_row, pair_slots), queries, hop[hops], pair[hops - 1], pair[hops], near, w_out)

    def project_some(x, steps, sizes):
        return pl.pallas_call(
            functools.partial(project_kernel, steps),
            in_specs=[VMEM, ANY],
            out_specs=[VMEM] * len(steps),
            out_shape=[sds((rows, n), BF16) for n in sizes],
            scratch_shapes=[pltpu.VMEM((heads * HD, sum(sizes)), BF16), pltpu.SemaphoreType.DMA((len(steps),))],
            compiler_params=params(PROJECT_MIB),
            cost_estimate=cost(BUSY, 0),
            name="project",
        )(x, w_out)

    flips = [[(i, i ^ (d + 1)) for i in range(n_head)] for d in range(others)]

    def to_heads(xs):
        return [lax.ppermute(x, "head", flip) for x, flip in zip(xs, flips, strict=True)]

    theirs = [to_heads(sent)]
    starts = [sum(chunks[:j]) for j in range(len(chunks))]
    later = range(1, len(chunks))
    steps, sizes = [(0, 0)], chunks[:1]
    for j in later:
        steps += [(d + 1, starts[j]) for d in range(others)]
        sizes = sizes + chunks[j:j + 1] * others
    mine, *sent = project_some(attended, steps, sizes)
    for j in later:
        theirs.append(to_heads(sent[(j - 1) * others:j * others]))

    def across(xs):
        return [xs[0]] + [lax.ppermute(xs[k], "ctx", [(i, i ^ k) for i in range(ctx)]) for k in range(1, ctx)]

    mark = -(-span // 16) * 16
    n = chunks[0]
    moved = pl.pallas_call(
        functools.partial(pick_kernel, ctx, span, mark),
        in_specs=[VMEM] * (2 + ctx + n_head),
        out_specs=[VMEM] * ctx,
        out_shape=[sds((mark + 8, n), BF16)] * ctx,
        compiler_params=params(8),
        cost_estimate=cost(0, 0),
        name="add_pick",
    )(after(buffer_pos, *sent), pair_slots, *slots, mine, *theirs[0])
    first = across(moved)

    ours = project_some(after(attended, *moved), [(0, starts[j]) for j in later], chunks[1:])
    held, last = [], list(moved)
    for j in later:
        n = chunks[j]
        stay, *leave = pl.pallas_call(
            functools.partial(split_kernel, cap),
            in_specs=[VMEM] * (1 + n_head),
            out_specs=[VMEM] * 3,
            out_shape=[sds((ctx * cap, n), BF16)] + [sds((ctx * cap // 2, n), BF16)] * 2,
            compiler_params=params(8),
            cost_estimate=cost(0, 0),
            name="add_split",
        )(after(buffer_pos, *last), ours[j - 1], *theirs[j])
        leave = [lax.ppermute(x, "rep", swap) for x in leave]
        moved = pl.pallas_call(
            functools.partial(merge_kernel, cap),
            in_specs=[VMEM] * 3,
            out_specs=[VMEM] * ctx,
            out_shape=[sds((span, n), BF16)] * ctx,
            compiler_params=params(8),
            cost_estimate=cost(0, 0),
            name="merge",
        )(stay, *leave)
        held.append(across(moved))
        last = list(moved)

    n = chunks[0]
    stay, leave = pl.pallas_call(
        functools.partial(place_kernel, ctx, cap, rows, mark),
        in_specs=[VMEM] * ctx,
        out_specs=[VMEM] * 2,
        out_shape=[sds((rows, n), BF16)] * 2,
        compiler_params=params(8),
        cost_estimate=cost(BUSY, 0),
        name="place",
    )(after(first[0], *held[0][:1]), *first[1:])
    leave = lax.ppermute(leave, "rep", swap)

    rest = pl.pallas_call(
        functools.partial(final_kernel, ctx, cap, mark),
        in_specs=[VMEM] * (2 * ctx),
        out_specs=VMEM,
        out_shape=sds((rows, chunks[1]), BF16),
        compiler_params=params(8),
        cost_estimate=cost(BUSY, 0),
        name="place_rest",
    )(first[0], *first[1:], *held[0])

    return pl.pallas_call(
        join_kernel,
        in_specs=[VMEM] * 3,
        out_specs=VMEM,
        out_shape=sds((rows, half), BF16),
        compiler_params=params(8),
        cost_estimate=cost(0, 0),
        name="join",
    )(stay, leave, rest)


def solution(mesh):
    return jax.shard_map(
        local,
        mesh=mesh,
        in_specs=(
            P(("grp", "ctx", "rep"), None),
            P(("grp", "ctx", "rep")),
            P(("grp", "ctx", "rep")),
            P(None, "head"),
            P(None, "head"),
            P(None, "head"),
            P("head", None),
        ),
        out_specs=P(("grp", "ctx", "rep"), "head"),
        check_vma=False,
    )
```
